32 devices in a mesh: cells: 8 (over z, x), genes: 4 (over y, core).
Axes of the slice: x: 2, y: 2, z: 4, core: 2. Of those that a mesh axis runs over, the one named last changes fastest.
Arguments:
- counts: bfloat16 [8192, 13500], P('cells', 'genes'), may hold values from 0.0099487305 to 200
- library: int32 [8192], P('cells'), may hold values from 1000 to 20000
- cell_mask: int32 [8192], P('cells'), may hold values 0 or 1
- slide_len: int32 [3], replicated, may hold values from 1 to 4096, 8192 in all
- kl_step: int32 [1], replicated, may hold values from 0 to 1999
- noise: bfloat16 [8192, 512], P('cells'), may hold values from -5 to 5
- emb_weight: bfloat16 [1024, 13500], P(None, 'genes'), may hold values from -0.0546875 to 0.0546875
- ln_gain: float32 [1024], replicated, may hold values from 0.5 to 1.5
- ln_bias: float32 [1024], replicated, may hold values from -1.5 to 1.5
- lat_weight: bfloat16 [1024, 1024], replicated, may hold values from -0.1875 to 0.1875
- lat_bias: float32 [1024], replicated, may hold values from -2 to 2
- up_weight: bfloat16 [1024, 512], replicated, may hold values from -0.25 to 0.25
- dec_weight: bfloat16 [1024, 13500], P(None, 'genes'), may hold values from -0.1875 to 0.1875
- prior_mean: float32 [512, 16], replicated, may hold values from -4 to 4
- prior_logvar: float32 [512, 16], replicated, may hold values from -1 to 1
- out_grad: bfloat16 [8192, 13500], P('cells', 'genes'), may hold values from -6 to 6
Outputs:
- decoded: bfloat16 [8192, 13500], P('cells', 'genes')
- counts_grad: bfloat16 [8192, 13500], P('cells', 'genes')
- emb_weight_grad: float32 [1024, 13500], P('cells', 'genes')
- ln_gain_grad: float32 [1024], P('cells')
- ln_bias_grad: float32 [1024], P('cells')
- lat_weight_grad: float32 [1024, 1024], P('cells')
- lat_bias_grad: float32 [1024], P('cells')
- up_weight_grad: float32 [1024, 512], P('cells')
- dec_weight_grad: float32 [1024, 13500], P('cells', 'genes')
- prior_mean_grad: float32 [512, 16], P('cells')
- prior_logvar_grad: float32 [512, 16], P('cells')
- kl_loss: float32 [1], replicated
The draws below stay inside these ranges and needn't reach their ends.
Inputs may be any that keep to these rules, and one draw needn't show every extreme that they name: `slide_len`: slide lengths sum to 8192.
All inputs are finite; a program needn't handle non-finite values. No bound on the sum of `cell_mask` on one device may be relied on, other than what follows from the above.
Results may differ from the reference program's by a relative error of at most 0.009.
Values may be sent and summed in bfloat16 or wider, within the bound.
A program may use at most 192 MiB of HBM per device.

```python
import math
import jax
import jax.numpy as jnp
import numpy as np
from jax import lax

D = 1024
G = 13500
LAT = 512
K = 16
R = 1024
WARM = 1000
CELLS = 8192
SLIDES = 3
MOST_SLIDE = 4096


def draw_library(key, part):
    place = jnp.arange(CELLS, dtype=jnp.int32)
    band = place // R % 4
    starts = jnp.array([1000, 2150, 4640, 10000], jnp.int32)
    low_end = jnp.sum(jnp.where(band[:, None] == jnp.arange(4, dtype=jnp.int32)[None, :], starts[None, :], 0), 1)
    pick = jax.random.randint(key, (CELLS,), 0, 10000, dtype=jnp.int32)
    values = low_end + pick * low_end // 10000
    values = jnp.where(place == 0, 1000, values)
    values = jnp.where(place == 4 * R - 1, 20000, values)
    return values.astype(jnp.int32)


def touch_ends(result, rng, smallest, top_value):
    shape = result.shape
    spot = [jax.random.randint(jax.random.fold_in(rng, axis), (), 0, shape[axis]) for axis in range(len(shape))]
    result = result.at[tuple(spot)].set(smallest)
    longest = shape.index(max(shape))
    spot[longest] = (spot[longest] + 1) % shape[longest]
    return result.at[tuple(spot)].set(top_value)


def block_levels(key, extent, cuts, smallest, largest):
    factor_of, own = 1.0, jax.random.fold_in(key, 6)
    for axis_at, parts in cuts:
        draws = jnp.exp(jax.random.uniform(jax.random.fold_in(own, axis_at), (parts,), jnp.float32, smallest / len(cuts), largest / len(cuts)))
        factor_of = factor_of * jnp.repeat(draws, extent[axis_at] // parts).reshape([-1 if axis == axis_at else 1 for axis in range(len(extent))])
    return factor_of


def split_up(number_of, total, bound, skew):
    loads = [(1 << 20) // math.isqrt(grade ** skew) + 1 for grade in range(2, number_of + 1)]
    surplus, given = total - bound - (number_of - 1), [1] * (number_of - 1)
    while surplus > 0:
        movable = [i for i in range(number_of - 1) if given[i] < bound]
        pool, remaining = sum([loads[i] for i in movable]), surplus
        for i in movable:
            addition = min(bound - given[i], max(1, remaining * loads[i] // pool), surplus)
            given[i] = given[i] + addition
            surplus = surplus - addition
    return np.array([bound] + given)


def ragged_sizes(key, count, total, bound, lean):
    if count == 2:
        one = jax.random.randint(key, (), max(1, total - bound), min(bound, total - 1) + 1)
        return jnp.stack([one, total - one])
    lengths = jnp.asarray(split_up(count, total, bound, lean), jnp.int32)
    couples = (count - 1) // 2
    source_of, receiver = lengths[1:1 + 2 * couples:2], lengths[2:2 + 2 * couples:2]
    room = jnp.minimum(source_of - 1, bound - receiver)
    moved = jax.random.randint(jax.random.fold_in(key, 1), (couples,), 0, 1 << 20) % (room + 1)
    lengths = lengths.at[1:1 + 2 * couples:2].set(source_of - moved).at[2:2 + 2 * couples:2].set(receiver + moved)
    return lengths[jax.random.permutation(jax.random.fold_in(key, 2), count)]


def bell_draw(key, dims, scale, reach, cuts=(), kind=jnp.bfloat16):
    factor_of = block_levels(key, dims, cuts, -0.22, 0.18) if cuts else 1.0
    entries = jax.random.normal(key, dims, jnp.float32) * scale * factor_of
    return jnp.minimum(jnp.maximum(entries, -reach), reach).astype(kind)


def setup_inputs(seed: int = 0) -> dict:
    arg_keys = jax.random.split(jax.random.key(seed), 17)
    return {
        "counts": jnp.clip(jnp.exp(math.log(200.0) - 9.9086277 * jax.random.uniform(arg_keys[0], (CELLS, G), jnp.float32) ** block_levels(arg_keys[0], (CELLS, G), ((0, 8), (1, 4)), -0.2, 0.2)), 0.0099487305, 200.0).astype(jnp.bfloat16),
        "library": draw_library(jax.random.fold_in(arg_keys[16], 71), 0),
        "cell_mask": touch_ends((jax.random.randint(arg_keys[2], (CELLS,), 0, 8) < 7).astype(jnp.int32), jax.random.fold_in(arg_keys[2], 1), 0, 1),
        "slide_len": ragged_sizes(arg_keys[3], SLIDES, CELLS, MOST_SLIDE, 2).astype(jnp.int32),
        "kl_step": jax.random.randint(arg_keys[4], (1,), 0, 2 * WARM).astype(jnp.int32),
        "noise": bell_draw(arg_keys[5], (CELLS, LAT), 1.0, 5.0, ((0, 8),)),
        "emb_weight": bell_draw(arg_keys[6], (D, G), G ** -0.5, 0.0546875, ((1, 4),)),
        "ln_gain": jnp.clip(1.0 + 0.1 * jax.random.normal(arg_keys[7], (D,), jnp.float32), 0.5, 1.5),
        "ln_bias": bell_draw(arg_keys[8], (D,), 0.3, 1.5, (), jnp.float32),
        "lat_weight": bell_draw(arg_keys[9], (D, 2 * LAT), D ** -0.5, 0.1875),
        "lat_bias": bell_draw(arg_keys[10], (2 * LAT,), 0.5, 2.0, (), jnp.float32),
        "up_weight": bell_draw(arg_keys[11], (D, LAT), LAT ** -0.5, 0.25),
        "dec_weight": bell_draw(arg_keys[12], (D, G), D ** -0.5, 0.1875, ((1, 4),)),
        "prior_mean": bell_draw(arg_keys[13], (LAT, K), 1.0, 4.0, (), jnp.float32),
        "prior_logvar": jnp.clip(jax.random.uniform(arg_keys[14], (LAT, K), jnp.float32, -1.0, 1.0), -1.0, 1.0),
        "out_grad": bell_draw(arg_keys[15], (CELLS, G), 1.0, 6.0, ((0, 8), (1, 4))),
    }


epsilon = 1e-05
free_bits = 1.0

@jax.custom_vjp
def low(v):
    return lax.optimization_barrier(v.astype(jnp.bfloat16)).astype(jnp.float32)

@jax.custom_vjp
def low_back(v):
    return v

def low_keep(v):
    return (low(v), None)

def low_pass(kept, grad):
    return (grad,)

def back_keep(v):
    return (v, None)

def back_low(kept, grad):
    return (low(grad),)
low.defvjp(low_keep, low_pass)
low_back.defvjp(back_keep, back_low)

def hidot(left, right):
    return jnp.dot(left, right, precision=lax.Precision.HIGHEST, preferred_element_type=jnp.float32)

def reference(counts, library, cell_mask, slide_len, kl_step, noise, emb_weight, ln_gain, ln_bias, lat_weight, lat_bias, up_weight, dec_weight, prior_mean, prior_logvar, out_grad):
    place = jnp.arange(CELLS, dtype=jnp.int32)
    ends = jnp.cumsum(slide_len)
    slide_of = lax.optimization_barrier(jnp.sum((ends[None, :] <= place[:, None]).astype(jnp.int32), 1))
    onehot = (slide_of[:, None] == jnp.arange(SLIDES, dtype=jnp.int32)[None, :]).astype(jnp.float32)
    live = cell_mask.astype(jnp.float32)
    libsize = library.astype(jnp.float32)
    lib_total = lax.optimization_barrier(jnp.sum(onehot * (libsize * live)[:, None], 0))
    live_total = lax.optimization_barrier(jnp.sum(onehot * live[:, None], 0))
    slide_lib = lib_total / jnp.maximum(live_total, 1.0)
    scale = lax.optimization_barrier(jnp.sum(onehot * slide_lib[None, :], 1)) / libsize
    total = jnp.maximum(jnp.sum(live_total), 1.0)
    beta = jnp.minimum(1.0, kl_step[0].astype(jnp.float32) / WARM)
    rows = math.gcd(CELLS, 4096)
    nblocks = CELLS // rows
    pieces = (counts.astype(jnp.float32).reshape(nblocks, rows, G), scale.reshape(nblocks, rows), noise.astype(jnp.float32).reshape(nblocks, rows, LAT), live.reshape(nblocks, rows))
    params = (emb_weight.astype(jnp.float32), ln_gain, ln_bias, lat_weight.astype(jnp.float32), lat_bias, up_weight.astype(jnp.float32), dec_weight.astype(jnp.float32), prior_mean, prior_logvar)

    def forward(pieces, params):
        emb, gain, shift, lat_w, lat_b, up_w, dec_w, pmean, plogv = params
        prec_tab = jnp.exp(-plogv)
        mean_prec = pmean * prec_tab
        const_tab = pmean * pmean * prec_tab + plogv

        def block(carry, piece):
            counts_blk, scale_blk, noise_blk, live_blk = piece
            normed = low(jnp.log1p(counts_blk * scale_blk[:, None]))
            embedded = low_back(hidot(normed, emb.T))
            centred = embedded - lax.optimization_barrier(jnp.mean(embedded, -1, keepdims=True))
            inv_dev = lax.rsqrt(lax.optimization_barrier(jnp.mean(centred * centred, -1, keepdims=True)) + epsilon)
            hidden = centred * inv_dev * gain + shift
            latent = low_back(hidot(low(hidden), lat_w) + lat_b)
            lat_mean = latent[:, :LAT]
            log_var = latent[:, LAT:]
            variance = jnp.exp(log_var)
            sample = low(lat_mean + jnp.exp(0.5 * log_var) * noise_blk)
            mixed = low(low_back(hidden + hidot(sample, up_w.T)))
            decoded = hidot(mixed, dec_w)
            logits = -0.5 * (hidot(lat_mean * lat_mean, prec_tab) - 2.0 * hidot(lat_mean, mean_prec) + lax.optimization_barrier(jnp.sum(const_tab, 0)))
            resp = jax.nn.softmax(logits * LAT ** (-0.5), axis=-1)
            diverge = 0.5 * (hidot(resp, const_tab.T) - log_var + (variance + lat_mean * lat_mean) * hidot(resp, prec_tab.T) - 2.0 * lat_mean * hidot(resp, mean_prec.T) - 1.0)
            return (carry + lax.optimization_barrier(jnp.sum(diverge * live_blk[:, None], 0)), decoded)
        sums, outs = lax.scan(jax.checkpoint(block), jnp.zeros((LAT,), jnp.float32), pieces)
        average = sums / total
        loss = beta * jnp.sum(jnp.maximum(average, free_bits))
        return (outs, loss)
    (outs, loss), pull = jax.vjp(forward, pieces, params)
    piece_grads, param_grads = pull((out_grad.astype(jnp.float32).reshape(nblocks, rows, G), jnp.ones((), jnp.float32)))
    emb_g, gain_g, shift_g, latw_g, latb_g, up_g, dec_g, pmean_g, plogv_g = param_grads
    counts_grad = piece_grads[0].reshape(CELLS, G).astype(jnp.bfloat16)
    decoded = outs.reshape(CELLS, G).astype(jnp.bfloat16)
    return (decoded, counts_grad, emb_g, gain_g, shift_g, latw_g, latb_g, up_g, dec_g, pmean_g, plogv_g, loss.reshape(1))
```

```python
import jax
import jax.numpy as jnp
from jax import lax
from jax.sharding import PartitionSpec as P

WARM = 1000
EPS = 1e-05
FREE = 1.0
BF = jnp.bfloat16
F32 = jnp.float32


def edot(left, right, dims=((1,), (0,))):
    return lax.dot_general(
        left, right, (dims, ((), ())), precision=lax.Precision.HIGHEST, preferred_element_type=F32
    )


def hdot(left, right, dims=((1,), (0,))):
    return lax.dot_general(left, right, (dims, ((), ())), preferred_element_type=F32)


def bits_of(n):
    return n.bit_length() - 1


def flip(x, axis, size, mask):
    return lax.ppermute(x, axis, [(i, i ^ mask) for i in range(size)])


def butterfly(x, axis, size):
    for k in range(bits_of(size)):
        x = x + flip(x, axis, size, 1 << k)
    return x


def scatter_rows(x, axis, size, at):
    for k in range(bits_of(size)):
        bit = (at >> k) & 1
        halves = x.reshape((2, x.shape[0] // 2) + x.shape[1:])
        keep = lax.dynamic_index_in_dim(halves, bit, 0, keepdims=False)
        send = lax.dynamic_index_in_dim(halves, 1 - bit, 0, keepdims=False)
        x = keep.astype(F32) + flip(send.astype(BF), axis, size, 1 << k).astype(F32)
    return x


def gather_rows(x, axis, size, at):
    for k in reversed(range(bits_of(size))):
        bit = (at >> k) & 1
        other = flip(x, axis, size, 1 << k)
        first = jnp.where(bit == 0, x, other)
        second = jnp.where(bit == 0, other, x)
        x = jnp.concatenate([first, second], 0)
    return x


def place_of(at, size):
    block = 0
    for k in range(bits_of(size)):
        block = block * 2 + ((at >> k) & 1)
    return block


def halving(blocks, right, axis, size, order):
    live = list(range(size))
    arrived = {r: [] for r in live}
    for k in order:
        sent = [r for r in live if (r >> k) & 1]
        live = [r for r in live if not (r >> k) & 1]
        part = hdot(jnp.concatenate([blocks[r] for r in sent], 1), right, ((0,), (0,)))
        for got in range(len(arrived[sent[0]])):
            part = part + jnp.concatenate([arrived[r][got] for r in sent], 0).astype(F32)
        came = flip(part.astype(BF), axis, size, 1 << k)
        width = blocks[0].shape[1]
        for i, r in enumerate(sent):
            arrived[r ^ (1 << k)].append(came[i * width : (i + 1) * width])
    total = hdot(blocks[0], right, ((0,), (0,)))
    for part in arrived[0]:
        total = total + part.astype(F32)
    return total


def cut(width, parts):
    step = -(-width // (parts * 128)) * 128
    edges = list(range(0, width, step)) + [width]
    return list(zip(edges[:-1], edges[1:]))


def on_device(
    counts,
    library,
    cell_mask,
    slide_len,
    kl_step,
    noise,
    emb_weight,
    ln_gain,
    ln_bias,
    lat_weight,
    lat_bias,
    up_weight,
    dec_weight,
    prior_mean,
    prior_logvar,
    out_grad,
    ncell,
    ngene,
):
    rows, width = counts.shape
    model = emb_weight.shape[0]
    latent_w = up_weight.shape[1]
    cell_at = lax.axis_index("cells")
    gene_at = lax.axis_index("genes")
    nslide = slide_len.shape[0]
    place = cell_at * rows + jnp.arange(rows, dtype=jnp.int32)
    ends = jnp.cumsum(slide_len)
    slide_of = jnp.sum((ends[None, :] <= place[:, None]).astype(jnp.int32), 1)
    onehot = (slide_of[:, None] == jnp.arange(nslide, dtype=jnp.int32)[None, :]).astype(F32)
    live = cell_mask.astype(F32)
    libsize = library.astype(F32)
    stats = jnp.concatenate(
        [jnp.sum(onehot * (libsize * live)[:, None], 0), jnp.sum(onehot * live[:, None], 0)]
    )
    stats = butterfly(stats, "cells", ncell)
    lib_total, live_total = stats[:nslide], stats[nslide:]
    slide_lib = lib_total / jnp.maximum(live_total, 1.0)
    scale = jnp.sum(onehot * slide_lib[None, :], 1) / libsize
    total = jnp.maximum(jnp.sum(live_total), 1.0)
    beta = jnp.minimum(1.0, kl_step[0].astype(F32) / WARM)

    partial_mixed = hdot(out_grad, dec_weight, ((1,), (1,))).astype(BF)
    mixed_grad = scatter_rows(partial_mixed, "genes", ngene, gene_at).astype(BF)

    counts_f = counts.astype(F32)
    normed = jnp.log(1.0 + counts_f * scale[:, None]).astype(BF)
    partial_embed = hdot(normed, emb_weight, ((1,), (1,))).astype(BF)
    embedded = scatter_rows(partial_embed, "genes", ngene, gene_at)

    mine = rows // ngene
    first = place_of(gene_at, ngene) * mine
    my_noise = lax.dynamic_slice_in_dim(noise, first, mine, 0).astype(F32)
    my_live = lax.dynamic_slice_in_dim(live, first, mine, 0)
    prec = jnp.exp(-prior_logvar)
    mprec = prior_mean * prec
    ctab = prior_mean * mprec + prior_logvar

    centred = embedded - jnp.mean(embedded, -1, keepdims=True)
    inv_dev = lax.rsqrt(jnp.mean(centred * centred, -1, keepdims=True) + EPS)
    normal = centred * inv_dev
    hidden = normal * ln_gain + ln_bias
    hidden_low = hidden.astype(BF)
    latent = hdot(hidden_low, lat_weight) + lat_bias
    lat_mean = latent[:, :latent_w]
    log_var = latent[:, latent_w:]
    variance = jnp.exp(log_var)
    spread = jnp.exp(0.5 * log_var)
    sample_low = (lat_mean + spread * my_noise).astype(BF)
    mixed_mine = (hidden + hdot(sample_low, up_weight, ((1,), (1,)))).astype(BF)
    mixed = gather_rows(mixed_mine, "genes", ngene, gene_at)

    step = model // ncell

    def blocks_of(x):
        return [
            lax.dynamic_slice_in_dim(x, (cell_at ^ r) * step, step, 1) for r in range(ncell)
        ]

    nbits = bits_of(ncell)
    straight = list(range(nbits))
    turned = [1, 0] + straight[2:] if nbits > 1 else straight
    pieces = cut(width, 4)

    def weight_sum(x, right):
        blocks = blocks_of(x)
        outs = []
        for i, (lo, hi) in enumerate(pieces):
            order = turned if i == 0 else straight
            outs.append(halving(blocks, right[:, lo:hi], "cells", ncell, order))
        return jnp.concatenate(outs, 1)

    dec_out = weight_sum(mixed, out_grad)
    decoded = hdot(mixed, dec_weight).astype(BF)

    moment = variance + lat_mean * lat_mean
    square = lat_mean * lat_mean
    logits = -0.5 * (
        edot(
            jnp.concatenate([square, lat_mean], 1), jnp.concatenate([prec, -2.0 * mprec], 0)
        )
        + jnp.sum(ctab, 0)
    )
    resp = jax.nn.softmax(logits * latent_w ** (-0.5), axis=-1)
    spreads = edot(resp, jnp.concatenate([ctab, prec, mprec], 0), ((1,), (1,)))
    resp_ctab = spreads[:, :latent_w]
    resp_prec = spreads[:, latent_w : 2 * latent_w]
    resp_mean = spreads[:, 2 * latent_w :]
    diverge = 0.5 * (
        resp_ctab - log_var + moment * resp_prec - 2.0 * lat_mean * resp_mean - 1.0
    )
    kl_sum = jnp.sum(diverge * my_live[:, None], 0)
    kl_sum = butterfly(butterfly(kl_sum, "genes", ngene), "cells", ncell)
    average = kl_sum / total
    kl_loss = beta * jnp.sum(jnp.maximum(average, FREE))
    active = (average > FREE).astype(F32)
    weight = beta * active[None, :] * my_live[:, None] / total

    up_part = hdot(mixed_grad, sample_low, ((0,), (0,)))
    sample_grad = hdot(mixed_grad, up_weight)
    mean_grad = sample_grad + weight * (lat_mean * resp_prec - resp_mean)
    var_grad = sample_grad * 0.5 * spread * my_noise + 0.5 * weight * (variance * resp_prec - 1.0)
    w_moment = weight * moment
    w_mean = weight * lat_mean
    left3 = jnp.concatenate([weight, w_moment, w_mean], 1)
    resp_grad = 0.5 * edot(left3, jnp.concatenate([ctab, prec, -2.0 * mprec], 0))
    logit_grad = (
        resp * (resp_grad - jnp.sum(resp * resp_grad, -1, keepdims=True)) * latent_w ** (-0.5)
    )
    back = edot(logit_grad, jnp.concatenate([prec, mprec], 0), ((1,), (1,)))
    mean_grad = mean_grad - lat_mean * back[:, :latent_w] + back[:, latent_w:]
    by_resp = edot(left3, resp, ((0,), (0,)))
    by_logit = edot(jnp.concatenate([square, lat_mean], 1), logit_grad, ((0,), (0,)))
    const_grad = 0.5 * by_resp[:latent_w] - 0.5 * jnp.sum(logit_grad, 0)[None, :]
    mprec_grad = by_logit[latent_w:] - by_resp[2 * latent_w :]
    prec_grad = (
        0.5 * by_resp[latent_w : 2 * latent_w]
        - 0.5 * by_logit[:latent_w]
        + prior_mean * prior_mean * const_grad
        + prior_mean * mprec_grad
    )
    pmean_part = 2.0 * prior_mean * prec * const_grad + prec * mprec_grad
    plogv_part = const_grad - prec * prec_grad
    latent_grad = jnp.concatenate([mean_grad, var_grad], 1).astype(BF)
    latb_part = jnp.sum(latent_grad.astype(F32), 0)
    hidden_grad = mixed_grad.astype(F32) + hdot(latent_grad, lat_weight, ((1,), (1,)))
    gain_part = jnp.sum(hidden_grad * normal, 0)
    shift_part = jnp.sum(hidden_grad, 0)
    normal_grad = hidden_grad * ln_gain
    embed_mine = (
        inv_dev
        * (
            normal_grad
            - jnp.mean(normal_grad, -1, keepdims=True)
            - normal * jnp.mean(normal_grad * normal, -1, keepdims=True)
        )
    ).astype(BF)
    embed_grad = gather_rows(embed_mine, "genes", ngene, gene_at)

    emb_out = weight_sum(embed_grad, normed)
    normed_grad = hdot(embed_grad, emb_weight)
    counts_grad = (normed_grad * scale[:, None] / (1.0 + counts_f * scale[:, None])).astype(BF)

    latw_part = hdot(hidden_low, latent_grad, ((0,), (0,)))
    small = jnp.concatenate([latw_part, up_part], 1).astype(BF)
    cols = small.shape[1]
    small = small.reshape(model, ngene, cols // ngene).transpose(1, 0, 2)
    small = scatter_rows(small, "genes", ngene, gene_at)
    small = small.reshape(ncell, step, cols // ngene)
    keepers = [lax.dynamic_index_in_dim(small, cell_at ^ r, 0, keepdims=False) for r in range(ncell)]
    for k in straight:
        sent = [r for r in range(ncell) if keepers[r] is not None and (r >> k) & 1]
        came = flip(jnp.stack([keepers[r] for r in sent]).astype(BF), "cells", ncell, 1 << k)
        for i, r in enumerate(sent):
            keepers[r] = None
            keepers[r ^ (1 << k)] = keepers[r ^ (1 << k)] + came[i].astype(F32)
    share = keepers[0].astype(BF)[None]
    small = gather_rows(share, "genes", ngene, gene_at).astype(F32)
    small = small.transpose(1, 0, 2).reshape(step, cols)
    latw_out = small[:, : 2 * latent_w]
    up_out = small[:, 2 * latent_w :]

    parts = jnp.concatenate(
        [
            gain_part.reshape(-1, 128),
            shift_part.reshape(-1, 128),
            latb_part.reshape(-1, 128),
            pmean_part.reshape(-1, 128),
            plogv_part.reshape(-1, 128),
        ],
        0,
    )
    parts = butterfly(butterfly(parts, "genes", ngene), "cells", ncell)
    vec = model // 128
    tab = pmean_part.size // 128

    def own(flat, full_shape):
        whole = flat.reshape(full_shape)
        each = full_shape[0] // ncell
        return lax.dynamic_slice_in_dim(whole, cell_at * each, each, 0)

    gain_out = own(parts[:vec], (model,))
    shift_out = own(parts[vec : 2 * vec], (model,))
    latb_out = own(parts[2 * vec : 3 * vec], (2 * latent_w,))
    pmean_out = own(parts[3 * vec : 3 * vec + tab], pmean_part.shape)
    plogv_out = own(parts[3 * vec + tab :], plogv_part.shape)
    return (
        decoded,
        counts_grad,
        emb_out,
        gain_out,
        shift_out,
        latw_out,
        latb_out,
        up_out,
        dec_out,
        pmean_out,
        plogv_out,
        kl_loss.reshape(1),
    )


def solution(mesh):
    ncell, ngene = mesh.shape["cells"], mesh.shape["genes"]

    def body(*args):
        return on_device(*args, ncell=ncell, ngene=ngene)

    return jax.shard_map(
        body,
        mesh=mesh,
        in_specs=(
            P("cells", "genes"),
            P("cells"),
            P("cells"),
            P(),
            P(),
            P("cells", None),
            P(None, "genes"),
            P(),
            P(),
            P(),
            P(),
            P(),
            P(None, "genes"),
            P(),
            P(),
            P("cells", "genes"),
        ),
        out_specs=(
            P("cells", "genes"),
            P("cells", "genes"),
            P("cells", "genes"),
            P("cells"),
            P("cells"),
            P("cells", None),
            P("cells"),
            P("cells", None),
            P("cells", "genes"),
            P("cells", None),
            P("cells", None),
            P(),
        ),
        check_vma=False,
    )
```

```python
import functools

import jax
import jax.numpy as jnp
from jax import lax
from jax.experimental import pallas as pl
from jax.experimental.pallas import tpu as pltpu
from jax.sharding import PartitionSpec as P

WARM = 1000
EPS = 1e-05
FREE = 1.0
BF = jnp.bfloat16
F32 = jnp.float32


MESH = pl.DeviceIdType.MESH


def chunks_of(width, step):
    edges = list(range(0, width, step)) + [width]
    return list(zip(edges[:-1], edges[1:]))


def xor_const(at, k_bits, value):
    out=0
    for k in range(k_bits):
        bit=lax.rem(lax.div(at, 1<<k), 2)
        if (value>>k)&1: bit=1-bit
        out=out+bit*(1<<k)
    return out

def rev(i, n):
    return int(format(i, f"0{n}b")[::-1], 2) if n else 0

TILE=256
def sum_kernel(ncell, chunks, *refs):
    nb=bits_of(ncell)
    nch=len(chunks)
    xts=refs[0:2]; rights=refs[2:4]; outs=refs[4:6]
    pos=6
    lefts=refs[pos:pos+2]; pos+=2
    sends=[refs[pos+t*nch:pos+(t+1)*nch] for t in range(2)]; pos+=2*nch
    recvs=[[refs[pos+(t*nch+i)*nb:pos+(t*nch+i+1)*nb] for i in range(nch)] for t in range(2)]; pos+=2*nch*nb
    lsem, ssem, rsem = refs[pos:pos+3]
    at=lax.axis_index("cells")
    model=xts[0].shape[0]
    step=model//ncell
    peers=[xor_const(at,nb,1<<k) for k in range(nb)]
    barrier=pltpu.get_barrier_semaphore()
    for p in peers:
        pl.semaphore_signal(barrier, inc=1, device_id={"cells":p}, device_id_type=MESH)
    loads=[]
    for t in range(2):
        for i in range(ncell):
            src=xor_const(at,nb,rev(i,nb))
            cp=pltpu.make_async_copy(xts[t].at[pl.ds(pl.multiple_of(src*step,step),step)], lefts[t].at[pl.ds(i*step,step)], lsem.at[t])
            cp.start(); loads.append(cp)
    pl.semaphore_wait(barrier, nb)

    def mm(t, c, lo, hi, emit):
        a,b=chunks[c]
        full=(b-a)//TILE
        def one(off, w):
            left=lefts[t][lo:hi,:]
            right=rights[t][:, pl.ds(a+off, w)]
            emit(off, w, jnp.dot(left,right,preferred_element_type=F32))
        if full:
            def body(j,_):
                one(pl.multiple_of(j*TILE,TILE),TILE); return 0
            lax.fori_loop(0,full,body,0)
        if (b-a)%TILE: one(full*TILE,(b-a)%TILE)

    copies={}
    def send(t,c,k,src):
        cp=pltpu.make_async_remote_copy(src_ref=src,dst_ref=recvs[t][c][k],send_sem=ssem.at[t,c,k],recv_sem=rsem.at[t,c,k],
            device_id={"cells":peers[k]},device_id_type=MESH)
        cp.start(); copies[t,c,k]=cp

    def stage(t,c,k):
        h=model>>(k+1)
        for j in range(k):
            if j==k-1: copies[t,c,j].wait_recv()
        if k==0:
            dst=sends[t][c];
            def emit(off,w,v): dst[:,pl.ds(off,w)]=v.astype(BF)
            mm(t,c,h,2*h,emit)
            send(t,c,0,dst)
            return
        dst=recvs[t][c][k-1]
        def emit(off,w,v):
            for j in range(k):
                v=v+recvs[t][c][j][h:2*h,pl.ds(off,w)].astype(F32)
            dst[h:2*h,pl.ds(off,w)]=v.astype(BF)
        mm(t,c,h,2*h,emit)
        send(t,c,k,dst.at[pl.ds(h,h)])

    def final(t,c):
        copies[t,c,nb-1].wait_recv()
        a,b=chunks[c]
        def emit(off,w,v):
            for j in range(nb):
                v=v+recvs[t][c][j][0:step,pl.ds(off,w)].astype(F32)
            outs[t][:,pl.ds(a+off,w)]=v
        mm(t,c,0,step,emit)

    for cp in loads[:ncell]: cp.wait()
    order=[(0,c) for c in range(nch)]+[(1,c) for c in range(nch)]
    n=len(order)
    ahead=3
    for i in range(min(ahead,n)):
        if i==0: pass
        if order[i][0]==1 and i>0 and order[i-1][0]==0:
            for cp in loads[ncell:]: cp.wait()
        stage(*order[i],0)
    for s in range(n+nb):
        if s+ahead<n:
            if order[s+ahead]==(1,0):
                for cp in loads[ncell:]: cp.wait()
            stage(*order[s+ahead],0)
        for k in range(1,nb+1):
            i=s-(k-1)
            if 0<=i<n:
                if k<nb: stage(*order[i],k)
                else: final(*order[i])
    for cp in copies.values(): cp.wait_send()

def pair_sums(xt_a, xt_b, right_a, right_b, ncell, chunk=512):
    model,rows=xt_a.shape; width=right_a.shape[1]
    nb=bits_of(ncell); step=model//ncell
    chunks=chunks_of(width,chunk); nch=len(chunks)
    sends=[pltpu.VMEM((model//2,b-a),BF) for _ in range(2) for a,b in chunks]
    recvs=[pltpu.VMEM((model>>(k+1),b-a),BF) for _ in range(2) for a,b in chunks for k in range(nb)]
    vm=pl.BlockSpec(memory_space=pltpu.VMEM); anyv=pl.BlockSpec(memory_space=pl.ANY)
    return pl.pallas_call(
        functools.partial(sum_kernel,ncell,chunks),
        out_shape=[jax.ShapeDtypeStruct((step,width),F32)]*2,
        in_specs=[anyv,anyv,vm,vm], out_specs=[vm,vm],
        scratch_shapes=[pltpu.VMEM((model,rows),BF)]*2+sends+recvs+[pltpu.SemaphoreType.DMA((2,)),pltpu.SemaphoreType.DMA((2,nch,nb)),pltpu.SemaphoreType.DMA((2,nch,nb))],
        compiler_params=pltpu.CompilerParams(collective_id=0,has_side_effects=True,vmem_limit_bytes=67043328),
        name="pair_sums",
    )(xt_a,xt_b,right_a,right_b)


def edot(left, right, dims=((1,), (0,))):
    return lax.dot_general(
        left, right, (dims, ((), ())), precision=lax.Precision.HIGHEST, preferred_element_type=F32
    )


def hdot(left, right, dims=((1,), (0,))):
    return lax.dot_general(left, right, (dims, ((), ())), preferred_element_type=F32)


def bits_of(n):
    return n.bit_length() - 1


def flip(x, axis, size, mask):
    return lax.ppermute(x, axis, [(i, i ^ mask) for i in range(size)])


def butterfly(x, axis, size):
    for k in range(bits_of(size)):
        x = x + flip(x, axis, size, 1 << k)
    return x


def scatter_rows(x, axis, size, at):
    for k in range(bits_of(size)):
        bit = (at >> k) & 1
        halves = x.reshape((2, x.shape[0] // 2) + x.shape[1:])
        keep = lax.dynamic_index_in_dim(halves, bit, 0, keepdims=False)
        send = lax.dynamic_index_in_dim(halves, 1 - bit, 0, keepdims=False)
        x = keep.astype(F32) + flip(send.astype(BF), axis, size, 1 << k).astype(F32)
    return x


def gather_rows(x, axis, size, at):
    for k in reversed(range(bits_of(size))):
        bit = (at >> k) & 1
        other = flip(x, axis, size, 1 << k)
        first = jnp.where(bit == 0, x, other)
        second = jnp.where(bit == 0, other, x)
        x = jnp.concatenate([first, second], 0)
    return x


def place_of(at, size):
    block = 0
    for k in range(bits_of(size)):
        block = block * 2 + ((at >> k) & 1)
    return block


def on_device(
    counts,
    library,
    cell_mask,
    slide_len,
    kl_step,
    noise,
    emb_weight,
    ln_gain,
    ln_bias,
    lat_weight,
    lat_bias,
    up_weight,
    dec_weight,
    prior_mean,
    prior_logvar,
    out_grad,
    ncell,
    ngene,
):
    rows, width = counts.shape
    model = emb_weight.shape[0]
    latent_w = up_weight.shape[1]
    cell_at = lax.axis_index("cells")
    gene_at = lax.axis_index("genes")
    nslide = slide_len.shape[0]
    place = cell_at * rows + jnp.arange(rows, dtype=jnp.int32)
    ends = jnp.cumsum(slide_len)
    slide_of = jnp.sum((ends[None, :] <= place[:, None]).astype(jnp.int32), 1)
    onehot = (slide_of[:, None] == jnp.arange(nslide, dtype=jnp.int32)[None, :]).astype(F32)
    live = cell_mask.astype(F32)
    libsize = library.astype(F32)
    stats = jnp.concatenate(
        [jnp.sum(onehot * (libsize * live)[:, None], 0), jnp.sum(onehot * live[:, None], 0)]
    )
    stats = butterfly(stats, "cells", ncell)
    lib_total, live_total = stats[:nslide], stats[nslide:]
    slide_lib = lib_total / jnp.maximum(live_total, 1.0)
    scale = jnp.sum(onehot * slide_lib[None, :], 1) / libsize
    total = jnp.maximum(jnp.sum(live_total), 1.0)
    beta = jnp.minimum(1.0, kl_step[0].astype(F32) / WARM)

    partial_mixed = hdot(out_grad, dec_weight, ((1,), (1,))).astype(BF)
    mixed_grad = scatter_rows(partial_mixed, "genes", ngene, gene_at).astype(BF)

    counts_f = counts.astype(F32)
    normed = jnp.log(1.0 + counts_f * scale[:, None]).astype(BF)
    partial_embed = hdot(normed, emb_weight, ((1,), (1,))).astype(BF)
    embedded = scatter_rows(partial_embed, "genes", ngene, gene_at)

    mine = rows // ngene
    first = place_of(gene_at, ngene) * mine
    my_noise = lax.dynamic_slice_in_dim(noise, first, mine, 0).astype(F32)
    my_live = lax.dynamic_slice_in_dim(live, first, mine, 0)
    prec = jnp.exp(-prior_logvar)
    mprec = prior_mean * prec
    ctab = prior_mean * mprec + prior_logvar

    centred = embedded - jnp.mean(embedded, -1, keepdims=True)
    inv_dev = lax.rsqrt(jnp.mean(centred * centred, -1, keepdims=True) + EPS)
    normal = centred * inv_dev
    hidden = normal * ln_gain + ln_bias
    hidden_low = hidden.astype(BF)
    latent = hdot(hidden_low, lat_weight) + lat_bias
    lat_mean = latent[:, :latent_w]
    log_var = latent[:, latent_w:]
    variance = jnp.exp(log_var)
    spread = jnp.exp(0.5 * log_var)
    sample_low = (lat_mean + spread * my_noise).astype(BF)
    mixed_mine = (hidden + hdot(sample_low, up_weight, ((1,), (1,)))).astype(BF)
    mixed = gather_rows(mixed_mine, "genes", ngene, gene_at)

    step = model // ncell
    straight = list(range(bits_of(ncell)))
    decoded = hdot(mixed, dec_weight).astype(BF)

    moment = variance + lat_mean * lat_mean
    square = lat_mean * lat_mean
    logits = -0.5 * (
        edot(
            jnp.concatenate([square, lat_mean], 1), jnp.concatenate([prec, -2.0 * mprec], 0)
        )
        + jnp.sum(ctab, 0)
    )
    resp = jax.nn.softmax(logits * latent_w ** (-0.5), axis=-1)
    spreads = edot(resp, jnp.concatenate([ctab, prec, mprec], 0), ((1,), (1,)))
    resp_ctab = spreads[:, :latent_w]
    resp_prec = spreads[:, latent_w : 2 * latent_w]
    resp_mean = spreads[:, 2 * latent_w :]
    diverge = 0.5 * (
        resp_ctab - log_var + moment * resp_prec - 2.0 * lat_mean * resp_mean - 1.0
    )
    kl_sum = jnp.sum(diverge * my_live[:, None], 0)
    kl_sum = butterfly(butterfly(kl_sum, "genes", ngene), "cells", ncell)
    average = kl_sum / total
    kl_loss = beta * jnp.sum(jnp.maximum(average, FREE))
    active = (average > FREE).astype(F32)
    weight = beta * active[None, :] * my_live[:, None] / total

    up_part = hdot(mixed_grad, sample_low, ((0,), (0,)))
    sample_grad = hdot(mixed_grad, up_weight)
    mean_grad = sample_grad + weight * (lat_mean * resp_prec - resp_mean)
    var_grad = sample_grad * 0.5 * spread * my_noise + 0.5 * weight * (variance * resp_prec - 1.0)
    w_moment = weight * moment
    w_mean = weight * lat_mean
    left3 = jnp.concatenate([weight, w_moment, w_mean], 1)
    resp_grad = 0.5 * edot(left3, jnp.concatenate([ctab, prec, -2.0 * mprec], 0))
    logit_grad = (
        resp * (resp_grad - jnp.sum(resp * resp_grad, -1, keepdims=True)) * latent_w ** (-0.5)
    )
    back = edot(logit_grad, jnp.concatenate([prec, mprec], 0), ((1,), (1,)))
    mean_grad = mean_grad - lat_mean * back[:, :latent_w] + back[:, latent_w:]
    by_resp = edot(left3, resp, ((0,), (0,)))
    by_logit = edot(jnp.concatenate([square, lat_mean], 1), logit_grad, ((0,), (0,)))
    const_grad = 0.5 * by_resp[:latent_w] - 0.5 * jnp.sum(logit_grad, 0)[None, :]
    mprec_grad = by_logit[latent_w:] - by_resp[2 * latent_w :]
    prec_grad = (
        0.5 * by_resp[latent_w : 2 * latent_w]
        - 0.5 * by_logit[:latent_w]
        + prior_mean * prior_mean * const_grad
        + prior_mean * mprec_grad
    )
    pmean_part = 2.0 * prior_mean * prec * const_grad + prec * mprec_grad
    plogv_part = const_grad - prec * prec_grad
    latent_grad = jnp.concatenate([mean_grad, var_grad], 1).astype(BF)
    latb_part = jnp.sum(latent_grad.astype(F32), 0)
    hidden_grad = mixed_grad.astype(F32) + hdot(latent_grad, lat_weight, ((1,), (1,)))
    gain_part = jnp.sum(hidden_grad * normal, 0)
    shift_part = jnp.sum(hidden_grad, 0)
    normal_grad = hidden_grad * ln_gain
    embed_mine = (
        inv_dev
        * (
            normal_grad
            - jnp.mean(normal_grad, -1, keepdims=True)
            - normal * jnp.mean(normal_grad * normal, -1, keepdims=True)
        )
    ).astype(BF)
    embed_grad = gather_rows(embed_mine, "genes", ngene, gene_at)

    dec_out, emb_out = pair_sums(mixed.T, embed_grad.T, out_grad, normed, ncell)
    normed_grad = hdot(embed_grad, emb_weight)
    counts_grad = (normed_grad * scale[:, None] / (1.0 + counts_f * scale[:, None])).astype(BF)

    latw_part = hdot(hidden_low, latent_grad, ((0,), (0,)))
    small = jnp.concatenate([latw_part, up_part], 1).astype(BF)
    cols = small.shape[1]
    small = small.reshape(model, ngene, cols // ngene).transpose(1, 0, 2)
    small = scatter_rows(small, "genes", ngene, gene_at)
    small = small.reshape(ncell, step, cols // ngene)
    keepers = [lax.dynamic_index_in_dim(small, cell_at ^ r, 0, keepdims=False) for r in range(ncell)]
    for k in straight:
        sent = [r for r in range(ncell) if keepers[r] is not None and (r >> k) & 1]
        came = flip(jnp.stack([keepers[r] for r in sent]).astype(BF), "cells", ncell, 1 << k)
        for i, r in enumerate(sent):
            keepers[r] = None
            keepers[r ^ (1 << k)] = keepers[r ^ (1 << k)] + came[i].astype(F32)
    share = keepers[0].astype(BF)[None]
    small = gather_rows(share, "genes", ngene, gene_at).astype(F32)
    small = small.transpose(1, 0, 2).reshape(step, cols)
    latw_out = small[:, : 2 * latent_w]
    up_out = small[:, 2 * latent_w :]

    parts = jnp.concatenate(
        [
            gain_part.reshape(-1, 128),
            shift_part.reshape(-1, 128),
            latb_part.reshape(-1, 128),
            pmean_part.reshape(-1, 128),
            plogv_part.reshape(-1, 128),
        ],
        0,
    )
    parts = butterfly(butterfly(parts, "genes", ngene), "cells", ncell)
    vec = model // 128
    tab = pmean_part.size // 128

    def own(flat, full_shape):
        whole = flat.reshape(full_shape)
        each = full_shape[0] // ncell
        return lax.dynamic_slice_in_dim(whole, cell_at * each, each, 0)

    gain_out = own(parts[:vec], (model,))
    shift_out = own(parts[vec : 2 * vec], (model,))
    latb_out = own(parts[2 * vec : 3 * vec], (2 * latent_w,))
    pmean_out = own(parts[3 * vec : 3 * vec + tab], pmean_part.shape)
    plogv_out = own(parts[3 * vec + tab :], plogv_part.shape)
    return (
        decoded,
        counts_grad,
        emb_out,
        gain_out,
        shift_out,
        latw_out,
        latb_out,
        up_out,
        dec_out,
        pmean_out,
        plogv_out,
        kl_loss.reshape(1),
    )


def solution(mesh):
    ncell, ngene = mesh.shape["cells"], mesh.shape["genes"]

    def body(*args):
        return on_device(*args, ncell=ncell, ngene=ngene)

    return jax.shard_map(
        body,
        mesh=mesh,
        in_specs=(
            P("cells", "genes"),
            P("cells"),
            P("cells"),
            P(),
            P(),
            P("cells", None),
            P(None, "genes"),
            P(),
            P(),
            P(),
            P(),
            P(),
            P(None, "genes"),
            P(),
            P(),
            P("cells", "genes"),
        ),
        out_specs=(
            P("cells", "genes"),
            P("cells", "genes"),
            P("cells", "genes"),
            P("cells"),
            P("cells"),
            P("cells", None),
            P("cells"),
            P("cells", None),
            P("cells", "genes"),
            P("cells", None),
            P("cells", None),
            P(),
        ),
        check_vma=False,
    )
```

```python
import functools

import jax
import jax.numpy as jnp
from jax import lax
from jax.experimental import pallas as pl
from jax.experimental.pallas import tpu as pltpu
from jax.sharding import PartitionSpec as P

WARM = 1000
EPS = 1e-05
FREE = 1.0
BF = jnp.bfloat16
F32 = jnp.float32


MESH = pl.DeviceIdType.MESH


def bits_of(n):
    return n.bit_length() - 1


def bit_of(at, k):
    return lax.rem(lax.div(at, 1 << k), 2)


def xor_of(at, nbits, value):
    out = 0
    for k in range(nbits):
        bit = bit_of(at, k)
        out = out + (1 - bit if (value >> k) & 1 else bit) * (1 << k)
    return out


def reversed_bits(i, n):
    out = 0
    for k in range(n):
        out = out * 2 + ((i >> k) & 1)
    return out


def weight_kernel(cfg, *refs):
    ncell, nch, ch, ahead, inplace = cfg
    nb = bits_of(ncell)
    take = iter(refs)
    og_ref, ct_ref, dw_ref, ew_ref, scale_ref, xm_hbm, xe_hbm, pm_hbm, pe_hbm = [next(take) for _ in range(9)]
    decoded_ref, cgrad_ref, dsum_ref, esum_ref = [next(take) for _ in range(4)]
    xm, xe, pm, pe, keep = [next(take) for _ in range(5)]
    recvs = [next(take) for _ in range(nb)]
    sends = {k: next(take) for k in range(nb) if k not in inplace}
    lsem, ssem, rsem = [next(take) for _ in range(3)]
    model = xm.shape[1]
    step = model // ncell
    half = model // 2
    at = lax.axis_index("cells")
    peers = [xor_of(at, nb, 1 << k) for k in range(nb)]
    s = pl.program_id(0)
    slots = keep.shape[0]

    def loads():
        out = [pltpu.make_async_copy(xm_hbm, xm, lsem.at[0]), pltpu.make_async_copy(xe_hbm, xe, lsem.at[1])]
        for t, (src, dst) in enumerate(((pm_hbm, pm), (pe_hbm, pe))):
            if step % 128:
                out.append(pltpu.make_async_copy(src, dst, lsem.at[2 + t]))
            else:
                for i in range(ncell):
                    block = xor_of(at, nb, reversed_bits(i, nb))
                    out.append(
                        pltpu.make_async_copy(
                            src.at[:, pl.ds(pl.multiple_of(block * step, step), step)],
                            dst.at[:, pl.ds(i * step, step)],
                            lsem.at[2 + t + 2 * i],
                        )
                    )
        return out

    def source(i, k):
        h = model >> (k + 1)
        if k in inplace:
            return recvs[k - 1].at[i, :, pl.ds(h, h)]
        return sends[k].at[i]

    def copy(i, k):
        return pltpu.make_async_remote_copy(
            src_ref=source(i, k),
            dst_ref=recvs[k].at[i],
            send_sem=ssem.at[k, i],
            recv_sem=rsem.at[k, i],
            device_id={"cells": peers[k]},
            device_id_type=MESH,
        )

    @pl.when(s == 0)
    def _():
        for cp in loads():
            cp.start()
        barrier = pltpu.get_barrier_semaphore()
        for p in peers:
            pl.semaphore_signal(barrier, inc=1, device_id={"cells": p}, device_id_type=MESH)
        for cp in loads():
            cp.wait()
        pl.semaphore_wait(barrier, nb)

    def out_parts(i, g, p_ref):
        sends[0][i] = jnp.dot(g, p_ref[:, half:], preferred_element_type=F32).astype(BF)
        copy(i, 0).start()
        keep[lax.rem(i, slots)] = jnp.dot(g, p_ref[:, :half], preferred_element_type=F32)

    @pl.when(s < nch)
    def _():
        out_parts(s, og_ref[...], pm)
        decoded_ref[...] = lax.dot_general(
            dw_ref[...], xm[...], (((1,), (1,)), ((), ())), preferred_element_type=F32
        ).astype(BF)

    @pl.when((s >= nch) & (s < 2 * nch))
    def _():
        scale = scale_ref[...]
        z = 1.0 + ct_ref[...].astype(F32) * scale
        out_parts(s, jnp.log(z).astype(BF), pe)
        grad = lax.dot_general(
            ew_ref[...], xe[...], (((1,), (1,)), ((), ())), preferred_element_type=F32
        )
        z = 1.0 + ct_ref[...].astype(F32) * scale
        cgrad_ref[...] = (grad * scale / z).astype(BF)

    for k in range(1, nb + 1):
        i = s - ahead - (k - 1)

        @pl.when((i >= 0) & (i < 2 * nch))
        def _(i=i, k=k):
            copy(i, k - 1).wait_recv()
            slot = lax.rem(i, slots)
            if k < nb:
                h = model >> (k + 1)
                lo, hi = h, 2 * h
            else:
                lo, hi = 0, step
            v = keep[slot, :, lo:hi]
            for j in range(k):
                v = v + recvs[j][i, :, lo:hi].astype(F32)
            if k < nb:
                if k in inplace:
                    recvs[k - 1][i, :, lo:hi] = v.astype(BF)
                else:
                    sends[k][i] = v.astype(BF)
                copy(i, k).start()
            else:

                @pl.when(i < nch)
                def _():
                    dsum_ref[...] = v

                @pl.when(i >= nch)
                def _():
                    esum_ref[...] = v

    @pl.when(s == pl.num_programs(0) - 1)
    def _():
        def body(i, _):
            for k in range(nb):
                copy(i, k).wait_send()
            return 0

        lax.fori_loop(0, 2 * nch, body, 0)


def weight_step(mixed, embed, og_t, counts_t, dec_t, emb_t, scale, ncell):
    width, rows = og_t.shape
    model = mixed.shape[1]
    nb = bits_of(ncell)
    step = model // ncell
    ch = 384
    nch = -(-width // ch)
    ahead = 3
    inplace = tuple(k for k in range(1, nb) if (model >> (k + 1)) % 128 == 0)
    n = 2 * nch
    if step % 128:
        order = jnp.array([reversed_bits(i, nb) for i in range(ncell)], jnp.int32)
        blocks = lax.axis_index("cells") ^ order
        mixed_p, embed_p = [
            jnp.take(x.reshape(rows, ncell, step), blocks, axis=1).reshape(rows, model)
            for x in (mixed, embed)
        ]
    else:
        mixed_p, embed_p = mixed, embed
    last = nch - 1
    first = lambda s: (jnp.minimum(s, last), 0)
    second = lambda s: (jnp.clip(s - nch, 0, last), 0)
    lag = ahead + nb - 1
    big = lambda f: pl.BlockSpec((ch, rows), f)
    anyv = pl.BlockSpec(memory_space=pl.ANY)
    cfg = (ncell, nch, ch, ahead, inplace)
    outs = pl.pallas_call(
        functools.partial(weight_kernel, cfg),
        grid=(n + lag,),
        out_shape=[
            jax.ShapeDtypeStruct((width, rows), BF),
            jax.ShapeDtypeStruct((width, rows), BF),
            jax.ShapeDtypeStruct((width, step), F32),
            jax.ShapeDtypeStruct((width, step), F32),
        ],
        in_specs=[
            big(first),
            big(second),
            pl.BlockSpec((ch, model), first),
            pl.BlockSpec((ch, model), second),
            pl.BlockSpec((1, rows), lambda s: (0, 0)),
            anyv,
            anyv,
            anyv,
            anyv,
        ],
        out_specs=[
            big(first),
            big(second),
            pl.BlockSpec((ch, step), lambda s: (jnp.clip(s - lag, 0, last), 0)),
            pl.BlockSpec((ch, step), lambda s: (jnp.clip(s - lag - nch, 0, last), 0)),
        ],
        scratch_shapes=[pltpu.VMEM((rows, model), BF)] * 4
        + [pltpu.VMEM((lag + 2, ch, model // 2), F32)]
        + [pltpu.VMEM((n, ch, model >> (k + 1)), BF) for k in range(nb)]
        + [pltpu.VMEM((n, ch, model >> (k + 1)), BF) for k in range(nb) if k not in inplace]
        + [
            pltpu.SemaphoreType.DMA((2 + 2 * ncell,)),
            pltpu.SemaphoreType.DMA((nb, n)),
            pltpu.SemaphoreType.DMA((nb, n)),
        ],
        compiler_params=pltpu.CompilerParams(
            collective_id=0, has_side_effects=True, vmem_limit_bytes=67043328
        ),
        name="weight_step",
    )(og_t, counts_t, dec_t, emb_t, scale, mixed, embed, mixed_p, embed_p)
    return outs


def edot(left, right, dims=((1,), (0,))):
    return lax.dot_general(
        left, right, (dims, ((), ())), precision=lax.Precision.HIGHEST, preferred_element_type=F32
    )


def hdot(left, right, dims=((1,), (0,))):
    return lax.dot_general(left, right, (dims, ((), ())), preferred_element_type=F32)


def flip(x, axis, size, mask):
    return lax.ppermute(x, axis, [(i, i ^ mask) for i in range(size)])


def butterfly(x, axis, size):
    for k in range(bits_of(size)):
        x = x + flip(x, axis, size, 1 << k)
    return x


def scatter_rows(x, axis, size, at):
    for k in range(bits_of(size)):
        bit = (at >> k) & 1
        halves = x.reshape((2, x.shape[0] // 2) + x.shape[1:])
        keep = lax.dynamic_index_in_dim(halves, bit, 0, keepdims=False)
        send = lax.dynamic_index_in_dim(halves, 1 - bit, 0, keepdims=False)
        x = keep.astype(F32) + flip(send.astype(BF), axis, size, 1 << k).astype(F32)
    return x


def gather_rows(x, axis, size, at):
    for k in reversed(range(bits_of(size))):
        bit = (at >> k) & 1
        other = flip(x, axis, size, 1 << k)
        first = jnp.where(bit == 0, x, other)
        second = jnp.where(bit == 0, other, x)
        x = jnp.concatenate([first, second], 0)
    return x


def place_of(at, size):
    block = 0
    for k in range(bits_of(size)):
        block = block * 2 + ((at >> k) & 1)
    return block


def on_device(
    counts,
    library,
    cell_mask,
    slide_len,
    kl_step,
    noise,
    emb_weight,
    ln_gain,
    ln_bias,
    lat_weight,
    lat_bias,
    up_weight,
    dec_weight,
    prior_mean,
    prior_logvar,
    out_grad,
    ncell,
    ngene,
):
    rows, width = counts.shape
    model = emb_weight.shape[0]
    latent_w = up_weight.shape[1]
    cell_at = lax.axis_index("cells")
    gene_at = lax.axis_index("genes")
    nslide = slide_len.shape[0]
    place = cell_at * rows + jnp.arange(rows, dtype=jnp.int32)
    ends = jnp.cumsum(slide_len)
    slide_of = jnp.sum((ends[None, :] <= place[:, None]).astype(jnp.int32), 1)
    onehot = (slide_of[:, None] == jnp.arange(nslide, dtype=jnp.int32)[None, :]).astype(F32)
    live = cell_mask.astype(F32)
    libsize = library.astype(F32)
    stats = jnp.concatenate(
        [jnp.sum(onehot * (libsize * live)[:, None], 0), jnp.sum(onehot * live[:, None], 0)]
    )
    stats = butterfly(stats, "cells", ncell)
    lib_total, live_total = stats[:nslide], stats[nslide:]
    slide_lib = lib_total / jnp.maximum(live_total, 1.0)
    scale = jnp.sum(onehot * slide_lib[None, :], 1) / libsize
    total = jnp.maximum(jnp.sum(live_total), 1.0)
    beta = jnp.minimum(1.0, kl_step[0].astype(F32) / WARM)

    partial_mixed = hdot(out_grad, dec_weight, ((1,), (1,))).astype(BF)
    mixed_grad = scatter_rows(partial_mixed, "genes", ngene, gene_at).astype(BF)

    counts_f = counts.astype(F32)
    normed = jnp.log(1.0 + counts_f * scale[:, None]).astype(BF)
    partial_embed = hdot(normed, emb_weight, ((1,), (1,))).astype(BF)
    embedded = scatter_rows(partial_embed, "genes", ngene, gene_at)

    mine = rows // ngene
    first = place_of(gene_at, ngene) * mine
    my_noise = lax.dynamic_slice_in_dim(noise, first, mine, 0).astype(F32)
    my_live = lax.dynamic_slice_in_dim(live, first, mine, 0)
    prec = jnp.exp(-prior_logvar)
    mprec = prior_mean * prec
    ctab = prior_mean * mprec + prior_logvar

    centred = embedded - jnp.mean(embedded, -1, keepdims=True)
    inv_dev = lax.rsqrt(jnp.mean(centred * centred, -1, keepdims=True) + EPS)
    normal = centred * inv_dev
    hidden = normal * ln_gain + ln_bias
    hidden_low = hidden.astype(BF)
    latent = hdot(hidden_low, lat_weight) + lat_bias
    lat_mean = latent[:, :latent_w]
    log_var = latent[:, latent_w:]
    variance = jnp.exp(log_var)
    spread = jnp.exp(0.5 * log_var)
    sample_low = (lat_mean + spread * my_noise).astype(BF)
    mixed_mine = (hidden + hdot(sample_low, up_weight, ((1,), (1,)))).astype(BF)
    mixed = gather_rows(mixed_mine, "genes", ngene, gene_at)

    step = model // ncell
    straight = list(range(bits_of(ncell)))

    moment = variance + lat_mean * lat_mean
    square = lat_mean * lat_mean
    logits = -0.5 * (
        edot(
            jnp.concatenate([square, lat_mean], 1), jnp.concatenate([prec, -2.0 * mprec], 0)
        )
        + jnp.sum(ctab, 0)
    )
    resp = jax.nn.softmax(logits * latent_w ** (-0.5), axis=-1)
    spreads = edot(resp, jnp.concatenate([ctab, prec, mprec], 0), ((1,), (1,)))
    resp_ctab = spreads[:, :latent_w]
    resp_prec = spreads[:, latent_w : 2 * latent_w]
    resp_mean = spreads[:, 2 * latent_w :]
    diverge = 0.5 * (
        resp_ctab - log_var + moment * resp_prec - 2.0 * lat_mean * resp_mean - 1.0
    )
    kl_sum = jnp.sum(diverge * my_live[:, None], 0)
    kl_sum = butterfly(butterfly(kl_sum, "genes", ngene), "cells", ncell)
    average = kl_sum / total
    kl_loss = beta * jnp.sum(jnp.maximum(average, FREE))
    active = (average > FREE).astype(F32)
    weight = beta * active[None, :] * my_live[:, None] / total

    up_part = hdot(mixed_grad, sample_low, ((0,), (0,)))
    sample_grad = hdot(mixed_grad, up_weight)
    mean_grad = sample_grad + weight * (lat_mean * resp_prec - resp_mean)
    var_grad = sample_grad * 0.5 * spread * my_noise + 0.5 * weight * (variance * resp_prec - 1.0)
    w_moment = weight * moment
    w_mean = weight * lat_mean
    left3 = jnp.concatenate([weight, w_moment, w_mean], 1)
    resp_grad = 0.5 * edot(left3, jnp.concatenate([ctab, prec, -2.0 * mprec], 0))
    logit_grad = (
        resp * (resp_grad - jnp.sum(resp * resp_grad, -1, keepdims=True)) * latent_w ** (-0.5)
    )
    back = edot(logit_grad, jnp.concatenate([prec, mprec], 0), ((1,), (1,)))
    mean_grad = mean_grad - lat_mean * back[:, :latent_w] + back[:, latent_w:]
    by_resp = edot(left3, resp, ((0,), (0,)))
    by_logit = edot(jnp.concatenate([square, lat_mean], 1), logit_grad, ((0,), (0,)))
    const_grad = 0.5 * by_resp[:latent_w] - 0.5 * jnp.sum(logit_grad, 0)[None, :]
    mprec_grad = by_logit[latent_w:] - by_resp[2 * latent_w :]
    prec_grad = (
        0.5 * by_resp[latent_w : 2 * latent_w]
        - 0.5 * by_logit[:latent_w]
        + prior_mean * prior_mean * const_grad
        + prior_mean * mprec_grad
    )
    pmean_part = 2.0 * prior_mean * prec * const_grad + prec * mprec_grad
    plogv_part = const_grad - prec * prec_grad
    latent_grad = jnp.concatenate([mean_grad, var_grad], 1).astype(BF)
    latb_part = jnp.sum(latent_grad.astype(F32), 0)
    hidden_grad = mixed_grad.astype(F32) + hdot(latent_grad, lat_weight, ((1,), (1,)))
    gain_part = jnp.sum(hidden_grad * normal, 0)
    shift_part = jnp.sum(hidden_grad, 0)
    normal_grad = hidden_grad * ln_gain
    embed_mine = (
        inv_dev
        * (
            normal_grad
            - jnp.mean(normal_grad, -1, keepdims=True)
            - normal * jnp.mean(normal_grad * normal, -1, keepdims=True)
        )
    ).astype(BF)
    embed_grad = gather_rows(embed_mine, "genes", ngene, gene_at)

    decoded, counts_grad, dec_out, emb_out = [
        x.T
        for x in weight_step(
            mixed,
            embed_grad,
            out_grad.T,
            counts.T,
            dec_weight.T,
            emb_weight.T,
            scale[None, :],
            ncell,
        )
    ]

    latw_part = hdot(hidden_low, latent_grad, ((0,), (0,)))
    small = jnp.concatenate([latw_part, up_part], 1).astype(BF)
    cols = small.shape[1]
    small = small.reshape(model, ngene, cols // ngene).transpose(1, 0, 2)
    small = scatter_rows(small, "genes", ngene, gene_at)
    small = small.reshape(ncell, step, cols // ngene)
    keepers = [lax.dynamic_index_in_dim(small, cell_at ^ r, 0, keepdims=False) for r in range(ncell)]
    for k in straight:
        sent = [r for r in range(ncell) if keepers[r] is not None and (r >> k) & 1]
        came = flip(jnp.stack([keepers[r] for r in sent]).astype(BF), "cells", ncell, 1 << k)
        for i, r in enumerate(sent):
            keepers[r] = None
            keepers[r ^ (1 << k)] = keepers[r ^ (1 << k)] + came[i].astype(F32)
    share = keepers[0].astype(BF)[None]
    small = gather_rows(share, "genes", ngene, gene_at).astype(F32)
    small = small.transpose(1, 0, 2).reshape(step, cols)
    latw_out = small[:, : 2 * latent_w]
    up_out = small[:, 2 * latent_w :]

    parts = jnp.concatenate(
        [
            gain_part.reshape(-1, 128),
            shift_part.reshape(-1, 128),
            latb_part.reshape(-1, 128),
            pmean_part.reshape(-1, 128),
            plogv_part.reshape(-1, 128),
        ],
        0,
    )
    parts = butterfly(butterfly(parts, "genes", ngene), "cells", ncell)
    vec = model // 128
    tab = pmean_part.size // 128

    def own(flat, full_shape):
        whole = flat.reshape(full_shape)
        each = full_shape[0] // ncell
        return lax.dynamic_slice_in_dim(whole, cell_at * each, each, 0)

    gain_out = own(parts[:vec], (model,))
    shift_out = own(parts[vec : 2 * vec], (model,))
    latb_out = own(parts[2 * vec : 3 * vec], (2 * latent_w,))
    pmean_out = own(parts[3 * vec : 3 * vec + tab], pmean_part.shape)
    plogv_out = own(parts[3 * vec + tab :], plogv_part.shape)
    return (
        decoded,
        counts_grad,
        emb_out,
        gain_out,
        shift_out,
        latw_out,
        latb_out,
        up_out,
        dec_out,
        pmean_out,
        plogv_out,
        kl_loss.reshape(1),
    )


def solution(mesh):
    ncell, ngene = mesh.shape["cells"], mesh.shape["genes"]

    def body(*args):
        return on_device(*args, ncell=ncell, ngene=ngene)

    return jax.shard_map(
        body,
        mesh=mesh,
        in_specs=(
            P("cells", "genes"),
            P("cells"),
            P("cells"),
            P(),
            P(),
            P("cells", None),
            P(None, "genes"),
            P(),
            P(),
            P(),
            P(),
            P(),
            P(None, "genes"),
            P(),
            P(),
            P("cells", "genes"),
        ),
        out_specs=(
            P("cells", "genes"),
            P("cells", "genes"),
            P("cells", "genes"),
            P("cells"),
            P("cells"),
            P("cells", None),
            P("cells"),
            P("cells", None),
            P("cells", "genes"),
            P("cells", None),
            P("cells", None),
            P(),
        ),
        check_vma=False,
    )
```

```python
import functools

import jax
import jax.numpy as jnp
from jax import lax
from jax.experimental import pallas as pl
from jax.experimental.pallas import tpu as pltpu
from jax.sharding import PartitionSpec as P

WARM = 1000
EPS = 1e-05
FREE = 1.0
BF = jnp.bfloat16
F32 = jnp.float32


MESH = pl.DeviceIdType.MESH


def bits_of(n):
    return n.bit_length() - 1


def bit_of(at, k):
    return lax.rem(lax.div(at, 1 << k), 2)


def xor_of(at, nbits, value):
    out = 0
    for k in range(nbits):
        bit = bit_of(at, k)
        out = out + (1 - bit if (value >> k) & 1 else bit) * (1 << k)
    return out


def reversed_bits(i, n):
    out = 0
    for k in range(n):
        out = out * 2 + ((i >> k) & 1)
    return out


def fdot(left, right, dims):
    return lax.dot_general(
        left, right, (dims, ((), ())), precision=lax.Precision.HIGHEST, preferred_element_type=F32
    )


def bdot(left, right, dims):
    return lax.dot_general(left, right, (dims, ((), ())), preferred_element_type=F32)


NN, NT, TN = ((1,), (0,)), ((1,), (1,)), ((0,), (0,))
AHEAD = 3


def main_kernel(cfg, *refs):
    ncell, nch, ch, inplace = cfg
    nb = bits_of(ncell)
    take = iter(refs)

    def some(count):
        return [next(take) for _ in range(count)]

    og_ref, ct_ref, dw_ref, ew_ref, scale_ref = some(5)
    emb_hbm, mg_hbm, noise_hbm, latw_hbm, upw_hbm = some(5)
    rowd_ref, const_ref, gain_ref, bias_ref, latb_ref, pmean_ref, plogv_ref = some(7)
    decoded_ref, cgrad_ref, dsum_ref, esum_ref, small_ref, vec_ref = some(6)
    xm, xe, px, keep = some(4)
    recvs = some(nb)
    sends = {k: next(take) for k in range(nb) if k not in inplace}
    normal, mg, noise, latw, upw, hlow, lmean, lvar, sample, lgrad, resp_s, inv_s, kpart = some(13)
    klbuf, vecbuf, sm_keep, sm_s1, sm_r1, sm_s2, sm_r2 = some(7)
    sm_sc, sm_rc = some(nb), some(nb)
    fin = next(take)
    lsem, ssem, rsem, asend, arecv = some(5)

    rows, model = xm.shape
    mine = rows // 4
    lat = model // 2
    step = model // ncell
    half = model // 2
    at = lax.axis_index("cells")
    gene = lax.axis_index("genes")
    core, wye = bit_of(gene, 0), bit_of(gene, 1)
    home = core * 2 + wye
    peers = [{"cells": xor_of(at, nb, 1 << k)} for k in range(nb)]
    gpeers = [{"genes": xor_of(gene, 2, 1)}, {"genes": xor_of(gene, 2, 2)}]
    allpeers = gpeers + peers
    nall = nb + 2
    s = pl.program_id(0)
    slots = keep.shape[0]

    def remote(src, dst, ssem_at, rsem_at, peer):
        return pltpu.make_async_remote_copy(
            src_ref=src,
            dst_ref=dst,
            send_sem=ssem_at,
            recv_sem=rsem_at,
            device_id=peer,
            device_id_type=MESH,
        )

    def source(i, k):
        h = model >> (k + 1)
        if k in inplace:
            return recvs[k - 1].at[i, :, pl.ds(h, h)]
        return sends[k].at[lax.rem(i, sends[k].shape[0])]

    def copy(i, k):
        return remote(source(i, k), recvs[k].at[i], ssem.at[k, i], rsem.at[k, i], peers[k])

    def free(i, k):
        ring = sends[k].shape[0]

        @pl.when(i >= ring)
        def _():
            copy(i - ring, k).wait_send()

    side = {}

    def add_side(name, src, dst, peer):
        side[name] = (len(side), src, dst, peer)

    def rowblock(ref, b):
        return ref.at[pl.ds(pl.multiple_of(b * mine, mine), mine)]

    for name, ref in (("m", xm), ("e", xe)):
        add_side(name + "core", rowblock(ref, home), rowblock(ref, home), gpeers[0])
        add_side(name + "wye", rowblock(ref, home), rowblock(ref, home), gpeers[1])
        other = core * 2 + (1 - wye)
        add_side(name + "pass", rowblock(ref, other), rowblock(ref, other), gpeers[0])
    for r in range(nall):
        add_side(f"k{r}", klbuf.at[r], klbuf.at[nall + r], allpeers[r])
        add_side(f"v{r}", vecbuf.at[r], vecbuf.at[nall + r], allpeers[r])
    add_side("s1", sm_s1, sm_r1, gpeers[0])
    add_side("s2", sm_s2, sm_r2, gpeers[1])
    for k in range(nb):
        add_side(f"c{k}", sm_sc[k], sm_rc[k], peers[k])
    add_side("f0", fin.at[home], fin.at[home], gpeers[1])
    add_side("f1", fin.at[pl.ds(core * 2, 2)], fin.at[pl.ds(core * 2, 2)], gpeers[0])

    def side_copy(name):
        at_sem, src, dst, peer = side[name]
        return remote(src, dst, asend.at[at_sem], arecv.at[at_sem], peer)

    def start(name):
        side_copy(name).start()

    def got(name):
        side_copy(name).wait_recv()

    def permute(x, sem_at):
        if step % 128 == 0:
            cps = []
            for i in range(ncell):
                block = xor_of(at, nb, reversed_bits(i, nb))
                cps.append(
                    pltpu.make_async_copy(
                        x.at[:, pl.ds(pl.multiple_of(block * step, step), step)],
                        px.at[:, pl.ds(i * step, step)],
                        lsem.at[sem_at + i],
                    )
                )
            for cp in cps:
                cp.start()
            for cp in cps:
                cp.wait()
        else:
            row = lax.broadcasted_iota(jnp.int32, (model, 128), 0)

            def part(j, _):
                col = lax.broadcasted_iota(jnp.int32, (model, 128), 1) + j * 128
                block = col // step
                target = col % step
                for k in range(nb):
                    flag = (block // (1 << (nb - 1 - k))) % 2
                    own = bit_of(at, k)
                    target = target + (flag + own - 2 * flag * own) * ((1 << k) * step)
                pick = (row == target).astype(F32).astype(BF)
                px[:, pl.ds(pl.multiple_of(j * 128, 128), 128)] = jnp.dot(
                    x[...], pick, preferred_element_type=F32
                ).astype(BF)
                return 0

            lax.fori_loop(0, model // 128, part, 0)

    def tables():
        prec = jnp.exp(-plogv_ref[...])
        mprec = pmean_ref[...] * prec
        return prec, mprec, pmean_ref[...] * mprec + plogv_ref[...]

    def loads():
        pairs = ((emb_hbm, normal), (latw_hbm, latw), (upw_hbm, upw), (mg_hbm, mg), (noise_hbm, noise))
        return [pltpu.make_async_copy(a, b, lsem.at[i]) for i, (a, b) in enumerate(pairs)]

    @pl.when(s == 0)
    def _():
        for cp in loads():
            cp.start()
        barrier = pltpu.get_barrier_semaphore()
        for p in allpeers:
            pl.semaphore_signal(barrier, inc=1, device_id=p, device_id_type=MESH)
        for cp in loads():
            cp.wait()
        e = normal[...]
        centred = e - jnp.mean(e, -1, keepdims=True)
        inv = lax.rsqrt(jnp.mean(centred * centred, -1, keepdims=True) + EPS)
        nrm = centred * inv
        normal[...] = nrm
        inv_s[...] = inv
        hidden = nrm * gain_ref[...] + bias_ref[...]
        hlow[...] = hidden.astype(BF)
        latent = bdot(hlow[...], latw[...], NN) + latb_ref[...]
        lm, lv = latent[:, :lat], latent[:, lat:]
        lmean[...] = lm
        lvar[...] = lv
        sample[...] = (lm + jnp.exp(0.5 * lv) * noise[...].astype(F32)).astype(BF)
        mixed = normal[...] * gain_ref[...] + bias_ref[...] + bdot(sample[...], upw[...], NT)
        xm[pl.ds(pl.multiple_of(home * mine, mine), mine), :] = mixed.astype(BF)
        pl.semaphore_wait(barrier, nall)
        start("mwye")
        start("mcore")
        prec, mprec, ctab = tables()
        lm, lv = lmean[...], lvar[...]
        csum = fdot(jnp.ones((8, lat), F32), ctab, NT)[0:1]
        logits = -0.5 * (fdot(lm * lm, prec, NT) - 2.0 * fdot(lm, mprec, NT) + csum)
        logits = logits * lat ** (-0.5)
        top = jnp.exp(logits - jnp.max(logits, -1, keepdims=True))
        resp = top / jnp.sum(top, -1, keepdims=True)
        resp_s[...] = resp
        moment = jnp.exp(lv) + lm * lm
        diverge = 0.5 * (
            fdot(resp, ctab, NN)
            - lv
            + moment * fdot(resp, prec, NN)
            - 2.0 * lm * fdot(resp, mprec, NN)
            - 1.0
        )
        klbuf[0] = jnp.sum(diverge * rowd_ref[:, 0:1], 0, keepdims=True)
        start("k0")
        got("mwye")
        start("mpass")
        got("mcore")
        got("mpass")
        permute(xm, 0)

    def out_parts(i, g):
        free(i, 0)
        sends[0][lax.rem(i, sends[0].shape[0])] = jnp.dot(
            g, px[:, half:], preferred_element_type=F32
        ).astype(BF)
        copy(i, 0).start()
        keep[lax.rem(i, slots)] = jnp.dot(g, px[:, :half], preferred_element_type=F32)

    @pl.when(s < nch)
    def _():
        out_parts(s, og_ref[...])
        decoded_ref[...] = bdot(dw_ref[...], xm[...], NT).astype(BF)

    @pl.when((s >= nch) & (s < 2 * nch))
    def _():
        scale = scale_ref[...]
        z = 1.0 + ct_ref[...].astype(F32) * scale
        out_parts(s, jnp.log(z).astype(BF))
        grad = bdot(ew_ref[...], xe[...], NT)
        z = 1.0 + ct_ref[...].astype(F32) * scale
        cgrad_ref[...] = (grad * scale / z).astype(BF)

    for k in range(1, nb + 1):
        i = s - AHEAD - (k - 1)

        @pl.when((i >= 0) & (i < 2 * nch))
        def _(i=i, k=k):
            copy(i, k - 1).wait_recv()
            slot = lax.rem(i, slots)
            if k < nb:
                h = model >> (k + 1)
                lo, hi = h, 2 * h
            else:
                lo, hi = 0, step
            v = keep[slot, :, lo:hi]
            for j in range(k):
                v = v + recvs[j][i, :, lo:hi].astype(F32)
            if k < nb:
                if k in inplace:
                    recvs[k - 1][i, :, lo:hi] = v.astype(BF)
                else:
                    free(i, k)
                    sends[k][lax.rem(i, sends[k].shape[0])] = v.astype(BF)
                copy(i, k).start()
            else:

                @pl.when(i < nch)
                def _():
                    dsum_ref[...] = v

                @pl.when(i >= nch)
                def _():
                    esum_ref[...] = v

    plan = {}

    def at_step(step_no):
        def put(fn):
            plan.setdefault(step_no, []).append(fn)
            return fn

        return put

    per = -(-nall // 4)
    for r in range(nall):

        @at_step(1 + r // per)
        def _(r=r):
            got(f"k{r}")
            v = klbuf[r] + klbuf[nall + r]
            if r + 1 < nall:
                klbuf[r + 1] = v
                start(f"k{r + 1}")
            else:
                kpart[...] = v

    back = 2 + (nall - 1) // per

    @at_step(back)
    def _():
        prec, mprec, ctab = tables()
        lm, lv = lmean[...], lvar[...]
        average = kpart[...] / const_ref[0:1]
        loss = const_ref[1:2] * jnp.sum(jnp.maximum(average, FREE), -1, keepdims=True)
        active = (average > FREE).astype(F32)
        weight = rowd_ref[:, 1:2] * active
        resp = resp_s[...]
        rprec = fdot(resp, prec, NN)
        rmean = fdot(resp, mprec, NN)
        variance = jnp.exp(lv)
        moment = variance + lm * lm
        wmom, wmean = weight * moment, weight * lm
        rgrad = 0.5 * (
            fdot(weight, ctab, NT) + fdot(wmom, prec, NT) - 2.0 * fdot(wmean, mprec, NT)
        )
        logit = resp * (rgrad - jnp.sum(resp * rgrad, -1, keepdims=True)) * lat ** (-0.5)
        sgrad = bdot(mg[...], upw[...], NN)
        mgrad = (
            sgrad
            + weight * (lm * rprec - rmean)
            - lm * fdot(logit, prec, NN)
            + fdot(logit, mprec, NN)
        )
        vgrad = sgrad * 0.5 * jnp.exp(0.5 * lv) * noise[...].astype(F32) + 0.5 * weight * (
            variance * rprec - 1.0
        )
        lgrad[:, :lat] = mgrad.astype(BF)
        lgrad[:, lat:] = vgrad.astype(BF)
        lcol = fdot(logit, jnp.ones((mine, 128), F32), TN)[:, 0:1]
        cg = 0.5 * fdot(resp, weight, TN) - 0.5 * lcol
        mpg = fdot(logit, lm, TN) - fdot(resp, wmean, TN)
        pmean = pmean_ref[...]
        pg = (
            0.5 * fdot(resp, wmom, TN)
            - 0.5 * fdot(logit, lm * lm, TN)
            + pmean * pmean * cg
            + pmean * mpg
        )
        nk = pmean.shape[0]
        vecbuf[0, 0:nk] = 2.0 * pmean * prec * cg + prec * mpg
        vecbuf[0, nk : 2 * nk] = cg - prec * pg
        base = 2 * nk
        vecbuf[0, base : base + 1] = loss * jnp.ones((1, lat), F32)
        lg = lgrad[...]
        lb = jnp.sum(lg.astype(F32), 0, keepdims=True)
        hgrad = mg[...].astype(F32) + bdot(lg, latw[...], NT)
        nrm = normal[...]
        gg = jnp.sum(hgrad * nrm, 0, keepdims=True)
        sg = jnp.sum(hgrad, 0, keepdims=True)
        for j, row in enumerate((gg, sg, lb)):
            for part in range(2):
                r = base + 1 + 2 * j + part
                vecbuf[0, r : r + 1] = row[:, part * lat : (part + 1) * lat]
        vecbuf[0, base + 7 : base + 8] = jnp.zeros((1, lat), F32)
        ng = hgrad * gain_ref[...]
        eg = inv_s[...] * (
            ng - jnp.mean(ng, -1, keepdims=True) - nrm * jnp.mean(ng * nrm, -1, keepdims=True)
        )
        xe[pl.ds(pl.multiple_of(home * mine, mine), mine), :] = eg.astype(BF)
        start("ewye")
        start("ecore")
        start("v0")

    @at_step(back + 1)
    def _():
        quarter = 3 * lat // 4

        def put(q, lo, hi, left, right):
            v = bdot(left, right, TN)

            @pl.when(core == q // 2)
            def _():
                sm_keep[q % 2, :, lo:hi] = v

            @pl.when(core != q // 2)
            def _():
                sm_s1[q % 2, :, lo:hi] = v.astype(BF)

        cut = 2 * lat - 2 * quarter
        put(0, 0, quarter, hlow[...], lgrad[:, :quarter])
        put(1, 0, quarter, hlow[...], lgrad[:, quarter : 2 * quarter])
        put(2, 0, cut, hlow[...], lgrad[:, 2 * quarter :])
        put(2, cut, quarter, mg[...], sample[:, : quarter - cut])
        put(3, 0, quarter, mg[...], sample[:, quarter - cut :])
        start("s1")
        got("ewye")
        start("epass")

    @at_step(nch - 1)
    def _():
        got("ecore")
        got("epass")
        permute(xe, ncell)

    assert back + 1 < nch - 1
    for r in range(nall):

        @at_step(back + 2 + r)
        def _(r=r):
            got(f"v{r}")
            v = vecbuf[r] + vecbuf[nall + r]
            if r + 1 < nall:
                vecbuf[r + 1] = v
                start(f"v{r + 1}")
            else:
                vec_ref[...] = v

    @at_step(back + 2)
    def _():
        got("s1")
        sm_keep[wye] = sm_keep[wye] + sm_r1[wye].astype(F32)
        sm_s2[...] = (sm_keep[1 - wye] + sm_r1[1 - wye].astype(F32)).astype(BF)
        start("s2")

    def span(k):
        base = 0
        for j in reversed(range(k + 1, nb)):
            base = base + bit_of(at, j) * (step << j)
        bit = bit_of(at, k)
        size = step << k
        return (
            pl.ds(pl.multiple_of(base + bit * size, step), size),
            pl.ds(pl.multiple_of(base + (1 - bit) * size, step), size),
        )

    @at_step(back + 3)
    def _():
        got("s2")
        sm_keep[wye] = sm_keep[wye] + sm_r2[...].astype(F32)
        sm_sc[nb - 1][...] = sm_keep[wye, span(nb - 1)[1], :].astype(BF)
        start(f"c{nb - 1}")

    for k in reversed(range(nb)):

        @at_step(back + 3 + nb - k)
        def _(k=k):
            got(f"c{k}")
            kept = span(k)[0]
            sm_keep[wye, kept, :] = sm_keep[wye, kept, :] + sm_rc[k][...].astype(F32)
            if k:
                sm_sc[k - 1][...] = sm_keep[wye, span(k - 1)[1], :].astype(BF)
                start(f"c{k - 1}")
            else:
                fin[home] = sm_keep[wye, kept, :].astype(BF)
                start("f0")

    @at_step(back + 4 + nb)
    def _():
        got("f0")
        start("f1")

    @at_step(back + 5 + nb)
    def _():
        got("f1")
        small_ref[...] = fin[...].astype(F32)

    for step_no in sorted(plan):

        @pl.when(s == step_no)
        def _(fns=plan[step_no]):
            for fn in fns:
                fn()

    @pl.when(s == pl.num_programs(0) - 1)
    def _():
        def body(i, _):
            for k in range(nb):
                if k in inplace:
                    copy(i, k).wait_send()
                else:

                    @pl.when(i >= 2 * nch - sends[k].shape[0])
                    def _(k=k):
                        copy(i, k).wait_send()

            return 0

        lax.fori_loop(0, 2 * nch, body, 0)
        for name in side:
            side_copy(name).wait_send()


def main_step(
    embedded, mixed_grad, noise, lat_w, up_w, rowd, const, gain, bias, lat_b, pmean_t, plogv_t,
    og_t, counts_t, dec_t, emb_t, scale, ncell
):
    width, rows = og_t.shape
    mine, model = embedded.shape
    lat = up_w.shape[1]
    nb = bits_of(ncell)
    nall = nb + 2
    step = model // ncell
    ch = 384 if step % 128 == 0 else 192
    nch = -(-width // ch)
    inplace = tuple(k for k in range(1, nb) if (model >> (k + 1)) % 128 == 0)
    n = 2 * nch
    last = nch - 1
    first = lambda s: (jnp.minimum(s, last), 0)
    second = lambda s: (jnp.clip(s - nch, 0, last), 0)
    fixed = lambda *shape: pl.BlockSpec(shape, lambda s: (0,) * len(shape))
    lag = AHEAD + nb - 1
    ring = AHEAD + 2
    quarter = 3 * lat // 4
    nk = pmean_t.shape[0]
    vec = 2 * nk + 8
    anyv = pl.BlockSpec(memory_space=pl.ANY)
    nside = 6 + 2 * nall + 2 + nb + 2
    vm = pltpu.VMEM
    return pl.pallas_call(
        functools.partial(main_kernel, (ncell, nch, ch, inplace)),
        grid=(n + lag,),
        out_shape=[
            jax.ShapeDtypeStruct((width, rows), BF),
            jax.ShapeDtypeStruct((width, rows), BF),
            jax.ShapeDtypeStruct((width, step), F32),
            jax.ShapeDtypeStruct((width, step), F32),
            jax.ShapeDtypeStruct((4, step, quarter), F32),
            jax.ShapeDtypeStruct((vec, lat), F32),
        ],
        in_specs=[
            pl.BlockSpec((ch, rows), first),
            pl.BlockSpec((ch, rows), second),
            pl.BlockSpec((ch, model), first),
            pl.BlockSpec((ch, model), second),
            fixed(1, rows),
            anyv,
            anyv,
            anyv,
            anyv,
            anyv,
            fixed(mine, 8),
            fixed(8, lat),
            fixed(1, model),
            fixed(1, model),
            fixed(1, model),
            fixed(nk, lat),
            fixed(nk, lat),
        ],
        out_specs=[
            pl.BlockSpec((ch, rows), first),
            pl.BlockSpec((ch, rows), second),
            pl.BlockSpec((ch, step), lambda s: (jnp.clip(s - lag, 0, last), 0)),
            pl.BlockSpec((ch, step), lambda s: (jnp.clip(s - lag - nch, 0, last), 0)),
            fixed(4, step, quarter),
            fixed(vec, lat),
        ],
        scratch_shapes=[vm((rows, model), BF)] * 3
        + [vm((lag + 2, ch, model // 2), F32)]
        + [vm((n, ch, model >> (k + 1)), BF) for k in range(nb)]
        + [vm((ring, ch, model >> (k + 1)), BF) for k in range(nb) if k not in inplace]
        + [
            vm((mine, model), F32),
            vm((mine, model), BF),
            vm((mine, lat), BF),
            vm((model, 2 * lat), BF),
            vm((model, lat), BF),
            vm((mine, model), BF),
            vm((mine, lat), F32),
            vm((mine, lat), F32),
            vm((mine, lat), BF),
            vm((mine, 2 * lat), BF),
            vm((mine, nk), F32),
            vm((mine, 1), F32),
            vm((1, lat), F32),
            vm((2 * nall, 1, lat), F32),
            vm((2 * nall, vec, lat), F32),
            vm((2, model, quarter), F32),
            vm((2, model, quarter), BF),
            vm((2, model, quarter), BF),
            vm((model, quarter), BF),
            vm((model, quarter), BF),
        ]
        + [vm((step << k, quarter), BF) for k in range(nb)] * 2
        + [
            vm((4, step, quarter), BF),
            pltpu.SemaphoreType.DMA((max(5, 2 * ncell),)),
            pltpu.SemaphoreType.DMA((nb, n)),
            pltpu.SemaphoreType.DMA((nb, n)),
            pltpu.SemaphoreType.DMA((nside,)),
            pltpu.SemaphoreType.DMA((nside,)),
        ],
        compiler_params=pltpu.CompilerParams(
            collective_id=0, has_side_effects=True, vmem_limit_bytes=67043328
        ),
        name="main_step",
    )(
        og_t, counts_t, dec_t, emb_t, scale, embedded, mixed_grad, noise, lat_w, up_w,
        rowd, const, gain, bias, lat_b, pmean_t, plogv_t,
    )


def hdot(left, right, dims=((1,), (0,))):
    return lax.dot_general(left, right, (dims, ((), ())), preferred_element_type=F32)


def flip(x, axis, size, mask):
    return lax.ppermute(x, axis, [(i, i ^ mask) for i in range(size)])


def butterfly(x, axis, size):
    for k in range(bits_of(size)):
        x = x + flip(x, axis, size, 1 << k)
    return x


def scatter_rows(x, axis, size, at):
    for k in range(bits_of(size)):
        bit = (at >> k) & 1
        halves = x.reshape((2, x.shape[0] // 2) + x.shape[1:])
        keep = lax.dynamic_index_in_dim(halves, bit, 0, keepdims=False)
        send = lax.dynamic_index_in_dim(halves, 1 - bit, 0, keepdims=False)
        x = keep.astype(F32) + flip(send.astype(BF), axis, size, 1 << k).astype(F32)
    return x


def place_of(at, size):
    block = 0
    for k in range(bits_of(size)):
        block = block * 2 + ((at >> k) & 1)
    return block


def on_device(
    counts,
    library,
    cell_mask,
    slide_len,
    kl_step,
    noise,
    emb_weight,
    ln_gain,
    ln_bias,
    lat_weight,
    lat_bias,
    up_weight,
    dec_weight,
    prior_mean,
    prior_logvar,
    out_grad,
    ncell,
    ngene,
):
    rows, width = counts.shape
    model = emb_weight.shape[0]
    latent_w = up_weight.shape[1]
    cell_at = lax.axis_index("cells")
    gene_at = lax.axis_index("genes")
    nslide = slide_len.shape[0]
    place = cell_at * rows + jnp.arange(rows, dtype=jnp.int32)
    ends = jnp.cumsum(slide_len)
    slide_of = jnp.sum((ends[None, :] <= place[:, None]).astype(jnp.int32), 1)
    onehot = (slide_of[:, None] == jnp.arange(nslide, dtype=jnp.int32)[None, :]).astype(F32)
    live = cell_mask.astype(F32)
    libsize = library.astype(F32)
    stats = jnp.concatenate(
        [jnp.sum(onehot * (libsize * live)[:, None], 0), jnp.sum(onehot * live[:, None], 0)]
    )
    stats = butterfly(stats, "cells", ncell)
    lib_total, live_total = stats[:nslide], stats[nslide:]
    slide_lib = lib_total / jnp.maximum(live_total, 1.0)
    scale = jnp.sum(onehot * slide_lib[None, :], 1) / libsize
    total = jnp.maximum(jnp.sum(live_total), 1.0)
    beta = jnp.minimum(1.0, kl_step[0].astype(F32) / WARM)

    partial_mixed = hdot(out_grad, dec_weight, ((1,), (1,))).astype(BF)
    mixed_grad = scatter_rows(partial_mixed, "genes", ngene, gene_at).astype(BF)

    counts_f = counts.astype(F32)
    normed = jnp.log(1.0 + counts_f * scale[:, None]).astype(BF)
    partial_embed = hdot(normed, emb_weight, ((1,), (1,))).astype(BF)
    embedded = scatter_rows(partial_embed, "genes", ngene, gene_at)

    mine = rows // ngene
    first = place_of(gene_at, ngene) * mine
    my_noise = lax.dynamic_slice_in_dim(noise, first, mine, 0)
    my_live = lax.dynamic_slice_in_dim(live, first, mine, 0)
    rowd = jnp.concatenate(
        [my_live[:, None], (beta * my_live / total)[:, None], jnp.zeros((mine, 6), F32)], 1
    )
    const = jnp.concatenate(
        [
            jnp.full((1, latent_w), 1.0) * total,
            jnp.full((1, latent_w), 1.0) * beta,
            jnp.zeros((6, latent_w), F32),
        ],
        0,
    )
    decoded, counts_grad, dec_out, emb_out, small, vec = main_step(
        embedded, mixed_grad, my_noise, lat_weight, up_weight, rowd, const,
        ln_gain[None, :], ln_bias[None, :], lat_bias[None, :], prior_mean.T, prior_logvar.T,
        out_grad.T, counts.T, dec_weight.T, emb_weight.T, scale[None, :], ncell,
    )
    decoded, counts_grad, dec_out, emb_out = decoded.T, counts_grad.T, dec_out.T, emb_out.T
    step = model // ncell
    small = small.transpose(1, 0, 2).reshape(step, 3 * latent_w)
    latw_out = small[:, : 2 * latent_w]
    up_out = small[:, 2 * latent_w :]
    nk = prior_mean.shape[1]

    def own(x, each, axis):
        return lax.dynamic_slice_in_dim(x, cell_at * each, each, axis)

    pmean_out = own(vec[:nk], latent_w // ncell, 1).T
    plogv_out = own(vec[nk : 2 * nk], latent_w // ncell, 1).T
    base = 2 * nk
    kl_loss = vec[base, :1] / (ncell * ngene)
    gain_out, shift_out, latb_out = [
        own(vec[base + 1 + 2 * j : base + 3 + 2 * j].reshape(model), step, 0) for j in range(3)
    ]
    return (
        decoded,
        counts_grad,
        emb_out,
        gain_out,
        shift_out,
        latw_out,
        latb_out,
        up_out,
        dec_out,
        pmean_out,
        plogv_out,
        kl_loss,
    )


def solution(mesh):
    ncell, ngene = mesh.shape["cells"], mesh.shape["genes"]

    def body(*args):
        return on_device(*args, ncell=ncell, ngene=ngene)

    return jax.shard_map(
        body,
        mesh=mesh,
        in_specs=(
            P("cells", "genes"),
            P("cells"),
            P("cells"),
            P(),
            P(),
            P("cells", None),
            P(None, "genes"),
            P(),
            P(),
            P(),
            P(),
            P(),
            P(None, "genes"),
            P(),
            P(),
            P("cells", "genes"),
        ),
        out_specs=(
            P("cells", "genes"),
            P("cells", "genes"),
            P("cells", "genes"),
            P("cells"),
            P("cells"),
            P("cells", None),
            P("cells"),
            P("cells", None),
            P("cells", "genes"),
            P("cells", None),
            P("cells", None),
            P(),
        ),
        check_vma=False,
    )
```

```python
import functools

import jax
import jax.numpy as jnp
from jax import lax
from jax.experimental import pallas as pl
from jax.experimental.pallas import tpu as pltpu
from jax.sharding import PartitionSpec as P

WARM = 1000
EPS = 1e-05
FREE = 1.0
BF = jnp.bfloat16
F32 = jnp.float32


MESH = pl.DeviceIdType.MESH


def bits_of(n):
    return n.bit_length() - 1


def bit_of(at, k):
    return lax.rem(lax.div(at, 1 << k), 2)


def xor_of(at, nbits, value):
    out = 0
    for k in range(nbits):
        bit = bit_of(at, k)
        out = out + (1 - bit if (value >> k) & 1 else bit) * (1 << k)
    return out


def reversed_bits(i, n):
    out = 0
    for k in range(n):
        out = out * 2 + ((i >> k) & 1)
    return out


def fdot(left, right, dims):
    return lax.dot_general(
        left, right, (dims, ((), ())), precision=lax.Precision.HIGHEST, preferred_element_type=F32
    )


def bdot(left, right, dims):
    return lax.dot_general(left, right, (dims, ((), ())), preferred_element_type=F32)


NN, NT, TN = ((1,), (0,)), ((1,), (1,)), ((0,), (0,))
AHEAD = 3


def front_kernel(cfg, *refs):
    ncell, nslide, lat = cfg
    nb = bits_of(ncell)
    slen_ref, kls_ref, lib_ref, mask_ref, ct_hbm, og_hbm, et_hbm, dt_hbm = refs[:8]
    emb_ref, mgk_ref, mgs_ref, scale_ref, const_ref, rowd_ref = refs[8:14]
    ct, og, et, dt, low, msend, mrecv, esend, erecv, ysend, yrecv, stb, stv = refs[14:27]
    lsem, asend, arecv = refs[27:]
    rows = lib_ref.shape[1]
    mine = rows // 4
    top = stv.shape[0] // 2
    at = lax.axis_index("cells")
    gene = lax.axis_index("genes")
    core, wye = bit_of(gene, 0), bit_of(gene, 1)
    home = core * 2 + wye
    peers = [{"cells": xor_of(at, nb, 1 << k)} for k in range(nb)]
    gpeers = [{"genes": xor_of(gene, 2, 1)}, {"genes": xor_of(gene, 2, 2)}]
    s = pl.program_id(0)

    def block_of(j):
        far, away = 1 - lax.rem(j, 2), 1 - lax.div(j, 2)
        side = far * (1 - core) + (1 - far) * core
        return side * 2 + away * (1 - wye) + (1 - away) * wye

    def cols(j):
        return pl.ds(pl.multiple_of(block_of(j) * mine, mine), mine)

    def load(which, j):
        src, dst = ((og_hbm, og), (ct_hbm, ct))[which]
        return pltpu.make_async_copy(src.at[:, cols(j)], dst.at[j], lsem.at[2 + 4 * which + j])

    def whole(which):
        src, dst = ((dt_hbm, dt), (et_hbm, et))[which]
        return pltpu.make_async_copy(src, dst, lsem.at[which])

    def remote(src, dst, sem, peer):
        return pltpu.make_async_remote_copy(
            src_ref=src,
            dst_ref=dst,
            send_sem=asend.at[sem],
            recv_sem=arecv.at[sem],
            device_id=peer,
            device_id_type=MESH,
        )

    def mcopy(h):
        return remote(msend.at[h], mrecv.at[h], h, gpeers[0])

    def ecopy(h):
        return remote(esend.at[h], erecv.at[h], 2 + h, gpeers[0])

    def ycopy():
        return remote(ysend, yrecv, 4, gpeers[1])

    def scopy(r):
        return remote(stb.at[r], stb.at[nb + r], 5 + r, peers[r])

    def slides():
        place = at * rows + lax.broadcasted_iota(jnp.int32, (1, rows), 1)
        begin = 0
        for q in range(nslide):
            end = begin + slen_ref[q]
            yield q, ((place >= begin) & (place < end)).astype(F32)
            begin = end

    def round_done(r):
        scopy(r).wait_recv()
        v = stb[r] + stb[nb + r]
        if r + 1 < nb:
            stb[r + 1] = v
            scopy(r + 1).start()
        else:
            stv[...] = v

    @pl.when(s == 0)
    def _():
        barrier = pltpu.get_barrier_semaphore()
        for p in peers + gpeers:
            pl.semaphore_signal(barrier, inc=1, device_id=p, device_id_type=MESH)
        whole(0).start()
        load(0, 0).start()
        load(0, 1).start()
        whole(1).start()
        for j in range(4):
            load(1, j).start()
        load(0, 2).start()
        load(0, 3).start()
        stb[0] = jnp.zeros_like(stv)
        live = mask_ref[...].astype(F32)
        libsize = lib_ref[...].astype(F32)
        for q, row in slides():
            stb[0, q : q + 1] = jnp.sum(row * (libsize * live), 1, keepdims=True) * jnp.ones(
                (1, 128), F32
            )
            stb[0, top + q : top + q + 1] = jnp.sum(
                row * live, 1, keepdims=True
            ) * jnp.ones((1, 128), F32)
        pl.semaphore_wait(barrier, nb + 2)
        scopy(0).start()
        whole(0).wait()

    @pl.when(s == 1)
    def _():
        round_done(0)

    @pl.when(s == 2)
    def _():
        for r in range(1, nb):
            round_done(r)
        whole(1).wait()
        live = mask_ref[...].astype(F32)
        total = jnp.zeros((1, 1), F32)
        scale = jnp.zeros((1, rows), F32)
        for q, row in slides():
            count = stv[top + q : top + q + 1, 0:1]
            scale = scale + row * (stv[q : q + 1, 0:1] / jnp.maximum(count, 1.0))
            total = total + count
        scale_ref[...] = scale / lib_ref[...].astype(F32)
        total = jnp.maximum(total, 1.0)
        beta = jnp.minimum(1.0, kls_ref[0].astype(F32) / WARM)
        line = lax.broadcasted_iota(jnp.int32, (8, lat), 0)
        const_ref[...] = jnp.where(line == 0, total, beta)
        own = mask_ref[:, pl.ds(pl.multiple_of(home * mine, mine), mine)].astype(F32)
        line = lax.broadcasted_iota(jnp.int32, (8, mine), 0)
        both = jnp.where(line == 0, own, jnp.where(line == 1, beta * own / total, 0.0))
        eye = (
            lax.broadcasted_iota(jnp.int32, (8, 128), 0)
            == lax.broadcasted_iota(jnp.int32, (8, 128), 1)
        ).astype(F32)
        rowd_ref[...] = fdot(both, eye, TN)

    def out_block(j, part):
        h = lax.div(j, 2)

        @pl.when(lax.rem(j, 2) == 0)
        def _():
            msend[h] = part.astype(BF)
            mcopy(h).start()

        @pl.when(j == 1)
        def _():
            mcopy(0).wait_recv()
            mgs_ref[...] = (part + mrecv[0].astype(F32)).astype(BF)

        @pl.when(j == 3)
        def _():
            mcopy(1).wait_recv()
            mgk_ref[...] = part + mrecv[1].astype(F32)

    @pl.when((s < 2) | (s >= 6))
    def _():
        j = s - 4 * lax.div(s, 6)
        load(0, j).wait()
        out_block(j, bdot(og[j], dt[...], TN))

    @pl.when((s >= 2) & (s < 6))
    def _():
        j = s - 2
        h = lax.div(j, 2)
        load(1, j).wait()
        low[...] = jnp.log(1.0 + ct[j].astype(F32) * scale_ref[:, cols(j)]).astype(BF)
        part = bdot(low[...], et[...], TN)

        @pl.when(lax.rem(j, 2) == 0)
        def _():
            esend[h] = part.astype(BF)
            ecopy(h).start()

        @pl.when(j == 1)
        def _():
            ecopy(0).wait_recv()
            ysend[...] = (part + erecv[0].astype(F32)).astype(BF)
            ycopy().start()

        @pl.when(j == 3)
        def _():
            ecopy(1).wait_recv()
            emb_ref[...] = part + erecv[1].astype(F32)

    @pl.when(s == 7)
    def _():
        ycopy().wait_recv()
        emb_ref[...] = emb_ref[...] + yrecv[...].astype(F32)
        for h in range(2):
            mcopy(h).wait_send()
            ecopy(h).wait_send()
        ycopy().wait_send()
        for r in range(nb):
            scopy(r).wait_send()


def front_step(slide_len, kl_step, library, mask, counts_t, og_t, emb_t, dec_t, ncell, lat):
    width, rows = counts_t.shape
    model = emb_t.shape[1]
    mine = rows // 4
    nb = bits_of(ncell)
    nslide = slide_len.shape[0]
    top = -(-nslide // 8) * 8
    anyv = pl.BlockSpec(memory_space=pl.ANY)
    smem = pl.BlockSpec(memory_space=pltpu.SMEM)
    fixed = lambda *shape: pl.BlockSpec(shape, lambda s: (0,) * len(shape))
    vm = pltpu.VMEM
    return pl.pallas_call(
        functools.partial(front_kernel, (ncell, nslide, lat)),
        grid=(8,),
        out_shape=[
            jax.ShapeDtypeStruct((mine, model), F32),
            jax.ShapeDtypeStruct((mine, model), F32),
            jax.ShapeDtypeStruct((mine, model), BF),
            jax.ShapeDtypeStruct((1, rows), F32),
            jax.ShapeDtypeStruct((8, lat), F32),
            jax.ShapeDtypeStruct((mine, 128), F32),
        ],
        in_specs=[smem, smem, fixed(1, rows), fixed(1, rows), anyv, anyv, anyv, anyv],
        out_specs=[
            fixed(mine, model),
            fixed(mine, model),
            fixed(mine, model),
            fixed(1, rows),
            fixed(8, lat),
            fixed(mine, 128),
        ],
        scratch_shapes=[vm((4, width, mine), BF)] * 2
        + [vm((width, model), BF)] * 2
        + [vm((width, mine), BF)]
        + [vm((2, mine, model), BF)] * 4
        + [vm((mine, model), BF)] * 2
        + [
            vm((2 * nb, 2 * top, 128), F32),
            vm((2 * top, 128), F32),
            pltpu.SemaphoreType.DMA((10,)),
            pltpu.SemaphoreType.DMA((5 + nb,)),
            pltpu.SemaphoreType.DMA((5 + nb,)),
        ],
        compiler_params=pltpu.CompilerParams(
            collective_id=1, has_side_effects=True, vmem_limit_bytes=67043328
        ),
        name="front_step",
    )(slide_len, kl_step, library, mask, counts_t, og_t, emb_t, dec_t)


def main_kernel(cfg, *refs):
    ncell, nch, ch, inplace = cfg
    nb = bits_of(ncell)
    take = iter(refs)

    def some(count):
        return [next(take) for _ in range(count)]

    og_ref, ct_ref, dw_ref, ew_ref, scale_ref = some(5)
    emb_hbm, mgk_hbm, mgs_hbm, noise_hbm, latw_hbm, upw_hbm = some(6)
    rowd_ref, const_ref, gain_ref, bias_ref, latb_ref, pmean_ref, plogv_ref = some(7)
    decoded_ref, cgrad_ref, dsum_ref, esum_ref, small_ref, vec_ref = some(6)
    xm, xe, px, keep = some(4)
    recvs = some(nb)
    sends = {k: next(take) for k in range(nb) if k not in inplace}
    normal, mgk, mg, noise, latw, upw, hlow, lmean, lvar, sample, lgrad, resp_s, inv_s, kpart = some(14)
    klbuf, vecbuf, sm_keep, sm_s1, sm_r1, sm_s2, sm_r2 = some(7)
    sm_sc, sm_rc = some(nb), some(nb)
    fin = next(take)
    lsem, ssem, rsem, asend, arecv = some(5)

    rows, model = xm.shape
    mine = rows // 4
    lat = model // 2
    step = model // ncell
    half = model // 2
    at = lax.axis_index("cells")
    gene = lax.axis_index("genes")
    core, wye = bit_of(gene, 0), bit_of(gene, 1)
    home = core * 2 + wye
    peers = [{"cells": xor_of(at, nb, 1 << k)} for k in range(nb)]
    gpeers = [{"genes": xor_of(gene, 2, 1)}, {"genes": xor_of(gene, 2, 2)}]
    allpeers = peers + gpeers
    nall = nb + 2
    s = pl.program_id(0)
    slots = keep.shape[0]

    def remote(src, dst, ssem_at, rsem_at, peer):
        return pltpu.make_async_remote_copy(
            src_ref=src,
            dst_ref=dst,
            send_sem=ssem_at,
            recv_sem=rsem_at,
            device_id=peer,
            device_id_type=MESH,
        )

    def source(i, k):
        h = model >> (k + 1)
        if k in inplace:
            return recvs[k - 1].at[i, :, pl.ds(h, h)]
        return sends[k].at[lax.rem(i, sends[k].shape[0])]

    def copy(i, k):
        return remote(source(i, k), recvs[k].at[i], ssem.at[k, i], rsem.at[k, i], peers[k])

    def free(i, k):
        ring = sends[k].shape[0]

        @pl.when(i >= ring)
        def _():
            copy(i - ring, k).wait_send()

    side = {}

    def add_side(name, src, dst, peer):
        side[name] = (len(side), src, dst, peer)

    def rowblock(ref, b):
        return ref.at[pl.ds(pl.multiple_of(b * mine, mine), mine)]

    for name, ref in (("m", xm), ("e", xe)):
        add_side(name + "core", rowblock(ref, home), rowblock(ref, home), gpeers[0])
        add_side(name + "wye", rowblock(ref, home), rowblock(ref, home), gpeers[1])
        other = core * 2 + (1 - wye)
        add_side(name + "pass", rowblock(ref, other), rowblock(ref, other), gpeers[0])
    add_side("g", mgs_hbm, rowblock(xe, core * 2 + (1 - wye)), gpeers[1])
    for r in range(nall):
        add_side(f"k{r}", klbuf.at[r], klbuf.at[nall + r], allpeers[r])
        add_side(f"v{r}", vecbuf.at[r], vecbuf.at[nall + r], allpeers[r])
    add_side("s1", sm_s1, sm_r1, gpeers[0])
    add_side("s2", sm_s2, sm_r2, gpeers[1])
    for k in range(nb):
        add_side(f"c{k}", sm_sc[k], sm_rc[k], peers[k])
    add_side("f0", fin.at[home], fin.at[home], gpeers[1])
    add_side("f1", fin.at[pl.ds(core * 2, 2)], fin.at[pl.ds(core * 2, 2)], gpeers[0])

    def side_copy(name):
        at_sem, src, dst, peer = side[name]
        return remote(src, dst, asend.at[at_sem], arecv.at[at_sem], peer)

    def start(name):
        side_copy(name).start()

    def got(name):
        side_copy(name).wait_recv()

    def permute(x, sem_at):
        if step % 128 == 0:
            cps = []
            for i in range(ncell):
                block = xor_of(at, nb, reversed_bits(i, nb))
                cps.append(
                    pltpu.make_async_copy(
                        x.at[:, pl.ds(pl.multiple_of(block * step, step), step)],
                        px.at[:, pl.ds(i * step, step)],
                        lsem.at[sem_at + i],
                    )
                )
            for cp in cps:
                cp.start()
            for cp in cps:
                cp.wait()
        else:
            row = lax.broadcasted_iota(jnp.int32, (model, 128), 0)

            def part(j, _):
                col = lax.broadcasted_iota(jnp.int32, (model, 128), 1) + j * 128
                block = col // step
                target = col % step
                for k in range(nb):
                    flag = (block // (1 << (nb - 1 - k))) % 2
                    own = bit_of(at, k)
                    target = target + (flag + own - 2 * flag * own) * ((1 << k) * step)
                pick = (row == target).astype(F32).astype(BF)
                px[:, pl.ds(pl.multiple_of(j * 128, 128), 128)] = jnp.dot(
                    x[...], pick, preferred_element_type=F32
                ).astype(BF)
                return 0

            lax.fori_loop(0, model // 128, part, 0)

    def tables():
        prec = jnp.exp(-plogv_ref[...])
        mprec = pmean_ref[...] * prec
        return prec, mprec, pmean_ref[...] * mprec + plogv_ref[...]

    def loads():
        pairs = (
            (emb_hbm, normal),
            (latw_hbm, latw),
            (upw_hbm, upw),
            (rowblock(noise_hbm, home), noise),
            (mgk_hbm, mgk),
        )
        return [pltpu.make_async_copy(a, b, lsem.at[i]) for i, (a, b) in enumerate(pairs)]

    @pl.when(s == 0)
    def _():
        for cp in loads():
            cp.start()
        barrier = pltpu.get_barrier_semaphore()
        for p in allpeers:
            pl.semaphore_signal(barrier, inc=1, device_id=p, device_id_type=MESH)
        for cp in loads():
            cp.wait()
        e = normal[...]
        centred = e - jnp.mean(e, -1, keepdims=True)
        inv = lax.rsqrt(jnp.mean(centred * centred, -1, keepdims=True) + EPS)
        nrm = centred * inv
        normal[...] = nrm
        inv_s[...] = inv
        hidden = nrm * gain_ref[...] + bias_ref[...]
        hlow[...] = hidden.astype(BF)
        latent = bdot(hlow[...], latw[...], NN) + latb_ref[...]
        lm, lv = latent[:, :lat], latent[:, lat:]
        lmean[...] = lm
        lvar[...] = lv
        sample[...] = (lm + jnp.exp(0.5 * lv) * noise[...].astype(F32)).astype(BF)
        mixed = normal[...] * gain_ref[...] + bias_ref[...] + bdot(sample[...], upw[...], NT)
        xm[pl.ds(pl.multiple_of(home * mine, mine), mine), :] = mixed.astype(BF)
        pl.semaphore_wait(barrier, nall)
        start("mwye")
        start("mcore")
        start("g")
        prec, mprec, ctab = tables()
        lm, lv = lmean[...], lvar[...]
        csum = fdot(jnp.ones((8, lat), F32), ctab, NT)[0:1]
        logits = -0.5 * (fdot(lm * lm, prec, NT) - 2.0 * fdot(lm, mprec, NT) + csum)
        logits = logits * lat ** (-0.5)
        top = jnp.exp(logits - jnp.max(logits, -1, keepdims=True))
        resp = top / jnp.sum(top, -1, keepdims=True)
        resp_s[...] = resp
        moment = jnp.exp(lv) + lm * lm
        diverge = 0.5 * (
            fdot(resp, ctab, NN)
            - lv
            + moment * fdot(resp, prec, NN)
            - 2.0 * lm * fdot(resp, mprec, NN)
            - 1.0
        )
        klbuf[0] = jnp.sum(diverge * rowd_ref[:, 0:1], 0, keepdims=True)
        start("k0")
        got("mwye")
        start("mpass")
        got("mcore")
        got("mpass")
        permute(xm, 0)

    def out_parts(i, g):
        free(i, 0)
        sends[0][lax.rem(i, sends[0].shape[0])] = jnp.dot(
            g, px[:, half:], preferred_element_type=F32
        ).astype(BF)
        copy(i, 0).start()
        keep[lax.rem(i, slots)] = jnp.dot(g, px[:, :half], preferred_element_type=F32)

    @pl.when(s < nch)
    def _():
        out_parts(s, og_ref[...])
        decoded_ref[...] = bdot(dw_ref[...], xm[...], NT).astype(BF)

    @pl.when((s >= nch) & (s < 2 * nch))
    def _():
        scale = scale_ref[...]
        z = 1.0 + ct_ref[...].astype(F32) * scale
        out_parts(s, jnp.log(z).astype(BF))
        grad = bdot(ew_ref[...], xe[...], NT)
        z = 1.0 + ct_ref[...].astype(F32) * scale
        cgrad_ref[...] = (grad * scale / z).astype(BF)

    for k in range(1, nb + 1):
        i = s - AHEAD - (k - 1)

        @pl.when((i >= 0) & (i < 2 * nch))
        def _(i=i, k=k):
            copy(i, k - 1).wait_recv()
            slot = lax.rem(i, slots)
            if k < nb:
                h = model >> (k + 1)
                lo, hi = h, 2 * h
            else:
                lo, hi = 0, step
            v = keep[slot, :, lo:hi]
            for j in range(k):
                v = v + recvs[j][i, :, lo:hi].astype(F32)
            if k < nb:
                if k in inplace:
                    recvs[k - 1][i, :, lo:hi] = v.astype(BF)
                else:
                    free(i, k)
                    sends[k][lax.rem(i, sends[k].shape[0])] = v.astype(BF)
                copy(i, k).start()
            else:

                @pl.when(i < nch)
                def _():
                    dsum_ref[...] = v

                @pl.when(i >= nch)
                def _():
                    esum_ref[...] = v

    plan = {}

    def at_step(step_no):
        def put(fn):
            plan.setdefault(step_no, []).append(fn)
            return fn

        return put

    per = -(-nall // 4)
    for r in range(nall):

        @at_step(1 + r // per)
        def _(r=r):
            got(f"k{r}")
            v = klbuf[r] + klbuf[nall + r]
            if r + 1 < nall:
                klbuf[r + 1] = v
                start(f"k{r + 1}")
            else:
                kpart[...] = v

    back = 2 + (nall - 1) // per

    @at_step(back)
    def _():
        prec, mprec, ctab = tables()
        lm, lv = lmean[...], lvar[...]
        average = kpart[...] / const_ref[0:1]
        loss = const_ref[1:2] * jnp.sum(jnp.maximum(average, FREE), -1, keepdims=True)
        active = (average > FREE).astype(F32)
        weight = rowd_ref[:, 1:2] * active
        resp = resp_s[...]
        rprec = fdot(resp, prec, NN)
        rmean = fdot(resp, mprec, NN)
        variance = jnp.exp(lv)
        moment = variance + lm * lm
        wmom, wmean = weight * moment, weight * lm
        rgrad = 0.5 * (
            fdot(weight, ctab, NT) + fdot(wmom, prec, NT) - 2.0 * fdot(wmean, mprec, NT)
        )
        logit = resp * (rgrad - jnp.sum(resp * rgrad, -1, keepdims=True)) * lat ** (-0.5)
        got("g")
        own = xe[pl.ds(pl.multiple_of(home * mine, mine), mine), :].astype(F32)
        mg[...] = (mgk[...] + own).astype(BF)
        sgrad = bdot(mg[...], upw[...], NN)
        mgrad = (
            sgrad
            + weight * (lm * rprec - rmean)
            - lm * fdot(logit, prec, NN)
            + fdot(logit, mprec, NN)
        )
        vgrad = sgrad * 0.5 * jnp.exp(0.5 * lv) * noise[...].astype(F32) + 0.5 * weight * (
            variance * rprec - 1.0
        )
        lgrad[:, :lat] = mgrad.astype(BF)
        lgrad[:, lat:] = vgrad.astype(BF)
        lcol = fdot(logit, jnp.ones((mine, 128), F32), TN)[:, 0:1]
        cg = 0.5 * fdot(resp, weight, TN) - 0.5 * lcol
        mpg = fdot(logit, lm, TN) - fdot(resp, wmean, TN)
        pmean = pmean_ref[...]
        pg = (
            0.5 * fdot(resp, wmom, TN)
            - 0.5 * fdot(logit, lm * lm, TN)
            + pmean * pmean * cg
            + pmean * mpg
        )
        nk = pmean.shape[0]
        vecbuf[0, 0:nk] = 2.0 * pmean * prec * cg + prec * mpg
        vecbuf[0, nk : 2 * nk] = cg - prec * pg
        base = 2 * nk
        vecbuf[0, base : base + 1] = loss * jnp.ones((1, lat), F32)
        lg = lgrad[...]
        lb = jnp.sum(lg.astype(F32), 0, keepdims=True)
        hgrad = mg[...].astype(F32) + bdot(lg, latw[...], NT)
        nrm = normal[...]
        gg = jnp.sum(hgrad * nrm, 0, keepdims=True)
        sg = jnp.sum(hgrad, 0, keepdims=True)
        for j, row in enumerate((gg, sg, lb)):
            for part in range(2):
                r = base + 1 + 2 * j + part
                vecbuf[0, r : r + 1] = row[:, part * lat : (part + 1) * lat]
        vecbuf[0, base + 7 : base + 8] = jnp.zeros((1, lat), F32)
        ng = hgrad * gain_ref[...]
        eg = inv_s[...] * (
            ng - jnp.mean(ng, -1, keepdims=True) - nrm * jnp.mean(ng * nrm, -1, keepdims=True)
        )
        xe[pl.ds(pl.multiple_of(home * mine, mine), mine), :] = eg.astype(BF)
        start("ewye")
        start("ecore")
        start("v0")

    @at_step(back + 1)
    def _():
        quarter = 3 * lat // 4

        def put(q, lo, hi, left, right):
            v = bdot(left, right, TN)

            @pl.when(core == q // 2)
            def _():
                sm_keep[q % 2, :, lo:hi] = v

            @pl.when(core != q // 2)
            def _():
                sm_s1[q % 2, :, lo:hi] = v.astype(BF)

        cut = 2 * lat - 2 * quarter
        put(0, 0, quarter, hlow[...], lgrad[:, :quarter])
        put(1, 0, quarter, hlow[...], lgrad[:, quarter : 2 * quarter])
        put(2, 0, cut, hlow[...], lgrad[:, 2 * quarter :])
        put(2, cut, quarter, mg[...], sample[:, : quarter - cut])
        put(3, 0, quarter, mg[...], sample[:, quarter - cut :])
        start("s1")

    @at_step(back + 2)
    def _():
        got("ewye")
        start("epass")

    @at_step(nch - 1)
    def _():
        got("ecore")
        got("epass")
        permute(xe, ncell)

    assert back + 2 < nch - 1
    for r in range(nall):

        @at_step(back + 4 + r)
        def _(r=r):
            got(f"v{r}")
            v = vecbuf[r] + vecbuf[nall + r]
            if r + 1 < nall:
                vecbuf[r + 1] = v
                start(f"v{r + 1}")
            else:
                vec_ref[...] = v

    @at_step(back + 2)
    def _():
        got("s1")
        sm_keep[wye] = sm_keep[wye] + sm_r1[wye].astype(F32)
        sm_s2[...] = (sm_keep[1 - wye] + sm_r1[1 - wye].astype(F32)).astype(BF)
        start("s2")

    def span(k):
        base = 0
        for j in reversed(range(k + 1, nb)):
            base = base + bit_of(at, j) * (step << j)
        bit = bit_of(at, k)
        size = step << k
        return (
            pl.ds(pl.multiple_of(base + bit * size, step), size),
            pl.ds(pl.multiple_of(base + (1 - bit) * size, step), size),
        )

    @at_step(back + 5)
    def _():
        got("s2")
        sm_keep[wye] = sm_keep[wye] + sm_r2[...].astype(F32)
        sm_sc[nb - 1][...] = sm_keep[wye, span(nb - 1)[1], :].astype(BF)
        start(f"c{nb - 1}")

    for k in reversed(range(nb)):

        @at_step(back + 5 + 2 * (nb - k) + (0 if k else 2))
        def _(k=k):
            got(f"c{k}")
            kept = span(k)[0]
            sm_keep[wye, kept, :] = sm_keep[wye, kept, :] + sm_rc[k][...].astype(F32)
            if k:
                sm_sc[k - 1][...] = sm_keep[wye, span(k - 1)[1], :].astype(BF)
                start(f"c{k - 1}")
            else:
                fin[home] = sm_keep[wye, kept, :].astype(BF)
                start("f0")

    @at_step(back + 8 + 2 * nb)
    def _():
        got("f0")
        start("f1")

    @at_step(back + 9 + 2 * nb)
    def _():
        got("f1")
        small_ref[...] = fin[...].astype(F32)


    for step_no in sorted(plan):

        @pl.when(s == step_no)
        def _(fns=plan[step_no]):
            for fn in fns:
                fn()

    @pl.when(s == pl.num_programs(0) - 1)
    def _():
        def body(i, _):
            for k in range(nb):
                if k in inplace:
                    copy(i, k).wait_send()
                else:

                    @pl.when(i >= 2 * nch - sends[k].shape[0])
                    def _(k=k):
                        copy(i, k).wait_send()

            return 0

        lax.fori_loop(0, 2 * nch, body, 0)
        for name in side:
            side_copy(name).wait_send()


def main_step(
    embedded, mg_kept, mg_sent, noise, lat_w, up_w, rowd, const, gain, bias, lat_b, pmean_t, plogv_t,
    og_t, counts_t, dec_t, emb_t, scale, ncell
):
    width, rows = og_t.shape
    mine, model = embedded.shape
    lat = up_w.shape[1]
    nb = bits_of(ncell)
    nall = nb + 2
    step = model // ncell
    ch = 384 if step % 128 == 0 else 192
    nch = -(-width // ch)
    inplace = tuple(k for k in range(1, nb) if (model >> (k + 1)) % 128 == 0)
    n = 2 * nch
    last = nch - 1
    first = lambda s: (jnp.minimum(s, last), 0)
    second = lambda s: (jnp.clip(s - nch, 0, last), 0)
    fixed = lambda *shape: pl.BlockSpec(shape, lambda s: (0,) * len(shape))
    lag = AHEAD + nb - 1
    ring = AHEAD + 2
    quarter = 3 * lat // 4
    nk = pmean_t.shape[0]
    vec = 2 * nk + 8
    anyv = pl.BlockSpec(memory_space=pl.ANY)
    nside = 7 + 2 * nall + 2 + nb + 2
    vm = pltpu.VMEM
    return pl.pallas_call(
        functools.partial(main_kernel, (ncell, nch, ch, inplace)),
        grid=(n + lag,),
        out_shape=[
            jax.ShapeDtypeStruct((width, rows), BF),
            jax.ShapeDtypeStruct((width, rows), BF),
            jax.ShapeDtypeStruct((width, step), F32),
            jax.ShapeDtypeStruct((width, step), F32),
            jax.ShapeDtypeStruct((4, step, quarter), F32),
            jax.ShapeDtypeStruct((vec, lat), F32),
        ],
        in_specs=[
            pl.BlockSpec((ch, rows), first),
            pl.BlockSpec((ch, rows), second),
            pl.BlockSpec((ch, model), first),
            pl.BlockSpec((ch, model), second),
            fixed(1, rows),
            anyv,
            anyv,
            anyv,
            anyv,
            anyv,
            anyv,
            fixed(mine, 128),
            fixed(8, lat),
            fixed(1, model),
            fixed(1, model),
            fixed(1, model),
            fixed(nk, lat),
            fixed(nk, lat),
        ],
        out_specs=[
            pl.BlockSpec((ch, rows), first),
            pl.BlockSpec((ch, rows), second),
            pl.BlockSpec((ch, step), lambda s: (jnp.clip(s - lag, 0, last), 0)),
            pl.BlockSpec((ch, step), lambda s: (jnp.clip(s - lag - nch, 0, last), 0)),
            fixed(4, step, quarter),
            fixed(vec, lat),
        ],
        scratch_shapes=[vm((rows, model), BF)] * 3
        + [vm((lag + 1, ch, model // 2), F32)]
        + [vm((n, ch, model >> (k + 1)), BF) for k in range(nb)]
        + [vm((ring, ch, model >> (k + 1)), BF) for k in range(nb) if k not in inplace]
        + [
            vm((mine, model), F32),
            vm((mine, model), F32),
            vm((mine, model), BF),
            vm((mine, lat), BF),
            vm((model, 2 * lat), BF),
            vm((model, lat), BF),
            vm((mine, model), BF),
            vm((mine, lat), F32),
            vm((mine, lat), F32),
            vm((mine, lat), BF),
            vm((mine, 2 * lat), BF),
            vm((mine, nk), F32),
            vm((mine, 1), F32),
            vm((1, lat), F32),
            vm((2 * nall, 1, lat), F32),
            vm((2 * nall, vec, lat), F32),
            vm((2, model, quarter), F32),
            vm((2, model, quarter), BF),
            vm((2, model, quarter), BF),
            vm((model, quarter), BF),
            vm((model, quarter), BF),
        ]
        + [vm((step << k, quarter), BF) for k in range(nb)] * 2
        + [
            vm((4, step, quarter), BF),
            pltpu.SemaphoreType.DMA((max(5, 2 * ncell),)),
            pltpu.SemaphoreType.DMA((nb, n)),
            pltpu.SemaphoreType.DMA((nb, n)),
            pltpu.SemaphoreType.DMA((nside,)),
            pltpu.SemaphoreType.DMA((nside,)),
        ],
        compiler_params=pltpu.CompilerParams(
            collective_id=0, has_side_effects=True, vmem_limit_bytes=67043328
        ),
        name="main_step",
    )(
        og_t, counts_t, dec_t, emb_t, scale, embedded, mg_kept, mg_sent, noise, lat_w, up_w,
        rowd, const, gain, bias, lat_b, pmean_t, plogv_t,
    )


def on_device(
    counts,
    library,
    cell_mask,
    slide_len,
    kl_step,
    noise,
    emb_weight,
    ln_gain,
    ln_bias,
    lat_weight,
    lat_bias,
    up_weight,
    dec_weight,
    prior_mean,
    prior_logvar,
    out_grad,
    ncell,
    ngene,
):
    rows, width = counts.shape
    model = emb_weight.shape[0]
    latent_w = up_weight.shape[1]
    cell_at = lax.axis_index("cells")
    og_t, counts_t, dec_t, emb_t = out_grad.T, counts.T, dec_weight.T, emb_weight.T
    embedded, mg_kept, mg_sent, scale, const, rowd = front_step(
        slide_len, kl_step, library[None, :], cell_mask[None, :], counts_t, og_t, emb_t, dec_t,
        ncell, latent_w,
    )
    decoded, counts_grad, dec_out, emb_out, small, vec = main_step(
        embedded, mg_kept, mg_sent, noise, lat_weight, up_weight, rowd, const,
        ln_gain[None, :], ln_bias[None, :], lat_bias[None, :], prior_mean.T, prior_logvar.T,
        og_t, counts_t, dec_t, emb_t, scale, ncell,
    )
    decoded, counts_grad, dec_out, emb_out = decoded.T, counts_grad.T, dec_out.T, emb_out.T
    step = model // ncell
    small = small.transpose(1, 0, 2).reshape(step, 3 * latent_w)
    latw_out = small[:, : 2 * latent_w]
    up_out = small[:, 2 * latent_w :]
    nk = prior_mean.shape[1]

    def own(x, each, axis):
        return lax.dynamic_slice_in_dim(x, cell_at * each, each, axis)

    pmean_out = own(vec[:nk], latent_w // ncell, 1).T
    plogv_out = own(vec[nk : 2 * nk], latent_w // ncell, 1).T
    base = 2 * nk
    kl_loss = vec[base, :1] / (ncell * ngene)
    gain_out, shift_out, latb_out = [
        own(vec[base + 1 + 2 * j : base + 3 + 2 * j].reshape(model), step, 0) for j in range(3)
    ]
    return (
        decoded,
        counts_grad,
        emb_out,
        gain_out,
        shift_out,
        latw_out,
        latb_out,
        up_out,
        dec_out,
        pmean_out,
        plogv_out,
        kl_loss,
    )


def solution(mesh):
    ncell, ngene = mesh.shape["cells"], mesh.shape["genes"]

    def body(*args):
        return on_device(*args, ncell=ncell, ngene=ngene)

    return jax.shard_map(
        body,
        mesh=mesh,
        in_specs=(
            P("cells", "genes"),
            P("cells"),
            P("cells"),
            P(),
            P(),
            P("cells", None),
            P(None, "genes"),
            P(),
            P(),
            P(),
            P(),
            P(),
            P(None, "genes"),
            P(),
            P(),
            P("cells", "genes"),
        ),
        out_specs=(
            P("cells", "genes"),
            P("cells", "genes"),
            P("cells", "genes"),
            P("cells"),
            P("cells"),
            P("cells", None),
            P("cells"),
            P("cells", None),
            P("cells", "genes"),
            P("cells", None),
            P("cells", None),
            P(),
        ),
        check_vma=False,
    )
```

```python
import functools

import jax
import jax.numpy as jnp
from jax import lax
from jax.experimental import pallas as pl
from jax.experimental.pallas import tpu as pltpu
from jax.sharding import PartitionSpec as P

WARM = 1000
EPS = 1e-05
FREE = 1.0
BF = jnp.bfloat16
F32 = jnp.float32


MESH = pl.DeviceIdType.MESH


def bits_of(n):
    return n.bit_length() - 1


def bit_of(at, k):
    return lax.rem(lax.div(at, 1 << k), 2)


def xor_of(at, nbits, value):
    out = 0
    for k in range(nbits):
        bit = bit_of(at, k)
        out = out + (1 - bit if (value >> k) & 1 else bit) * (1 << k)
    return out


def reversed_bits(i, n):
    out = 0
    for k in range(n):
        out = out * 2 + ((i >> k) & 1)
    return out


def fdot(left, right, dims):
    return lax.dot_general(
        left, right, (dims, ((), ())), precision=lax.Precision.HIGHEST, preferred_element_type=F32
    )


def bdot(left, right, dims):
    return lax.dot_general(left, right, (dims, ((), ())), preferred_element_type=F32)


NN, NT, TN = ((1,), (0,)), ((1,), (1,)), ((0,), (0,))
AHEAD = 3


def front_kernel(cfg, *refs):
    ncell, nslide, lat = cfg
    nb = bits_of(ncell)
    slen_ref, kls_ref, lib_ref, mask_ref, ct_hbm, og_hbm, et_hbm, dt_hbm = refs[:8]
    emb_ref, mgk_ref, mgs_ref, scale_ref, const_ref, rowd_ref = refs[8:14]
    ct, og, et, dt, low, msend, mrecv, esend, erecv, ysend, yrecv, stb, stv = refs[14:27]
    lsem, asend, arecv = refs[27:]
    rows = lib_ref.shape[1]
    mine = rows // 4
    top = stv.shape[0] // 2
    at = lax.axis_index("cells")
    gene = lax.axis_index("genes")
    core, wye = bit_of(gene, 0), bit_of(gene, 1)
    home = core * 2 + wye
    peers = [{"cells": xor_of(at, nb, 1 << k)} for k in range(nb)]
    gpeers = [{"genes": xor_of(gene, 2, 1)}, {"genes": xor_of(gene, 2, 2)}]
    s = pl.program_id(0)

    def block_of(j):
        far, away = 1 - lax.rem(j, 2), 1 - lax.div(j, 2)
        side = far * (1 - core) + (1 - far) * core
        return side * 2 + away * (1 - wye) + (1 - away) * wye

    def cols(j):
        return pl.ds(pl.multiple_of(block_of(j) * mine, mine), mine)

    def load(which, h, f):
        src, dst = ((og_hbm, og), (ct_hbm, ct))[which]
        j = 2 * h + f
        return pltpu.make_async_copy(
            src.at[:, cols(j)],
            dst.at[h, :, pl.ds(f * mine, mine)],
            lsem.at[2 + 4 * which + j],
        )

    def whole(which):
        src, dst = ((dt_hbm, dt), (et_hbm, et))[which]
        return pltpu.make_async_copy(src, dst, lsem.at[which])

    def remote(src, dst, sem, peer):
        return pltpu.make_async_remote_copy(
            src_ref=src,
            dst_ref=dst,
            send_sem=asend.at[sem],
            recv_sem=arecv.at[sem],
            device_id=peer,
            device_id_type=MESH,
        )

    def mcopy(h):
        return remote(msend.at[h], mrecv.at[h], h, gpeers[0])

    def ecopy(h):
        return remote(esend.at[h], erecv.at[h], 2 + h, gpeers[0])

    def ycopy():
        return remote(ysend, yrecv, 4, gpeers[1])

    def scopy(r):
        return remote(stb.at[r], stb.at[nb + r], 5 + r, peers[r])

    def slides():
        place = at * rows + lax.broadcasted_iota(jnp.int32, (1, rows), 1)
        begin = 0
        for q in range(nslide):
            end = begin + slen_ref[q]
            yield q, ((place >= begin) & (place < end)).astype(F32)
            begin = end

    def round_done(r):
        scopy(r).wait_recv()
        v = stb[r] + stb[nb + r]
        if r + 1 < nb:
            stb[r + 1] = v
            scopy(r + 1).start()
        else:
            stv[...] = v

    @pl.when(s == 0)
    def _():
        barrier = pltpu.get_barrier_semaphore()
        for p in peers + gpeers:
            pl.semaphore_signal(barrier, inc=1, device_id=p, device_id_type=MESH)
        whole(0).start()
        for which, h in ((0, 0), (1, 0), (1, 1), (0, 1)):
            for f in range(2):
                load(which, h, f).start()
            if (which, h) == (0, 0):
                whole(1).start()
        stb[0] = jnp.zeros_like(stv)
        live = mask_ref[...].astype(F32)
        libsize = lib_ref[...].astype(F32)
        for q, row in slides():
            stb[0, q : q + 1] = jnp.sum(row * (libsize * live), 1, keepdims=True) * jnp.ones(
                (1, 128), F32
            )
            stb[0, top + q : top + q + 1] = jnp.sum(
                row * live, 1, keepdims=True
            ) * jnp.ones((1, 128), F32)
        pl.semaphore_wait(barrier, nb + 2)
        scopy(0).start()
        whole(0).wait()
        round_done(0)

    @pl.when(s == 1)
    def _():
        for r in range(1, nb):
            round_done(r)
        whole(1).wait()
        live = mask_ref[...].astype(F32)
        total = jnp.zeros((1, 1), F32)
        scale = jnp.zeros((1, rows), F32)
        for q, row in slides():
            count = stv[top + q : top + q + 1, 0:1]
            scale = scale + row * (stv[q : q + 1, 0:1] / jnp.maximum(count, 1.0))
            total = total + count
        scale_ref[...] = scale / lib_ref[...].astype(F32)
        total = jnp.maximum(total, 1.0)
        beta = jnp.minimum(1.0, kls_ref[0].astype(F32) / WARM)
        line = lax.broadcasted_iota(jnp.int32, (8, lat), 0)
        const_ref[...] = jnp.where(line == 0, total, beta)
        own = mask_ref[:, pl.ds(pl.multiple_of(home * mine, mine), mine)].astype(F32)
        line = lax.broadcasted_iota(jnp.int32, (8, mine), 0)
        both = jnp.where(line == 0, own, jnp.where(line == 1, beta * own / total, 0.0))
        eye = (
            lax.broadcasted_iota(jnp.int32, (8, 128), 0)
            == lax.broadcasted_iota(jnp.int32, (8, 128), 1)
        ).astype(F32)
        rowd_ref[...] = fdot(both, eye, TN)

    def pair(h, left, right, kept, send, copy):
        part = bdot(left, right, TN)
        send[h] = part[:mine].astype(BF)
        copy(h).start()
        kept[...] = part[mine:]

    @pl.when((s == 0) | (s == 3))
    def _():
        h = lax.div(s, 3)
        for f in range(2):
            load(0, h, f).wait()
        pair(h, og[h], dt[...], mgk_ref, msend, mcopy)

    @pl.when((s == 1) | (s == 2))
    def _():
        h = s - 1
        for f in range(2):
            load(1, h, f).wait()
            z = 1.0 + ct[h, :, f * mine : (f + 1) * mine].astype(F32) * scale_ref[
                :, cols(2 * h + f)
            ]
            low[:, f * mine : (f + 1) * mine] = jnp.log(z).astype(BF)
        pair(h, low[...], et[...], emb_ref, esend, ecopy)

    @pl.when(s == 1)
    def _():
        ecopy(0).wait_recv()
        ysend[...] = (emb_ref[...] + erecv[0].astype(F32)).astype(BF)
        ycopy().start()
        mcopy(0).wait_recv()
        mgs_ref[...] = (mgk_ref[...] + mrecv[0].astype(F32)).astype(BF)

    @pl.when(s == 3)
    def _():
        ecopy(1).wait_recv()
        emb_ref[...] = emb_ref[...] + erecv[1].astype(F32)
        mcopy(1).wait_recv()
        mgk_ref[...] = mgk_ref[...] + mrecv[1].astype(F32)

    @pl.when(s == 3)
    def _():
        ycopy().wait_recv()
        emb_ref[...] = emb_ref[...] + yrecv[...].astype(F32)
        for h in range(2):
            mcopy(h).wait_send()
            ecopy(h).wait_send()
        ycopy().wait_send()
        for r in range(nb):
            scopy(r).wait_send()


def front_step(slide_len, kl_step, library, mask, counts_t, og_t, emb_t, dec_t, ncell, lat):
    width, rows = counts_t.shape
    model = emb_t.shape[1]
    mine = rows // 4
    nb = bits_of(ncell)
    nslide = slide_len.shape[0]
    top = -(-nslide // 8) * 8
    anyv = pl.BlockSpec(memory_space=pl.ANY)
    smem = pl.BlockSpec(memory_space=pltpu.SMEM)
    fixed = lambda *shape: pl.BlockSpec(shape, lambda s: (0,) * len(shape))
    vm = pltpu.VMEM
    return pl.pallas_call(
        functools.partial(front_kernel, (ncell, nslide, lat)),
        grid=(4,),
        out_shape=[
            jax.ShapeDtypeStruct((mine, model), F32),
            jax.ShapeDtypeStruct((mine, model), F32),
            jax.ShapeDtypeStruct((mine, model), BF),
            jax.ShapeDtypeStruct((1, rows), F32),
            jax.ShapeDtypeStruct((8, lat), F32),
            jax.ShapeDtypeStruct((mine, 128), F32),
        ],
        in_specs=[smem, smem, fixed(1, rows), fixed(1, rows), anyv, anyv, anyv, anyv],
        out_specs=[
            fixed(mine, model),
            fixed(mine, model),
            fixed(mine, model),
            fixed(1, rows),
            fixed(8, lat),
            fixed(mine, 128),
        ],
        scratch_shapes=[vm((2, width, 2 * mine), BF)] * 2
        + [vm((width, model), BF)] * 2
        + [vm((width, 2 * mine), BF)]
        + [vm((2, mine, model), BF)] * 4
        + [vm((mine, model), BF)] * 2
        + [
            vm((2 * nb, 2 * top, 128), F32),
            vm((2 * top, 128), F32),
            pltpu.SemaphoreType.DMA((10,)),
            pltpu.SemaphoreType.DMA((5 + nb,)),
            pltpu.SemaphoreType.DMA((5 + nb,)),
        ],
        compiler_params=pltpu.CompilerParams(
            collective_id=1, has_side_effects=True, vmem_limit_bytes=67043328
        ),
        name="front_step",
    )(slide_len, kl_step, library, mask, counts_t, og_t, emb_t, dec_t)


def main_kernel(cfg, *refs):
    ncell, nch, ch, inplace = cfg
    nb = bits_of(ncell)
    take = iter(refs)

    def some(count):
        return [next(take) for _ in range(count)]

    og_ref, ct_ref, dw_ref, ew_ref, scale_ref = some(5)
    emb_hbm, mgk_hbm, mgs_hbm, noise_hbm, latw_hbm, upw_hbm = some(6)
    rowd_ref, const_ref, gain_ref, bias_ref, latb_ref, pmean_ref, plogv_ref = some(7)
    decoded_ref, cgrad_ref, dsum_ref, esum_ref, small_ref, vec_ref = some(6)
    xm, xe, px, keep = some(4)
    recvs = some(nb)
    sends = {k: next(take) for k in range(nb) if k not in inplace}
    normal, mgk, mg, noise, latw, upw, hlow, lmean, lvar, sample, lgrad, resp_s, inv_s, kpart = some(14)
    klbuf, vecbuf, sm_keep, sm_s1, sm_r1, sm_s2, sm_r2 = some(7)
    sm_sc, sm_rc = some(nb), some(nb)
    fin = next(take)
    lsem, ssem, rsem, asend, arecv = some(5)

    rows, model = xm.shape
    mine = rows // 4
    lat = model // 2
    step = model // ncell
    half = model // 2
    at = lax.axis_index("cells")
    gene = lax.axis_index("genes")
    core, wye = bit_of(gene, 0), bit_of(gene, 1)
    home = core * 2 + wye
    peers = [{"cells": xor_of(at, nb, 1 << k)} for k in range(nb)]
    gpeers = [{"genes": xor_of(gene, 2, 1)}, {"genes": xor_of(gene, 2, 2)}]
    allpeers = peers + gpeers
    nall = nb + 2
    s = pl.program_id(0)
    slots = keep.shape[0]

    def remote(src, dst, ssem_at, rsem_at, peer):
        return pltpu.make_async_remote_copy(
            src_ref=src,
            dst_ref=dst,
            send_sem=ssem_at,
            recv_sem=rsem_at,
            device_id=peer,
            device_id_type=MESH,
        )

    def source(i, k):
        h = model >> (k + 1)
        if k in inplace:
            return recvs[k - 1].at[i, :, pl.ds(h, h)]
        return sends[k].at[lax.rem(i, sends[k].shape[0])]

    def copy(i, k):
        return remote(source(i, k), recvs[k].at[i], ssem.at[k, i], rsem.at[k, i], peers[k])

    def free(i, k):
        ring = sends[k].shape[0]

        @pl.when(i >= ring)
        def _():
            copy(i - ring, k).wait_send()

    side = {}

    def add_side(name, src, dst, peer):
        side[name] = (len(side), src, dst, peer)

    def rowblock(ref, b):
        return ref.at[pl.ds(pl.multiple_of(b * mine, mine), mine)]

    for name, ref in (("m", xm), ("e", xe)):
        add_side(name + "core", rowblock(ref, home), rowblock(ref, home), gpeers[0])
        add_side(name + "wye", rowblock(ref, home), rowblock(ref, home), gpeers[1])
        other = core * 2 + (1 - wye)
        add_side(name + "pass", rowblock(ref, other), rowblock(ref, other), gpeers[0])
    add_side("g", mgs_hbm, rowblock(xe, core * 2 + (1 - wye)), gpeers[1])
    for r in range(nall):
        add_side(f"k{r}", klbuf.at[r], klbuf.at[nall + r], allpeers[r])
        add_side(f"v{r}", vecbuf.at[r], vecbuf.at[nall + r], allpeers[r])
    add_side("s1", sm_s1, sm_r1, gpeers[0])
    add_side("s2", sm_s2, sm_r2, gpeers[1])
    for k in range(nb):
        add_side(f"c{k}", sm_sc[k], sm_rc[k], peers[k])
    add_side("f0", fin.at[home], fin.at[home], gpeers[1])
    add_side("f1", fin.at[pl.ds(core * 2, 2)], fin.at[pl.ds(core * 2, 2)], gpeers[0])

    def side_copy(name):
        at_sem, src, dst, peer = side[name]
        return remote(src, dst, asend.at[at_sem], arecv.at[at_sem], peer)

    def start(name):
        side_copy(name).start()

    def got(name):
        side_copy(name).wait_recv()

    def permute(x, sem_at):
        if step % 128 == 0:
            cps = []
            for i in range(ncell):
                block = xor_of(at, nb, reversed_bits(i, nb))
                cps.append(
                    pltpu.make_async_copy(
                        x.at[:, pl.ds(pl.multiple_of(block * step, step), step)],
                        px.at[:, pl.ds(i * step, step)],
                        lsem.at[sem_at + i],
                    )
                )
            for cp in cps:
                cp.start()
            for cp in cps:
                cp.wait()
        else:
            row = lax.broadcasted_iota(jnp.int32, (model, 128), 0)

            def part(j, _):
                col = lax.broadcasted_iota(jnp.int32, (model, 128), 1) + j * 128
                block = col // step
                target = col % step
                for k in range(nb):
                    flag = (block // (1 << (nb - 1 - k))) % 2
                    own = bit_of(at, k)
                    target = target + (flag + own - 2 * flag * own) * ((1 << k) * step)
                pick = (row == target).astype(F32).astype(BF)
                px[:, pl.ds(pl.multiple_of(j * 128, 128), 128)] = jnp.dot(
                    x[...], pick, preferred_element_type=F32
                ).astype(BF)
                return 0

            lax.fori_loop(0, model // 128, part, 0)

    def tables():
        prec = jnp.exp(-plogv_ref[...])
        mprec = pmean_ref[...] * prec
        return prec, mprec, pmean_ref[...] * mprec + plogv_ref[...]

    def loads():
        pairs = (
            (emb_hbm, normal),
            (latw_hbm, latw),
            (upw_hbm, upw),
            (rowblock(noise_hbm, home), noise),
            (mgk_hbm, mgk),
        )
        return [pltpu.make_async_copy(a, b, lsem.at[i]) for i, (a, b) in enumerate(pairs)]

    @pl.when(s == 0)
    def _():
        for cp in loads():
            cp.start()
        barrier = pltpu.get_barrier_semaphore()
        for p in allpeers:
            pl.semaphore_signal(barrier, inc=1, device_id=p, device_id_type=MESH)
        for cp in loads():
            cp.wait()
        e = normal[...]
        centred = e - jnp.mean(e, -1, keepdims=True)
        inv = lax.rsqrt(jnp.mean(centred * centred, -1, keepdims=True) + EPS)
        nrm = centred * inv
        normal[...] = nrm
        inv_s[...] = inv
        hidden = nrm * gain_ref[...] + bias_ref[...]
        hlow[...] = hidden.astype(BF)
        latent = bdot(hlow[...], latw[...], NN) + latb_ref[...]
        lm, lv = latent[:, :lat], latent[:, lat:]
        lmean[...] = lm
        lvar[...] = lv
        sample[...] = (lm + jnp.exp(0.5 * lv) * noise[...].astype(F32)).astype(BF)
        mixed = normal[...] * gain_ref[...] + bias_ref[...] + bdot(sample[...], upw[...], NT)
        xm[pl.ds(pl.multiple_of(home * mine, mine), mine), :] = mixed.astype(BF)
        pl.semaphore_wait(barrier, nall)
        start("mwye")
        start("mcore")
        start("g")
        prec, mprec, ctab = tables()
        lm, lv = lmean[...], lvar[...]
        csum = fdot(jnp.ones((8, lat), F32), ctab, NT)[0:1]
        logits = -0.5 * (fdot(lm * lm, prec, NT) - 2.0 * fdot(lm, mprec, NT) + csum)
        logits = logits * lat ** (-0.5)
        top = jnp.exp(logits - jnp.max(logits, -1, keepdims=True))
        resp = top / jnp.sum(top, -1, keepdims=True)
        resp_s[...] = resp
        moment = jnp.exp(lv) + lm * lm
        diverge = 0.5 * (
            fdot(resp, ctab, NN)
            - lv
            + moment * fdot(resp, prec, NN)
            - 2.0 * lm * fdot(resp, mprec, NN)
            - 1.0
        )
        klbuf[0] = jnp.sum(diverge * rowd_ref[:, 0:1], 0, keepdims=True)
        start("k0")
        got("mwye")
        start("mpass")
        got("mcore")
        got("mpass")
        permute(xm, 0)

    def out_parts(i, g):
        free(i, 0)
        sends[0][lax.rem(i, sends[0].shape[0])] = jnp.dot(
            g, px[:, half:], preferred_element_type=F32
        ).astype(BF)
        copy(i, 0).start()
        keep[lax.rem(i, slots)] = jnp.dot(g, px[:, :half], preferred_element_type=F32)

    @pl.when(s < nch)
    def _():
        out_parts(s, og_ref[...])
        decoded_ref[...] = bdot(dw_ref[...], xm[...], NT).astype(BF)

    @pl.when((s >= nch) & (s < 2 * nch))
    def _():
        scale = scale_ref[...]
        z = 1.0 + ct_ref[...].astype(F32) * scale
        out_parts(s, jnp.log(z).astype(BF))
        grad = bdot(ew_ref[...], xe[...], NT)
        z = 1.0 + ct_ref[...].astype(F32) * scale
        cgrad_ref[...] = (grad * scale / z).astype(BF)

    for k in range(1, nb + 1):
        i = s - AHEAD - (k - 1)

        @pl.when((i >= 0) & (i < 2 * nch))
        def _(i=i, k=k):
            copy(i, k - 1).wait_recv()
            slot = lax.rem(i, slots)
            if k < nb:
                h = model >> (k + 1)
                lo, hi = h, 2 * h
            else:
                lo, hi = 0, step
            v = keep[slot, :, lo:hi]
            for j in range(k):
                v = v + recvs[j][i, :, lo:hi].astype(F32)
            if k < nb:
                if k in inplace:
                    recvs[k - 1][i, :, lo:hi] = v.astype(BF)
                else:
                    free(i, k)
                    sends[k][lax.rem(i, sends[k].shape[0])] = v.astype(BF)
                copy(i, k).start()
            else:

                @pl.when(i < nch)
                def _():
                    dsum_ref[...] = v

                @pl.when(i >= nch)
                def _():
                    esum_ref[...] = v

    plan = {}

    def at_step(step_no):
        def put(fn):
            plan.setdefault(step_no, []).append(fn)
            return fn

        return put

    per = -(-nall // 4)
    for r in range(nall):

        @at_step(1 + r // per)
        def _(r=r):
            got(f"k{r}")
            v = klbuf[r] + klbuf[nall + r]
            if r + 1 < nall:
                klbuf[r + 1] = v
                start(f"k{r + 1}")
            else:
                kpart[...] = v

    back = 2 + (nall - 1) // per

    @at_step(back)
    def _():
        prec, mprec, ctab = tables()
        lm, lv = lmean[...], lvar[...]
        average = kpart[...] / const_ref[0:1]
        loss = const_ref[1:2] * jnp.sum(jnp.maximum(average, FREE), -1, keepdims=True)
        active = (average > FREE).astype(F32)
        weight = rowd_ref[:, 1:2] * active
        resp = resp_s[...]
        rprec = fdot(resp, prec, NN)
        rmean = fdot(resp, mprec, NN)
        variance = jnp.exp(lv)
        moment = variance + lm * lm
        wmom, wmean = weight * moment, weight * lm
        rgrad = 0.5 * (
            fdot(weight, ctab, NT) + fdot(wmom, prec, NT) - 2.0 * fdot(wmean, mprec, NT)
        )
        logit = resp * (rgrad - jnp.sum(resp * rgrad, -1, keepdims=True)) * lat ** (-0.5)
        got("g")
        own = xe[pl.ds(pl.multiple_of(home * mine, mine), mine), :].astype(F32)
        mg[...] = (mgk[...] + own).astype(BF)
        sgrad = bdot(mg[...], upw[...], NN)
        mgrad = (
            sgrad
            + weight * (lm * rprec - rmean)
            - lm * fdot(logit, prec, NN)
            + fdot(logit, mprec, NN)
        )
        vgrad = sgrad * 0.5 * jnp.exp(0.5 * lv) * noise[...].astype(F32) + 0.5 * weight * (
            variance * rprec - 1.0
        )
        lgrad[:, :lat] = mgrad.astype(BF)
        lgrad[:, lat:] = vgrad.astype(BF)
        lcol = fdot(logit, jnp.ones((mine, 128), F32), TN)[:, 0:1]
        cg = 0.5 * fdot(resp, weight, TN) - 0.5 * lcol
        mpg = fdot(logit, lm, TN) - fdot(resp, wmean, TN)
        pmean = pmean_ref[...]
        pg = (
            0.5 * fdot(resp, wmom, TN)
            - 0.5 * fdot(logit, lm * lm, TN)
            + pmean * pmean * cg
            + pmean * mpg
        )
        nk = pmean.shape[0]
        vecbuf[0, 0:nk] = 2.0 * pmean * prec * cg + prec * mpg
        vecbuf[0, nk : 2 * nk] = cg - prec * pg
        base = 2 * nk
        vecbuf[0, base : base + 1] = loss * jnp.ones((1, lat), F32)
        lg = lgrad[...]
        lb = jnp.sum(lg.astype(F32), 0, keepdims=True)
        hgrad = mg[...].astype(F32) + bdot(lg, latw[...], NT)
        nrm = normal[...]
        gg = jnp.sum(hgrad * nrm, 0, keepdims=True)
        sg = jnp.sum(hgrad, 0, keepdims=True)
        for j, row in enumerate((gg, sg, lb)):
            for part in range(2):
                r = base + 1 + 2 * j + part
                vecbuf[0, r : r + 1] = row[:, part * lat : (part + 1) * lat]
        vecbuf[0, base + 7 : base + 8] = jnp.zeros((1, lat), F32)
        ng = hgrad * gain_ref[...]
        eg = inv_s[...] * (
            ng - jnp.mean(ng, -1, keepdims=True) - nrm * jnp.mean(ng * nrm, -1, keepdims=True)
        )
        xe[pl.ds(pl.multiple_of(home * mine, mine), mine), :] = eg.astype(BF)
        start("ewye")
        start("ecore")
        start("v0")

    @at_step(back + 1)
    def _():
        quarter = 3 * lat // 4

        def put(q, lo, hi, left, right):
            v = bdot(left, right, TN)

            @pl.when(core == q // 2)
            def _():
                sm_keep[q % 2, :, lo:hi] = v

            @pl.when(core != q // 2)
            def _():
                sm_s1[q % 2, :, lo:hi] = v.astype(BF)

        cut = 2 * lat - 2 * quarter
        put(0, 0, quarter, hlow[...], lgrad[:, :quarter])
        put(1, 0, quarter, hlow[...], lgrad[:, quarter : 2 * quarter])
        put(2, 0, cut, hlow[...], lgrad[:, 2 * quarter :])
        put(2, cut, quarter, mg[...], sample[:, : quarter - cut])
        put(3, 0, quarter, mg[...], sample[:, quarter - cut :])
        start("s1")

    @at_step(back + 2)
    def _():
        got("ewye")
        start("epass")

    @at_step(nch - 1)
    def _():
        got("ecore")
        got("epass")
        permute(xe, ncell)

    assert back + 2 < nch - 1
    for r in range(nall):

        @at_step(back + 4 + r)
        def _(r=r):
            got(f"v{r}")
            v = vecbuf[r] + vecbuf[nall + r]
            if r + 1 < nall:
                vecbuf[r + 1] = v
                start(f"v{r + 1}")
            else:
                vec_ref[...] = v

    @at_step(back + 2)
    def _():
        got("s1")
        sm_keep[wye] = sm_keep[wye] + sm_r1[wye].astype(F32)
        sm_s2[...] = (sm_keep[1 - wye] + sm_r1[1 - wye].astype(F32)).astype(BF)
        start("s2")

    def span(k):
        base = 0
        for j in reversed(range(k + 1, nb)):
            base = base + bit_of(at, j) * (step << j)
        bit = bit_of(at, k)
        size = step << k
        return (
            pl.ds(pl.multiple_of(base + bit * size, step), size),
            pl.ds(pl.multiple_of(base + (1 - bit) * size, step), size),
        )

    @at_step(back + 5)
    def _():
        got("s2")
        sm_keep[wye] = sm_keep[wye] + sm_r2[...].astype(F32)
        sm_sc[nb - 1][...] = sm_keep[wye, span(nb - 1)[1], :].astype(BF)
        start(f"c{nb - 1}")

    for k in reversed(range(nb)):

        @at_step(back + 5 + 2 * (nb - k) + (0 if k else 2))
        def _(k=k):
            got(f"c{k}")
            kept = span(k)[0]
            sm_keep[wye, kept, :] = sm_keep[wye, kept, :] + sm_rc[k][...].astype(F32)
            if k:
                sm_sc[k - 1][...] = sm_keep[wye, span(k - 1)[1], :].astype(BF)
                start(f"c{k - 1}")
            else:
                fin[home] = sm_keep[wye, kept, :].astype(BF)
                start("f0")

    @at_step(back + 8 + 2 * nb)
    def _():
        got("f0")
        start("f1")

    @at_step(back + 9 + 2 * nb)
    def _():
        got("f1")
        small_ref[...] = fin[...].astype(F32)


    for step_no in sorted(plan):

        @pl.when(s == step_no)
        def _(fns=plan[step_no]):
            for fn in fns:
                fn()

    @pl.when(s == pl.num_programs(0) - 1)
    def _():
        def body(i, _):
            for k in range(nb):
                if k in inplace:
                    copy(i, k).wait_send()
                else:

                    @pl.when(i >= 2 * nch - sends[k].shape[0])
                    def _(k=k):
                        copy(i, k).wait_send()

            return 0

        lax.fori_loop(0, 2 * nch, body, 0)
        for name in side:
            side_copy(name).wait_send()


def main_step(
    embedded, mg_kept, mg_sent, noise, lat_w, up_w, rowd, const, gain, bias, lat_b, pmean_t, plogv_t,
    og_t, counts_t, dec_t, emb_t, scale, ncell
):
    width, rows = og_t.shape
    mine, model = embedded.shape
    lat = up_w.shape[1]
    nb = bits_of(ncell)
    nall = nb + 2
    step = model // ncell
    ch = 376 if step % 128 == 0 else 192
    nch = -(-width // ch)
    inplace = tuple(k for k in range(1, nb) if (model >> (k + 1)) % 128 == 0)
    n = 2 * nch
    last = nch - 1
    first = lambda s: (jnp.minimum(s, last), 0)
    second = lambda s: (jnp.clip(s - nch, 0, last), 0)
    fixed = lambda *shape: pl.BlockSpec(shape, lambda s: (0,) * len(shape))
    lag = AHEAD + nb - 1
    ring = AHEAD + 2
    quarter = 3 * lat // 4
    nk = pmean_t.shape[0]
    vec = 2 * nk + 8
    anyv = pl.BlockSpec(memory_space=pl.ANY)
    nside = 7 + 2 * nall + 2 + nb + 2
    vm = pltpu.VMEM
    return pl.pallas_call(
        functools.partial(main_kernel, (ncell, nch, ch, inplace)),
        grid=(n + lag,),
        out_shape=[
            jax.ShapeDtypeStruct((width, rows), BF),
            jax.ShapeDtypeStruct((width, rows), BF),
            jax.ShapeDtypeStruct((width, step), F32),
            jax.ShapeDtypeStruct((width, step), F32),
            jax.ShapeDtypeStruct((4, step, quarter), F32),
            jax.ShapeDtypeStruct((vec, lat), F32),
        ],
        in_specs=[
            pl.BlockSpec((ch, rows), first),
            pl.BlockSpec((ch, rows), second),
            pl.BlockSpec((ch, model), first),
            pl.BlockSpec((ch, model), second),
            fixed(1, rows),
            anyv,
            anyv,
            anyv,
            anyv,
            anyv,
            anyv,
            fixed(mine, 128),
            fixed(8, lat),
            fixed(1, model),
            fixed(1, model),
            fixed(1, model),
            fixed(nk, lat),
            fixed(nk, lat),
        ],
        out_specs=[
            pl.BlockSpec((ch, rows), first),
            pl.BlockSpec((ch, rows), second),
            pl.BlockSpec((ch, step), lambda s: (jnp.clip(s - lag, 0, last), 0)),
            pl.BlockSpec((ch, step), lambda s: (jnp.clip(s - lag - nch, 0, last), 0)),
            fixed(4, step, quarter),
            fixed(vec, lat),
        ],
        scratch_shapes=[vm((rows, model), BF)] * 3
        + [vm((lag + 1, ch, model // 2), F32)]
        + [vm((n, ch, model >> (k + 1)), BF) for k in range(nb)]
        + [vm((ring, ch, model >> (k + 1)), BF) for k in range(nb) if k not in inplace]
        + [
            vm((mine, model), F32),
            vm((mine, model), F32),
            vm((mine, model), BF),
            vm((mine, lat), BF),
            vm((model, 2 * lat), BF),
            vm((model, lat), BF),
            vm((mine, model), BF),
            vm((mine, lat), F32),
            vm((mine, lat), F32),
            vm((mine, lat), BF),
            vm((mine, 2 * lat), BF),
            vm((mine, nk), F32),
            vm((mine, 1), F32),
            vm((1, lat), F32),
            vm((2 * nall, 1, lat), F32),
            vm((2 * nall, vec, lat), F32),
            vm((2, model, quarter), F32),
            vm((2, model, quarter), BF),
            vm((2, model, quarter), BF),
            vm((model, quarter), BF),
            vm((model, quarter), BF),
        ]
        + [vm((step << k, quarter), BF) for k in range(nb)] * 2
        + [
            vm((4, step, quarter), BF),
            pltpu.SemaphoreType.DMA((max(5, 2 * ncell),)),
            pltpu.SemaphoreType.DMA((nb, n)),
            pltpu.SemaphoreType.DMA((nb, n)),
            pltpu.SemaphoreType.DMA((nside,)),
            pltpu.SemaphoreType.DMA((nside,)),
        ],
        compiler_params=pltpu.CompilerParams(
            collective_id=0, has_side_effects=True, vmem_limit_bytes=67043328
        ),
        name="main_step",
    )(
        og_t, counts_t, dec_t, emb_t, scale, embedded, mg_kept, mg_sent, noise, lat_w, up_w,
        rowd, const, gain, bias, lat_b, pmean_t, plogv_t,
    )


def last_kernel(cfg, *refs):
    ncell, ngene, nk = cfg
    big_in, (small, vec) = refs[:4], refs[4:6]
    big_out = refs[6:10]
    gain, shift, latw, latb, up, pmean, plogv, loss = refs[10:18]
    held, sem = refs[18:22], refs[22]
    part = 256
    pieces = []
    for src, dst, mid in zip(big_in, big_out, held):
        for c in range(0, src.shape[1], part):
            cut = pl.ds(c, min(part, src.shape[1] - c))
            i = len(pieces)
            pieces.append(
                (
                    pltpu.make_async_copy(src.at[:, cut], mid.at[:, cut], sem.at[0, i]),
                    pltpu.make_async_copy(mid.at[:, cut], dst.at[:, cut], sem.at[1, i]),
                )
            )
    for come, _ in pieces:
        come.start()

    def small_outputs():
        at = lax.axis_index("cells")
        lat = vec.shape[1]
        step, each = gain.shape[1], pmean.shape[1]
        quarter = small.shape[2]
        cut = 2 * lat - 2 * quarter
        latw[:, :quarter] = small[0]
        latw[:, quarter : 2 * quarter] = small[1]
        latw[:, 2 * quarter :] = small[2, :, :cut]
        up[:, : quarter - cut] = small[2, :, cut:]
        up[:, quarter - cut :] = small[3]

        def own(rows, size, base):
            col = lax.broadcasted_iota(jnp.int32, (lat, size), 0) + base
            mine = lax.broadcasted_iota(jnp.int32, (lat, size), 1) + at * size
            return fdot(rows, (col == mine).astype(F32), NN)

        pmean[...] = own(vec[:nk], each, 0)
        plogv[...] = own(vec[nk : 2 * nk], each, 0)
        tail = vec[2 * nk : 2 * nk + 8]
        first, second = own(tail, step, 0), own(tail, step, lat)
        for j, ref in enumerate((gain, shift, latb)):
            ref[...] = first[1 + 2 * j : 2 + 2 * j] + second[2 + 2 * j : 3 + 2 * j]
        loss[...] = tail[0:1, 0:1] * (1.0 / (ncell * ngene))

    for i, (come, go) in enumerate(pieces):
        come.wait()
        go.start()
        if i == 0:
            small_outputs()
    for _, go in pieces:
        go.wait()


def last_step(decoded, cgrad, dsum, esum, small, vec, nk, ncell, ngene):
    width, rows = decoded.shape
    step = dsum.shape[1]
    lat = vec.shape[1]
    model = step * ncell
    each = lat // ncell
    fixed = lambda shape: pl.BlockSpec(shape, lambda: (0,) * len(shape))
    big = [pl.BlockSpec(memory_space=pl.ANY)] * 4
    wide = sum(-(-n // 256) for n in (rows, rows, step, step))
    shapes = [(1, step), (1, step), (step, 2 * lat), (1, step), (step, lat)]
    shapes += [(nk, each), (nk, each), (1, 1)]
    return pl.pallas_call(
        functools.partial(last_kernel, (ncell, ngene, nk)),
        out_shape=[jax.ShapeDtypeStruct(x.shape, x.dtype) for x in (decoded, cgrad, dsum, esum)]
        + [jax.ShapeDtypeStruct(shape, F32) for shape in shapes],
        in_specs=big + [fixed(small.shape), fixed(vec.shape)],
        out_specs=big + [fixed(shape) for shape in shapes],
        scratch_shapes=[pltpu.VMEM(x.shape, x.dtype) for x in (decoded, cgrad, dsum, esum)]
        + [pltpu.SemaphoreType.DMA((2, wide))],
        compiler_params=pltpu.CompilerParams(vmem_limit_bytes=67043328),
        name="last_step",
    )(decoded, cgrad, dsum, esum, small, vec)


def on_device(
    counts,
    library,
    cell_mask,
    slide_len,
    kl_step,
    noise,
    emb_weight,
    ln_gain,
    ln_bias,
    lat_weight,
    lat_bias,
    up_weight,
    dec_weight,
    prior_mean,
    prior_logvar,
    out_grad,
    ncell,
    ngene,
):
    rows, width = counts.shape
    model = emb_weight.shape[0]
    latent_w = up_weight.shape[1]
    og_t, counts_t, dec_t, emb_t = out_grad.T, counts.T, dec_weight.T, emb_weight.T
    embedded, mg_kept, mg_sent, scale, const, rowd = front_step(
        slide_len, kl_step, library[None, :], cell_mask[None, :], counts_t, og_t, emb_t, dec_t,
        ncell, latent_w,
    )
    decoded, counts_grad, dec_out, emb_out, small, vec = main_step(
        embedded, mg_kept, mg_sent, noise, lat_weight, up_weight, rowd, const,
        ln_gain[None, :], ln_bias[None, :], lat_bias[None, :], prior_mean.T, prior_logvar.T,
        og_t, counts_t, dec_t, emb_t, scale, ncell,
    )
    decoded, counts_grad, dec_out, emb_out, gain, shift, latw, latb, up, pmean, plogv, loss = last_step(
        decoded, counts_grad, dec_out, emb_out, small, vec, prior_mean.shape[1], ncell, ngene
    )
    return (
        decoded.T,
        counts_grad.T,
        emb_out.T,
        gain[0],
        shift[0],
        latw,
        latb[0],
        up,
        dec_out.T,
        pmean.T,
        plogv.T,
        loss[0],
    )


def solution(mesh):
    ncell, ngene = mesh.shape["cells"], mesh.shape["genes"]

    def body(*args):
        return on_device(*args, ncell=ncell, ngene=ngene)

    return jax.shard_map(
        body,
        mesh=mesh,
        in_specs=(
            P("cells", "genes"),
            P("cells"),
            P("cells"),
            P(),
            P(),
            P("cells", None),
            P(None, "genes"),
            P(),
            P(),
            P(),
            P(),
            P(),
            P(None, "genes"),
            P(),
            P(),
            P("cells", "genes"),
        ),
        out_specs=(
            P("cells", "genes"),
            P("cells", "genes"),
            P("cells", "genes"),
            P("cells"),
            P("cells"),
            P("cells", None),
            P("cells"),
            P("cells", None),
            P("cells", "genes"),
            P("cells", None),
            P("cells", None),
            P(),
        ),
        check_vma=False,
    )
```

```python
import functools

import jax
import jax.numpy as jnp
from jax import lax
from jax.experimental import pallas as pl
from jax.experimental.pallas import tpu as pltpu
from jax.sharding import PartitionSpec as P

WARM = 1000
EPS = 1e-05
FREE = 1.0
BF = jnp.bfloat16
F32 = jnp.float32


MESH = pl.DeviceIdType.MESH


def bits_of(n):
    return n.bit_length() - 1


def bit_of(at, k):
    return lax.rem(lax.div(at, 1 << k), 2)


def xor_of(at, nbits, value):
    out = 0
    for k in range(nbits):
        bit = bit_of(at, k)
        out = out + (1 - bit if (value >> k) & 1 else bit) * (1 << k)
    return out


def reversed_bits(i, n):
    out = 0
    for k in range(n):
        out = out * 2 + ((i >> k) & 1)
    return out


def fdot(left, right, dims):
    return lax.dot_general(
        left, right, (dims, ((), ())), precision=lax.Precision.HIGHEST, preferred_element_type=F32
    )


def bdot(left, right, dims):
    return lax.dot_general(left, right, (dims, ((), ())), preferred_element_type=F32)


NN, NT, TN = ((1,), (0,)), ((1,), (1,)), ((0,), (0,))
AHEAD = 3


def front_kernel(cfg, *refs):
    ncell, nslide, lat = cfg
    nb = bits_of(ncell)
    slen_ref, kls_ref, lib_ref, mask_ref, ct_hbm, og_hbm, et_hbm, dt_hbm = refs[:8]
    emb_ref, mgk_ref, mgs_ref, scale_ref, const_ref, rowd_ref = refs[8:14]
    ct, og, et, dt, low, msend, mrecv, esend, erecv, ysend, yrecv, stb, stv = refs[14:27]
    lsem, asend, arecv = refs[27:]
    rows = lib_ref.shape[1]
    mine = rows // 4
    top = stv.shape[0] // 2
    at = lax.axis_index("cells")
    gene = lax.axis_index("genes")
    core, wye = bit_of(gene, 0), bit_of(gene, 1)
    home = core * 2 + wye
    peers = [{"cells": xor_of(at, nb, 1 << k)} for k in range(nb)]
    gpeers = [{"genes": xor_of(gene, 2, 1)}, {"genes": xor_of(gene, 2, 2)}]
    s = pl.program_id(0)

    def block_of(j):
        far, away = 1 - lax.rem(j, 2), 1 - lax.div(j, 2)
        side = far * (1 - core) + (1 - far) * core
        return side * 2 + away * (1 - wye) + (1 - away) * wye

    def cols(j):
        return pl.ds(pl.multiple_of(block_of(j) * mine, mine), mine)

    def load(which, h, f):
        src, dst = ((og_hbm, og), (ct_hbm, ct))[which]
        j = 2 * h + f
        return pltpu.make_async_copy(
            src.at[:, cols(j)],
            dst.at[h, :, pl.ds(f * mine, mine)],
            lsem.at[2 + 4 * which + j],
        )

    def whole(which):
        src, dst = ((dt_hbm, dt), (et_hbm, et))[which]
        return pltpu.make_async_copy(src, dst, lsem.at[which])

    def remote(src, dst, sem, peer):
        return pltpu.make_async_remote_copy(
            src_ref=src,
            dst_ref=dst,
            send_sem=asend.at[sem],
            recv_sem=arecv.at[sem],
            device_id=peer,
            device_id_type=MESH,
        )

    half = dt.shape[1] // 2

    def mcopy(h):
        return remote(msend.at[h], mrecv.at[h], h, gpeers[0])

    def ecopy(h, c):
        cut = pl.ds(c * half, half)
        return remote(esend.at[h, :, cut], erecv.at[h, :, cut], 2 + 2 * h + c, gpeers[0])

    def ycopy(c):
        cut = pl.ds(c * half, half)
        return remote(ysend.at[:, cut], yrecv.at[:, cut], 6 + c, gpeers[1])

    def scopy(r):
        return remote(stb.at[r], stb.at[nb + r], 8 + r, peers[r])

    def slides():
        place = at * rows + lax.broadcasted_iota(jnp.int32, (1, rows), 1)
        begin = 0
        for q in range(nslide):
            end = begin + slen_ref[q]
            yield q, ((place >= begin) & (place < end)).astype(F32)
            begin = end

    def round_done(r):
        scopy(r).wait_recv()
        v = stb[r] + stb[nb + r]
        if r + 1 < nb:
            stb[r + 1] = v
            scopy(r + 1).start()
        else:
            stv[...] = v

    @pl.when(s == 0)
    def _():
        barrier = pltpu.get_barrier_semaphore()
        for p in peers + gpeers:
            pl.semaphore_signal(barrier, inc=1, device_id=p, device_id_type=MESH)
        whole(0).start()
        for which, h in ((0, 0), (1, 0), (1, 1), (0, 1)):
            for f in range(2):
                load(which, h, f).start()
            if (which, h) == (0, 0):
                whole(1).start()
        stb[0] = jnp.zeros_like(stv)
        live = mask_ref[...].astype(F32)
        libsize = lib_ref[...].astype(F32)
        for q, row in slides():
            stb[0, q : q + 1] = jnp.sum(row * (libsize * live), 1, keepdims=True) * jnp.ones(
                (1, 128), F32
            )
            stb[0, top + q : top + q + 1] = jnp.sum(
                row * live, 1, keepdims=True
            ) * jnp.ones((1, 128), F32)
        pl.semaphore_wait(barrier, nb + 2)
        scopy(0).start()
        whole(0).wait()
        round_done(0)

    @pl.when(s == 1)
    def _():
        for r in range(3, nb):
            round_done(r)
        whole(1).wait()
        live = mask_ref[...].astype(F32)
        total = jnp.zeros((1, 1), F32)
        scale = jnp.zeros((1, rows), F32)
        for q, row in slides():
            count = stv[top + q : top + q + 1, 0:1]
            scale = scale + row * (stv[q : q + 1, 0:1] / jnp.maximum(count, 1.0))
            total = total + count
        scale_ref[...] = scale / lib_ref[...].astype(F32)
        total = jnp.maximum(total, 1.0)
        beta = jnp.minimum(1.0, kls_ref[0].astype(F32) / WARM)
        line = lax.broadcasted_iota(jnp.int32, (8, lat), 0)
        const_ref[...] = jnp.where(line == 0, total, beta)
        own = mask_ref[:, pl.ds(pl.multiple_of(home * mine, mine), mine)].astype(F32)
        line = lax.broadcasted_iota(jnp.int32, (8, mine), 0)
        both = jnp.where(line == 0, own, jnp.where(line == 1, beta * own / total, 0.0))
        eye = (
            lax.broadcasted_iota(jnp.int32, (8, 128), 0)
            == lax.broadcasted_iota(jnp.int32, (8, 128), 1)
        ).astype(F32)
        rowd_ref[...] = fdot(both, eye, TN)

    @pl.when((s == 0) | (s == 3))
    def _():
        h = lax.div(s, 3)
        for f in range(2):
            load(0, h, f).wait()
        for f in range(2):
            part = bdot(og[h, :, f * mine : (f + 1) * mine], dt[...], TN)
            if f == 0:
                msend[h] = part.astype(BF)
                mcopy(h).start()
            else:
                mgk_ref[...] = part
            if f + 1 < nb:

                @pl.when(s == 0)
                def _(f=f):
                    round_done(f + 1)


    def forward(c):
        cut = slice(c * half, (c + 1) * half)
        ecopy(0, c).wait_recv()
        ysend[:, cut] = (emb_ref[:, cut] + erecv[0, :, cut].astype(F32)).astype(BF)
        ycopy(c).start()

    @pl.when((s == 1) | (s == 2))
    def _():
        h = s - 1
        for f in range(2):
            load(1, h, f).wait()
            z = 1.0 + ct[h, :, f * mine : (f + 1) * mine].astype(F32) * scale_ref[
                :, cols(2 * h + f)
            ]
            low[:, f * mine : (f + 1) * mine] = jnp.log(z).astype(BF)
        for c in range(2):
            cut = slice(c * half, (c + 1) * half)
            part = bdot(low[...], et[:, cut], TN)
            esend[h, :, cut] = part[:mine].astype(BF)
            ecopy(h, c).start()
            emb_ref[:, cut] = part[mine:]

            @pl.when((s == 1) & (c == 1))
            def _():
                forward(0)

    @pl.when(s == 1)
    def _():
        forward(1)
        mcopy(0).wait_recv()
        mgs_ref[...] = (mgk_ref[...] + mrecv[0].astype(F32)).astype(BF)

    @pl.when(s == 3)
    def _():
        for c in range(2):
            ecopy(1, c).wait_recv()
        emb_ref[...] = emb_ref[...] + erecv[1].astype(F32)
        mcopy(1).wait_recv()
        mgk_ref[...] = mgk_ref[...] + mrecv[1].astype(F32)

    @pl.when(s == 3)
    def _():
        for c in range(2):
            ycopy(c).wait_recv()
        emb_ref[...] = emb_ref[...] + yrecv[...].astype(F32)
        for h in range(2):
            mcopy(h).wait_send()
            ycopy(h).wait_send()
            for c in range(2):
                ecopy(h, c).wait_send()
        for r in range(nb):
            scopy(r).wait_send()


def front_step(slide_len, kl_step, library, mask, counts_t, og_t, emb_t, dec_t, ncell, lat):
    width, rows = counts_t.shape
    model = emb_t.shape[1]
    mine = rows // 4
    nb = bits_of(ncell)
    nslide = slide_len.shape[0]
    top = -(-nslide // 8) * 8
    anyv = pl.BlockSpec(memory_space=pl.ANY)
    smem = pl.BlockSpec(memory_space=pltpu.SMEM)
    fixed = lambda *shape: pl.BlockSpec(shape, lambda s: (0,) * len(shape))
    vm = pltpu.VMEM
    return pl.pallas_call(
        functools.partial(front_kernel, (ncell, nslide, lat)),
        grid=(4,),
        out_shape=[
            jax.ShapeDtypeStruct((mine, model), F32),
            jax.ShapeDtypeStruct((mine, model), F32),
            jax.ShapeDtypeStruct((mine, model), BF),
            jax.ShapeDtypeStruct((1, rows), F32),
            jax.ShapeDtypeStruct((8, lat), F32),
            jax.ShapeDtypeStruct((mine, 128), F32),
        ],
        in_specs=[smem, smem, fixed(1, rows), fixed(1, rows), anyv, anyv, anyv, anyv],
        out_specs=[
            fixed(mine, model),
            fixed(mine, model),
            fixed(mine, model),
            fixed(1, rows),
            fixed(8, lat),
            fixed(mine, 128),
        ],
        scratch_shapes=[vm((2, width, 2 * mine), BF)] * 2
        + [vm((width, model), BF)] * 2
        + [vm((width, 2 * mine), BF)]
        + [vm((2, mine, model), BF)] * 4
        + [vm((mine, model), BF)] * 2
        + [
            vm((2 * nb, 2 * top, 128), F32),
            vm((2 * top, 128), F32),
            pltpu.SemaphoreType.DMA((10,)),
            pltpu.SemaphoreType.DMA((8 + nb,)),
            pltpu.SemaphoreType.DMA((8 + nb,)),
        ],
        compiler_params=pltpu.CompilerParams(
            collective_id=1, has_side_effects=True, vmem_limit_bytes=67043328
        ),
        name="front_step",
    )(slide_len, kl_step, library, mask, counts_t, og_t, emb_t, dec_t)


def main_kernel(cfg, *refs):
    ncell, nch, ch, inplace = cfg
    nb = bits_of(ncell)
    take = iter(refs)

    def some(count):
        return [next(take) for _ in range(count)]

    og_ref, ct_ref, dw_ref, ew_ref, scale_ref = some(5)
    emb_hbm, mgk_hbm, mgs_hbm, noise_hbm, latw_hbm, upw_hbm = some(6)
    rowd_ref, const_ref, gain_ref, bias_ref, latb_ref, pmean_ref, plogv_ref = some(7)
    decoded_ref, cgrad_ref, dsum_ref, esum_ref, small_ref, vec_ref = some(6)
    xm, xe, px, keep = some(4)
    recvs = some(nb)
    sends = {k: next(take) for k in range(nb) if k not in inplace}
    normal, mgk, mg, noise, latw, upw, hlow, lmean, lvar, sample, lgrad, resp_s, inv_s, kpart = some(14)
    klbuf, vecbuf, sm_keep, sm_s1, sm_r1, sm_s2, sm_r2 = some(7)
    sm_sc, sm_rc = some(nb), some(nb)
    fin = next(take)
    lsem, ssem, rsem, asend, arecv = some(5)

    rows, model = xm.shape
    mine = rows // 4
    lat = model // 2
    step = model // ncell
    half = model // 2
    at = lax.axis_index("cells")
    gene = lax.axis_index("genes")
    core, wye = bit_of(gene, 0), bit_of(gene, 1)
    home = core * 2 + wye
    peers = [{"cells": xor_of(at, nb, 1 << k)} for k in range(nb)]
    gpeers = [{"genes": xor_of(gene, 2, 1)}, {"genes": xor_of(gene, 2, 2)}]
    allpeers = peers + gpeers
    nall = nb + 2
    s = pl.program_id(0)
    slots = keep.shape[0]

    def remote(src, dst, ssem_at, rsem_at, peer):
        return pltpu.make_async_remote_copy(
            src_ref=src,
            dst_ref=dst,
            send_sem=ssem_at,
            recv_sem=rsem_at,
            device_id=peer,
            device_id_type=MESH,
        )

    def source(i, k):
        h = model >> (k + 1)
        if k in inplace:
            return recvs[k - 1].at[i, :, pl.ds(h, h)]
        return sends[k].at[lax.rem(i, sends[k].shape[0])]

    def copy(i, k):
        return remote(source(i, k), recvs[k].at[i], ssem.at[k, i], rsem.at[k, i], peers[k])

    def free(i, k):
        ring = sends[k].shape[0]

        @pl.when(i >= ring)
        def _():
            copy(i - ring, k).wait_send()

    side = {}

    def add_side(name, src, dst, peer):
        side[name] = (len(side), src, dst, peer)

    def rowblock(ref, b):
        return ref.at[pl.ds(pl.multiple_of(b * mine, mine), mine)]

    for name, ref in (("m", xm), ("e", xe)):
        add_side(name + "core", rowblock(ref, home), rowblock(ref, home), gpeers[0])
        add_side(name + "wye", rowblock(ref, home), rowblock(ref, home), gpeers[1])
        other = core * 2 + (1 - wye)
        add_side(name + "pass", rowblock(ref, other), rowblock(ref, other), gpeers[0])
    add_side("g", mgs_hbm, rowblock(xe, core * 2 + (1 - wye)), gpeers[1])
    for r in range(nall):
        add_side(f"k{r}", klbuf.at[r], klbuf.at[nall + r], allpeers[r])
        add_side(f"v{r}", vecbuf.at[r], vecbuf.at[nall + r], allpeers[r])
    add_side("s1", sm_s1, sm_r1, gpeers[0])
    add_side("s2", sm_s2, sm_r2, gpeers[1])
    for k in range(nb):
        add_side(f"c{k}", sm_sc[k], sm_rc[k], peers[k])
    add_side("f0", fin.at[home], fin.at[home], gpeers[1])
    add_side("f1", fin.at[pl.ds(core * 2, 2)], fin.at[pl.ds(core * 2, 2)], gpeers[0])

    def side_copy(name):
        at_sem, src, dst, peer = side[name]
        return remote(src, dst, asend.at[at_sem], arecv.at[at_sem], peer)

    def start(name):
        side_copy(name).start()

    def got(name):
        side_copy(name).wait_recv()

    def permute(x, sem_at):
        if step % 128 == 0:
            cps = []
            for i in range(ncell):
                block = xor_of(at, nb, reversed_bits(i, nb))
                cps.append(
                    pltpu.make_async_copy(
                        x.at[:, pl.ds(pl.multiple_of(block * step, step), step)],
                        px.at[:, pl.ds(i * step, step)],
                        lsem.at[sem_at + i],
                    )
                )
            for cp in cps:
                cp.start()
            for cp in cps:
                cp.wait()
        else:
            row = lax.broadcasted_iota(jnp.int32, (model, 128), 0)

            def part(j, _):
                col = lax.broadcasted_iota(jnp.int32, (model, 128), 1) + j * 128
                block = col // step
                target = col % step
                for k in range(nb):
                    flag = (block // (1 << (nb - 1 - k))) % 2
                    own = bit_of(at, k)
                    target = target + (flag + own - 2 * flag * own) * ((1 << k) * step)
                pick = (row == target).astype(F32).astype(BF)
                px[:, pl.ds(pl.multiple_of(j * 128, 128), 128)] = jnp.dot(
                    x[...], pick, preferred_element_type=F32
                ).astype(BF)
                return 0

            lax.fori_loop(0, model // 128, part, 0)

    def tables():
        prec = jnp.exp(-plogv_ref[...])
        mprec = pmean_ref[...] * prec
        return prec, mprec, pmean_ref[...] * mprec + plogv_ref[...]

    def loads():
        pairs = (
            (emb_hbm, normal),
            (latw_hbm, latw),
            (upw_hbm, upw),
            (rowblock(noise_hbm, home), noise),
            (mgk_hbm, mgk),
        )
        return [pltpu.make_async_copy(a, b, lsem.at[i]) for i, (a, b) in enumerate(pairs)]

    @pl.when(s == 0)
    def _():
        for cp in loads():
            cp.start()
        barrier = pltpu.get_barrier_semaphore()
        for p in allpeers:
            pl.semaphore_signal(barrier, inc=1, device_id=p, device_id_type=MESH)
        first, latw_in, upw_in, noise_in, mgk_in = loads()
        first.wait()
        e = normal[...]
        centred = e - jnp.mean(e, -1, keepdims=True)
        inv = lax.rsqrt(jnp.mean(centred * centred, -1, keepdims=True) + EPS)
        nrm = centred * inv
        normal[...] = nrm
        inv_s[...] = inv
        hidden = nrm * gain_ref[...] + bias_ref[...]
        hlow[...] = hidden.astype(BF)
        latw_in.wait()
        latent = bdot(hlow[...], latw[...], NN) + latb_ref[...]
        lm, lv = latent[:, :lat], latent[:, lat:]
        lmean[...] = lm
        lvar[...] = lv
        noise_in.wait()
        upw_in.wait()
        sample[...] = (lm + jnp.exp(0.5 * lv) * noise[...].astype(F32)).astype(BF)
        mixed = normal[...] * gain_ref[...] + bias_ref[...] + bdot(sample[...], upw[...], NT)
        xm[pl.ds(pl.multiple_of(home * mine, mine), mine), :] = mixed.astype(BF)
        pl.semaphore_wait(barrier, nall)
        start("mwye")
        start("mcore")
        start("g")
        mgk_in.wait()
        prec, mprec, ctab = tables()
        lm, lv = lmean[...], lvar[...]
        csum = fdot(jnp.ones((8, lat), F32), ctab, NT)[0:1]
        logits = -0.5 * (fdot(lm * lm, prec, NT) - 2.0 * fdot(lm, mprec, NT) + csum)
        logits = logits * lat ** (-0.5)
        top = jnp.exp(logits - jnp.max(logits, -1, keepdims=True))
        resp = top / jnp.sum(top, -1, keepdims=True)
        resp_s[...] = resp
        moment = jnp.exp(lv) + lm * lm
        diverge = 0.5 * (
            fdot(resp, ctab, NN)
            - lv
            + moment * fdot(resp, prec, NN)
            - 2.0 * lm * fdot(resp, mprec, NN)
            - 1.0
        )
        klbuf[0] = jnp.sum(diverge * rowd_ref[:, 0:1], 0, keepdims=True)
        start("k0")
        got("mwye")
        start("mpass")
        got("mcore")
        got("mpass")
        permute(xm, 0)

    def out_parts(i, g):
        free(i, 0)
        sends[0][lax.rem(i, sends[0].shape[0])] = jnp.dot(
            g, px[:, half:], preferred_element_type=F32
        ).astype(BF)
        copy(i, 0).start()
        keep[lax.rem(i, slots)] = jnp.dot(g, px[:, :half], preferred_element_type=F32)

    @pl.when(s < nch)
    def _():
        out_parts(s, og_ref[...])
        decoded_ref[...] = bdot(dw_ref[...], xm[...], NT).astype(BF)

    @pl.when((s >= nch) & (s < 2 * nch))
    def _():
        scale = scale_ref[...]
        z = 1.0 + ct_ref[...].astype(F32) * scale
        out_parts(s, jnp.log(z).astype(BF))
        grad = bdot(ew_ref[...], xe[...], NT)
        z = 1.0 + ct_ref[...].astype(F32) * scale
        cgrad_ref[...] = (grad * scale / z).astype(BF)

    for k in range(1, nb + 1):
        i = s - AHEAD - (k - 1)

        @pl.when((i >= 0) & (i < 2 * nch))
        def _(i=i, k=k):
            copy(i, k - 1).wait_recv()
            slot = lax.rem(i, slots)
            if k < nb:
                h = model >> (k + 1)
                lo, hi = h, 2 * h
            else:
                lo, hi = 0, step
            v = keep[slot, :, lo:hi]
            for j in range(k):
                v = v + recvs[j][i, :, lo:hi].astype(F32)
            if k < nb:
                if k in inplace:
                    recvs[k - 1][i, :, lo:hi] = v.astype(BF)
                else:
                    free(i, k)
                    sends[k][lax.rem(i, sends[k].shape[0])] = v.astype(BF)
                copy(i, k).start()
            else:

                @pl.when(i < nch)
                def _():
                    dsum_ref[...] = v

                @pl.when(i >= nch)
                def _():
                    esum_ref[...] = v

    plan = {}

    def at_step(step_no):
        def put(fn):
            plan.setdefault(step_no, []).append(fn)
            return fn

        return put

    per = -(-nall // 4)
    for r in range(nall):

        @at_step(1 + r // per)
        def _(r=r):
            got(f"k{r}")
            v = klbuf[r] + klbuf[nall + r]
            if r + 1 < nall:
                klbuf[r + 1] = v
                start(f"k{r + 1}")
            else:
                kpart[...] = v

    back = 2 + (nall - 1) // per

    @at_step(back)
    def _():
        prec, mprec, ctab = tables()
        lm, lv = lmean[...], lvar[...]
        average = kpart[...] / const_ref[0:1]
        loss = const_ref[1:2] * jnp.sum(jnp.maximum(average, FREE), -1, keepdims=True)
        active = (average > FREE).astype(F32)
        weight = rowd_ref[:, 1:2] * active
        resp = resp_s[...]
        rprec = fdot(resp, prec, NN)
        rmean = fdot(resp, mprec, NN)
        variance = jnp.exp(lv)
        moment = variance + lm * lm
        wmom, wmean = weight * moment, weight * lm
        rgrad = 0.5 * (
            fdot(weight, ctab, NT) + fdot(wmom, prec, NT) - 2.0 * fdot(wmean, mprec, NT)
        )
        logit = resp * (rgrad - jnp.sum(resp * rgrad, -1, keepdims=True)) * lat ** (-0.5)
        got("g")
        own = xe[pl.ds(pl.multiple_of(home * mine, mine), mine), :].astype(F32)
        mg[...] = (mgk[...] + own).astype(BF)
        sgrad = bdot(mg[...], upw[...], NN)
        mgrad = (
            sgrad
            + weight * (lm * rprec - rmean)
            - lm * fdot(logit, prec, NN)
            + fdot(logit, mprec, NN)
        )
        vgrad = sgrad * 0.5 * jnp.exp(0.5 * lv) * noise[...].astype(F32) + 0.5 * weight * (
            variance * rprec - 1.0
        )
        lgrad[:, :lat] = mgrad.astype(BF)
        lgrad[:, lat:] = vgrad.astype(BF)
        lcol = fdot(logit, jnp.ones((mine, 128), F32), TN)[:, 0:1]
        cg = 0.5 * fdot(resp, weight, TN) - 0.5 * lcol
        mpg = fdot(logit, lm, TN) - fdot(resp, wmean, TN)
        pmean = pmean_ref[...]
        pg = (
            0.5 * fdot(resp, wmom, TN)
            - 0.5 * fdot(logit, lm * lm, TN)
            + pmean * pmean * cg
            + pmean * mpg
        )
        nk = pmean.shape[0]
        vecbuf[0, 0:nk] = 2.0 * pmean * prec * cg + prec * mpg
        vecbuf[0, nk : 2 * nk] = cg - prec * pg
        base = 2 * nk
        vecbuf[0, base : base + 1] = loss * jnp.ones((1, lat), F32)
        lg = lgrad[...]
        lb = jnp.sum(lg.astype(F32), 0, keepdims=True)
        hgrad = mg[...].astype(F32) + bdot(lg, latw[...], NT)
        nrm = normal[...]
        gg = jnp.sum(hgrad * nrm, 0, keepdims=True)
        sg = jnp.sum(hgrad, 0, keepdims=True)
        for j, row in enumerate((gg, sg, lb)):
            for part in range(2):
                r = base + 1 + 2 * j + part
                vecbuf[0, r : r + 1] = row[:, part * lat : (part + 1) * lat]
        vecbuf[0, base + 7 : base + 8] = jnp.zeros((1, lat), F32)
        ng = hgrad * gain_ref[...]
        eg = inv_s[...] * (
            ng - jnp.mean(ng, -1, keepdims=True) - nrm * jnp.mean(ng * nrm, -1, keepdims=True)
        )
        xe[pl.ds(pl.multiple_of(home * mine, mine), mine), :] = eg.astype(BF)
        start("ewye")
        start("ecore")
        start("v0")

    @at_step(back + 1)
    def _():
        quarter = 3 * lat // 4

        def put(q, lo, hi, left, right):
            v = bdot(left, right, TN)

            @pl.when(core == q // 2)
            def _():
                sm_keep[q % 2, :, lo:hi] = v

            @pl.when(core != q // 2)
            def _():
                sm_s1[q % 2, :, lo:hi] = v.astype(BF)

        cut = 2 * lat - 2 * quarter
        put(0, 0, quarter, hlow[...], lgrad[:, :quarter])
        put(1, 0, quarter, hlow[...], lgrad[:, quarter : 2 * quarter])
        put(2, 0, cut, hlow[...], lgrad[:, 2 * quarter :])
        put(2, cut, quarter, mg[...], sample[:, : quarter - cut])
        put(3, 0, quarter, mg[...], sample[:, quarter - cut :])
        start("s1")

    @at_step(back + 2)
    def _():
        got("ewye")
        start("epass")

    @at_step(nch - 1)
    def _():
        got("ecore")
        got("epass")
        permute(xe, ncell)

    assert back + 2 < nch - 1
    for r in range(nall):

        @at_step(back + 4 + r)
        def _(r=r):
            got(f"v{r}")
            v = vecbuf[r] + vecbuf[nall + r]
            if r + 1 < nall:
                vecbuf[r + 1] = v
                start(f"v{r + 1}")
            else:
                vec_ref[...] = v

    @at_step(back + 2)
    def _():
        got("s1")
        sm_keep[wye] = sm_keep[wye] + sm_r1[wye].astype(F32)
        sm_s2[...] = (sm_keep[1 - wye] + sm_r1[1 - wye].astype(F32)).astype(BF)
        start("s2")

    def span(k):
        base = 0
        for j in reversed(range(k + 1, nb)):
            base = base + bit_of(at, j) * (step << j)
        bit = bit_of(at, k)
        size = step << k
        return (
            pl.ds(pl.multiple_of(base + bit * size, step), size),
            pl.ds(pl.multiple_of(base + (1 - bit) * size, step), size),
        )

    @at_step(back + 5)
    def _():
        got("s2")
        sm_keep[wye] = sm_keep[wye] + sm_r2[...].astype(F32)
        sm_sc[nb - 1][...] = sm_keep[wye, span(nb - 1)[1], :].astype(BF)
        start(f"c{nb - 1}")

    for k in reversed(range(nb)):

        @at_step(back + 5 + 2 * (nb - k) + (0 if k else 2))
        def _(k=k):
            got(f"c{k}")
            kept = span(k)[0]
            sm_keep[wye, kept, :] = sm_keep[wye, kept, :] + sm_rc[k][...].astype(F32)
            if k:
                sm_sc[k - 1][...] = sm_keep[wye, span(k - 1)[1], :].astype(BF)
                start(f"c{k - 1}")
            else:
                fin[home] = sm_keep[wye, kept, :].astype(BF)
                start("f0")

    @at_step(back + 8 + 2 * nb)
    def _():
        got("f0")
        start("f1")

    @at_step(back + 9 + 2 * nb)
    def _():
        got("f1")
        small_ref[...] = fin[...].astype(F32)


    for step_no in sorted(plan):

        @pl.when(s == step_no)
        def _(fns=plan[step_no]):
            for fn in fns:
                fn()

    @pl.when(s == pl.num_programs(0) - 1)
    def _():
        def body(i, _):
            for k in range(nb):
                if k in inplace:
                    copy(i, k).wait_send()
                else:

                    @pl.when(i >= 2 * nch - sends[k].shape[0])
                    def _(k=k):
                        copy(i, k).wait_send()

            return 0

        lax.fori_loop(0, 2 * nch, body, 0)
        for name in side:
            side_copy(name).wait_send()


def main_step(
    embedded, mg_kept, mg_sent, noise, lat_w, up_w, rowd, const, gain, bias, lat_b, pmean_t, plogv_t,
    og_t, counts_t, dec_t, emb_t, scale, ncell
):
    width, rows = og_t.shape
    mine, model = embedded.shape
    lat = up_w.shape[1]
    nb = bits_of(ncell)
    nall = nb + 2
    step = model // ncell
    ch = 376 if step % 128 == 0 else 192
    nch = -(-width // ch)
    inplace = tuple(k for k in range(1, nb) if (model >> (k + 1)) % 128 == 0)
    n = 2 * nch
    last = nch - 1
    first = lambda s: (jnp.minimum(s, last), 0)
    second = lambda s: (jnp.clip(s - nch, 0, last), 0)
    fixed = lambda *shape: pl.BlockSpec(shape, lambda s: (0,) * len(shape))
    lag = AHEAD + nb - 1
    ring = AHEAD + 2
    quarter = 3 * lat // 4
    nk = pmean_t.shape[0]
    vec = 2 * nk + 8
    anyv = pl.BlockSpec(memory_space=pl.ANY)
    nside = 7 + 2 * nall + 2 + nb + 2
    vm = pltpu.VMEM
    return pl.pallas_call(
        functools.partial(main_kernel, (ncell, nch, ch, inplace)),
        grid=(n + lag,),
        out_shape=[
            jax.ShapeDtypeStruct((width, rows), BF),
            jax.ShapeDtypeStruct((width, rows), BF),
            jax.ShapeDtypeStruct((width, step), F32),
            jax.ShapeDtypeStruct((width, step), F32),
            jax.ShapeDtypeStruct((4, step, quarter), F32),
            jax.ShapeDtypeStruct((vec, lat), F32),
        ],
        in_specs=[
            pl.BlockSpec((ch, rows), first),
            pl.BlockSpec((ch, rows), second),
            pl.BlockSpec((ch, model), first),
            pl.BlockSpec((ch, model), second),
            fixed(1, rows),
            anyv,
            anyv,
            anyv,
            anyv,
            anyv,
            anyv,
            fixed(mine, 128),
            fixed(8, lat),
            fixed(1, model),
            fixed(1, model),
            fixed(1, model),
            fixed(nk, lat),
            fixed(nk, lat),
        ],
        out_specs=[
            pl.BlockSpec((ch, rows), first),
            pl.BlockSpec((ch, rows), second),
            pl.BlockSpec((ch, step), lambda s: (jnp.clip(s - lag, 0, last), 0)),
            pl.BlockSpec((ch, step), lambda s: (jnp.clip(s - lag - nch, 0, last), 0)),
            fixed(4, step, quarter),
            fixed(vec, lat),
        ],
        scratch_shapes=[vm((rows, model), BF)] * 3
        + [vm((lag + 1, ch, model // 2), F32)]
        + [vm((n, ch, model >> (k + 1)), BF) for k in range(nb)]
        + [vm((ring, ch, model >> (k + 1)), BF) for k in range(nb) if k not in inplace]
        + [
            vm((mine, model), F32),
            vm((mine, model), F32),
            vm((mine, model), BF),
            vm((mine, lat), BF),
            vm((model, 2 * lat), BF),
            vm((model, lat), BF),
            vm((mine, model), BF),
            vm((mine, lat), F32),
            vm((mine, lat), F32),
            vm((mine, lat), BF),
            vm((mine, 2 * lat), BF),
            vm((mine, nk), F32),
            vm((mine, 1), F32),
            vm((1, lat), F32),
            vm((2 * nall, 1, lat), F32),
            vm((2 * nall, vec, lat), F32),
            vm((2, model, quarter), F32),
            vm((2, model, quarter), BF),
            vm((2, model, quarter), BF),
            vm((model, quarter), BF),
            vm((model, quarter), BF),
        ]
        + [vm((step << k, quarter), BF) for k in range(nb)] * 2
        + [
            vm((4, step, quarter), BF),
            pltpu.SemaphoreType.DMA((max(5, 2 * ncell),)),
            pltpu.SemaphoreType.DMA((nb, n)),
            pltpu.SemaphoreType.DMA((nb, n)),
            pltpu.SemaphoreType.DMA((nside,)),
            pltpu.SemaphoreType.DMA((nside,)),
        ],
        compiler_params=pltpu.CompilerParams(
            collective_id=0, has_side_effects=True, vmem_limit_bytes=67043328
        ),
        name="main_step",
    )(
        og_t, counts_t, dec_t, emb_t, scale, embedded, mg_kept, mg_sent, noise, lat_w, up_w,
        rowd, const, gain, bias, lat_b, pmean_t, plogv_t,
    )


def last_kernel(cfg, *refs):
    ncell, ngene, nk = cfg
    big_in, (small, vec) = refs[:4], refs[4:6]
    big_out = refs[6:10]
    gain, shift, latw, latb, up, pmean, plogv, loss = refs[10:18]
    held, sem = refs[18:22], refs[22]
    part = 256
    pieces = []
    for src, dst, mid in zip(big_in, big_out, held):
        for c in range(0, src.shape[1], part):
            cut = pl.ds(c, min(part, src.shape[1] - c))
            i = len(pieces)
            pieces.append(
                (
                    pltpu.make_async_copy(src.at[:, cut], mid.at[:, cut], sem.at[0, i]),
                    pltpu.make_async_copy(mid.at[:, cut], dst.at[:, cut], sem.at[1, i]),
                )
            )
    for come, _ in pieces:
        come.start()

    def small_outputs():
        at = lax.axis_index("cells")
        lat = vec.shape[1]
        step, each = gain.shape[1], pmean.shape[1]
        quarter = small.shape[2]
        cut = 2 * lat - 2 * quarter
        latw[:, :quarter] = small[0]
        latw[:, quarter : 2 * quarter] = small[1]
        latw[:, 2 * quarter :] = small[2, :, :cut]
        up[:, : quarter - cut] = small[2, :, cut:]
        up[:, quarter - cut :] = small[3]

        def own(rows, size, base):
            col = lax.broadcasted_iota(jnp.int32, (lat, size), 0) + base
            mine = lax.broadcasted_iota(jnp.int32, (lat, size), 1) + at * size
            return fdot(rows, (col == mine).astype(F32), NN)

        pmean[...] = own(vec[:nk], each, 0)
        plogv[...] = own(vec[nk : 2 * nk], each, 0)
        tail = vec[2 * nk : 2 * nk + 8]
        first, second = own(tail, step, 0), own(tail, step, lat)
        for j, ref in enumerate((gain, shift, latb)):
            ref[...] = first[1 + 2 * j : 2 + 2 * j] + second[2 + 2 * j : 3 + 2 * j]
        loss[...] = tail[0:1, 0:1] * (1.0 / (ncell * ngene))

    for i, (come, go) in enumerate(pieces):
        come.wait()
        go.start()
        if i == 0:
            small_outputs()
    for _, go in pieces:
        go.wait()


def last_step(decoded, cgrad, dsum, esum, small, vec, nk, ncell, ngene):
    width, rows = decoded.shape
    step = dsum.shape[1]
    lat = vec.shape[1]
    model = step * ncell
    each = lat // ncell
    fixed = lambda shape: pl.BlockSpec(shape, lambda: (0,) * len(shape))
    big = [pl.BlockSpec(memory_space=pl.ANY)] * 4
    wide = sum(-(-n // 256) for n in (rows, rows, step, step))
    shapes = [(1, step), (1, step), (step, 2 * lat), (1, step), (step, lat)]
    shapes += [(nk, each), (nk, each), (1, 1)]
    return pl.pallas_call(
        functools.partial(last_kernel, (ncell, ngene, nk)),
        out_shape=[jax.ShapeDtypeStruct(x.shape, x.dtype) for x in (decoded, cgrad, dsum, esum)]
        + [jax.ShapeDtypeStruct(shape, F32) for shape in shapes],
        in_specs=big + [fixed(small.shape), fixed(vec.shape)],
        out_specs=big + [fixed(shape) for shape in shapes],
        scratch_shapes=[pltpu.VMEM(x.shape, x.dtype) for x in (decoded, cgrad, dsum, esum)]
        + [pltpu.SemaphoreType.DMA((2, wide))],
        compiler_params=pltpu.CompilerParams(vmem_limit_bytes=67043328),
        name="last_step",
    )(decoded, cgrad, dsum, esum, small, vec)


def on_device(
    counts,
    library,
    cell_mask,
    slide_len,
    kl_step,
    noise,
    emb_weight,
    ln_gain,
    ln_bias,
    lat_weight,
    lat_bias,
    up_weight,
    dec_weight,
    prior_mean,
    prior_logvar,
    out_grad,
    ncell,
    ngene,
):
    rows, width = counts.shape
    model = emb_weight.shape[0]
    latent_w = up_weight.shape[1]
    og_t, counts_t, dec_t, emb_t = out_grad.T, counts.T, dec_weight.T, emb_weight.T
    embedded, mg_kept, mg_sent, scale, const, rowd = front_step(
        slide_len, kl_step, library[None, :], cell_mask[None, :], counts_t, og_t, emb_t, dec_t,
        ncell, latent_w,
    )
    decoded, counts_grad, dec_out, emb_out, small, vec = main_step(
        embedded, mg_kept, mg_sent, noise, lat_weight, up_weight, rowd, const,
        ln_gain[None, :], ln_bias[None, :], lat_bias[None, :], prior_mean.T, prior_logvar.T,
        og_t, counts_t, dec_t, emb_t, scale, ncell,
    )
    decoded, counts_grad, dec_out, emb_out, gain, shift, latw, latb, up, pmean, plogv, loss = last_step(
        decoded, counts_grad, dec_out, emb_out, small, vec, prior_mean.shape[1], ncell, ngene
    )
    return (
        decoded.T,
        counts_grad.T,
        emb_out.T,
        gain[0],
        shift[0],
        latw,
        latb[0],
        up,
        dec_out.T,
        pmean.T,
        plogv.T,
        loss[0],
    )


def solution(mesh):
    ncell, ngene = mesh.shape["cells"], mesh.shape["genes"]

    def body(*args):
        return on_device(*args, ncell=ncell, ngene=ngene)

    return jax.shard_map(
        body,
        mesh=mesh,
        in_specs=(
            P("cells", "genes"),
            P("cells"),
            P("cells"),
            P(),
            P(),
            P("cells", None),
            P(None, "genes"),
            P(),
            P(),
            P(),
            P(),
            P(),
            P(None, "genes"),
            P(),
            P(),
            P("cells", "genes"),
        ),
        out_specs=(
            P("cells", "genes"),
            P("cells", "genes"),
            P("cells", "genes"),
            P("cells"),
            P("cells"),
            P("cells", None),
            P("cells"),
            P("cells", None),
            P("cells", "genes"),
            P("cells", None),
            P("cells", None),
            P(),
        ),
        check_vma=False,
    )
```
